32 devices in a mesh: row: 16 (over z, y, x), col: 2 (over core).
Axes of the slice: x: 2, y: 2, z: 4, core: 2. Of those that a mesh axis runs over, the one named last changes fastest.
Arguments:
- hidden_in: bfloat16 [8192, 1536], P(('row', 'col')), may hold values from -6 to 6
- segments: int32 [16, 512], P('row'), may hold values from 0 to 3, never falling along the last dimension, each value on 1 to 256 neighbouring positions
- routes: int32 [8192, 4], P('row'), may hold values from 0 to 31, all different within a row; in each aligned block of 512 rows (0 to 511, 512 to 1023, ...) at most 96 rows name the same one
- attention_gain: bfloat16 [1536], P('row'), may hold values from 0.099609375 to 1.8984375
- query_weight: bfloat16 [1536, 1536], P('row', 'col'), may hold values from -0.15625 to 0.15625
- key_matrix: bfloat16 [1536, 256], P('row', 'col'), may hold values from -0.15625 to 0.15625
- value_matrix: bfloat16 [1536, 256], P('row', 'col'), may hold values from -0.15625 to 0.15625
- output_weight: bfloat16 [1536, 1536], P('col', 'row'), may hold values from -1.5 to 1.5
- expert_gain: bfloat16 [1536], P('row'), may hold values from 0.099609375 to 1.8984375
- router_weight: bfloat16 [1536, 32], P('row'), may hold values from -0.078125 to 0.078125
- gate_weight: bfloat16 [32, 1536, 768], P(None, 'row', 'col'), may hold values from -0.15625 to 0.15625
- up_weight: bfloat16 [32, 1536, 768], P(None, 'row', 'col'), may hold values from -0.15625 to 0.15625
- down_weight: bfloat16 [32, 768, 1536], P(None, 'col', 'row'), may hold values from -0.4375 to 0.4375
- cotangent: bfloat16 [8192, 1536], P(('row', 'col')), may hold values from -6 to 6
Outputs:
- block_out: bfloat16 [8192, 1536], P(('row', 'col'))
- input_grad: float32 [8192, 1536], P(('row', 'col'))
- attention_gain_grad: float32 [1536], P('row')
- query_weight_grad: float32 [1536, 1536], P('row', 'col')
- key_weight_grad: float32 [1536, 256], P('row', 'col')
- value_weight_grad: float32 [1536, 256], P('row', 'col')
- output_weight_grad: float32 [1536, 1536], P('col', 'row')
- expert_gain_grad: float32 [1536], P('row')
- router_weight_grad: float32 [1536, 32], P('row')
- gate_weight_grad: float32 [32, 1536, 768], P(None, 'row', 'col')
- up_weight_grad: float32 [32, 1536, 768], P(None, 'row', 'col')
- down_weight_grad: float32 [32, 768, 1536], P(None, 'col', 'row')
The draws below stay inside these ranges and needn't reach their ends.
Inputs may be any that keep to these rules, and one draw needn't show every extreme that they name: Each row of segments numbers the documents of one packed sequence from 0 without falling; a document is one run of positions of at most 256. `routes`: each row names 4 different experts. Among the 512 rows of one sequence no expert is named more than 96 times, a bound that some block reaches.
All inputs are finite; a program needn't handle non-finite values.
Results may differ from the reference program's by a relative error of at most 0.02.
Values may be sent and summed in bfloat16 or wider, within the bound.
No kernel may reach another device: no remote copies, remote signals or barrier semaphores. Data moves between devices by JAX's collectives and lax.ppermute only.
A program may use at most 448 MiB of HBM per device.

```python
import math
from functools import partial
import jax
import jax.numpy as jnp
import numpy as np
from jax import lax

MODEL_WIDTH = 1536
QUERY_HEADS = 12
KEY_VALUE_HEADS = 2
HEAD_SIZE = 128
E = 32
FFE = 768
TOPK = 4
DOCS = 4
TOK_DEV = 512
SEQS = 16
TOKENS = 8192
CAP = 96
DOC_MOST = 256


def shard_levels(key, extent, cuts, smallest, top_value):
    def one(dim, parts):
        heights = jax.random.uniform(jax.random.fold_in(jax.random.fold_in(key, 6), dim), (parts,), jnp.float32, smallest / len(cuts), top_value / len(cuts))
        return jnp.repeat(jnp.exp(heights), extent[dim] // parts).reshape((-1,) + (1,) * (len(extent) - dim - 1))

    gain = one(*cuts[0])
    for cut in cuts[1:]:
        gain = gain * one(*cut)
    return gain


def length_profile(amount, total, reach, skew):
    portions = [(1 << 20) // math.isqrt(rank ** skew) + 1 for rank in range(2, amount + 1)]
    rest, counts = total - reach - (amount - 1), [1] * (amount - 1)
    while rest > 0:
        free = [i for i in range(amount - 1) if counts[i] < reach]
        whole, budget = sum([portions[i] for i in free]), rest
        for i in free:
            addition = min(reach - counts[i], max(1, budget * portions[i] // whole), rest)
            counts[i] = counts[i] + addition
            rest = rest - addition
    return np.array([reach] + counts)


def ragged(key, number_of, total, bound, slope):
    if number_of == 2:
        one = jax.random.randint(key, (), max(1, total - bound), min(bound, total - 1) + 1)
        return jnp.stack([one, total - one])
    lengths = jnp.asarray(length_profile(number_of, total, bound, slope), jnp.int32)
    pairs = (number_of - 1) // 2
    source_of, taker = lengths[1:1 + 2 * pairs:2], lengths[2:2 + 2 * pairs:2]
    slack = jnp.minimum(source_of - 1, bound - taker)
    shifted = jax.random.randint(jax.random.fold_in(key, 1), (pairs,), 0, 1 << 20) % (slack + 1)
    lengths = lengths.at[1:1 + 2 * pairs:2].set(source_of - shifted).at[2:2 + 2 * pairs:2].set(taker + shifted)
    return lengths[jax.random.permutation(jax.random.fold_in(key, 2), number_of)]


def routed_block(own_key, own, number, rows, count, top, most, slope):
    ranking = jax.random.permutation(own_key, count)
    crowded, ordinary = load_shares(count, rows * top, most, slope, True), load_shares(count, rows * top, most, slope, False)
    places = jnp.arange(count)

    def named(sizes, offset_by):
        used = int((sizes > 0).sum())
        fixed = max(1, used // 4)
        shifted = fixed + (places - fixed + offset_by * (used - fixed)) % max(1, count - fixed)
        return jnp.zeros((count,), jnp.int32).at[ranking[jnp.where(places < fixed, places, shifted)]].set(jnp.asarray(sizes, jnp.int32))

    sizes = jnp.where(number % 4 == 0, named(crowded, number // 4), named(ordinary, number - number // 4 - 1))
    mixed = jax.random.permutation(jax.random.fold_in(own, 3), count)
    giver, taker = mixed[0:count // 2 * 2:2], mixed[1:count // 2 * 2:2]
    room = jnp.minimum(sizes[giver] - 1, most - sizes[taker]) // 2
    room = jnp.where((giver == ranking[0]) | (taker == ranking[0]) | (sizes[taker] == 0), 0, jnp.maximum(room, 0))
    shifted = jax.random.randint(jax.random.fold_in(own, 4), (count // 2,), 0, 1 << 20) % (room + 1)
    sizes = sizes.at[giver].add(-shifted).at[taker].add(shifted)
    labels = jnp.searchsorted(jnp.cumsum(sizes), jnp.arange(rows * top), side="right").astype(jnp.int32)
    table = labels.reshape(top, rows).T
    table = table[jax.random.permutation(jax.random.fold_in(own, 1), rows)]
    offset_by = jax.random.randint(jax.random.fold_in(own, 2), (rows, 1), 0, top)
    return jnp.take_along_axis(table, (jnp.arange(top)[None, :] + offset_by) % top, axis=1)


def load_shares(amount, total, most, slope, full):
    loads = [(1 << 20) // math.isqrt(standing ** slope) + 1 for standing in range(1, amount + 1)]
    largest = most if full else min(most, max(-(-total // amount), total * loads[0] // sum(loads)))
    least = 1 if total - largest >= amount - 1 else 0
    given, spare = [largest] + [least] * (amount - 1), total - largest - least * (amount - 1)
    while spare > 0:
        candidates = [i for i in range(1, amount) if given[i] < largest] or [i for i in range(1, amount) if given[i] < most]
        mass, budget = sum([loads[i] for i in candidates]), spare
        for i in candidates:
            extra = min(most - given[i], max(1, budget * loads[i] // mass), spare)
            given[i] = given[i] + extra
            spare = spare - extra
    return np.array(given)


def centred(stream_key, extent, width, most, cuts=(), kind=jnp.bfloat16):
    values = width * jax.random.normal(stream_key, extent, jnp.float32)
    if cuts:
        values = values * shard_levels(stream_key, extent, cuts, -0.22, 0.18)
    return jnp.clip(values, -most, most).astype(kind)


def setup_inputs(seed: int = 0) -> dict:
    seeds = jax.random.split(jax.random.key(seed), 15)
    hidden_in = centred(seeds[0], (TOKENS, MODEL_WIDTH), 1.0, 6.0, ((0, 32),))
    segments = jax.vmap(lambda own: jnp.searchsorted(jnp.cumsum(ragged(own, DOCS, TOK_DEV, DOC_MOST, 1)), jnp.arange(TOK_DEV), side="right"))(jax.random.split(seeds[1], SEQS)).reshape((SEQS, TOK_DEV)).astype(jnp.int32)
    routes_keys = jax.random.split(jax.random.fold_in(seeds[2], 1), TOKENS // TOK_DEV)
    routes_turns = jax.random.permutation(jax.random.fold_in(seeds[2], 3), TOKENS // TOK_DEV)
    routes = jax.vmap(lambda own, number: routed_block(jax.random.fold_in(seeds[2], 2), own, number, TOK_DEV, E, TOPK, CAP, 1))(routes_keys, routes_turns).reshape((TOKENS, TOPK))
    attention_gain = jnp.clip(1.0 + 0.18 * jax.random.normal(seeds[3], (MODEL_WIDTH,), jnp.float32), 0.099609375, 1.8984375).astype(jnp.bfloat16)
    query_weight = centred(seeds[4], (MODEL_WIDTH, QUERY_HEADS * HEAD_SIZE), MODEL_WIDTH ** -0.5, 0.15625, ((0, 16), (1, 2)))
    key_matrix = centred(seeds[5], (MODEL_WIDTH, KEY_VALUE_HEADS * HEAD_SIZE), MODEL_WIDTH ** -0.5, 0.15625, ((0, 16), (1, 2)))
    value_matrix = centred(seeds[6], (MODEL_WIDTH, KEY_VALUE_HEADS * HEAD_SIZE), MODEL_WIDTH ** -0.5, 0.15625, ((0, 16), (1, 2)))
    output_weight = centred(seeds[7], (QUERY_HEADS * HEAD_SIZE, MODEL_WIDTH), 16 ** -0.5, 1.5, ((0, 2), (1, 16)))
    expert_gain = jnp.clip(1.0 + 0.18 * jax.random.normal(seeds[8], (MODEL_WIDTH,), jnp.float32), 0.099609375, 1.8984375).astype(jnp.bfloat16)
    router_weight = centred(seeds[9], (MODEL_WIDTH, E), (4 * MODEL_WIDTH) ** -0.5, 0.078125, ((0, 16),))
    gate_weight = centred(seeds[10], (E, MODEL_WIDTH, FFE), MODEL_WIDTH ** -0.5, 0.15625, ((1, 16), (2, 2)))
    up_weight = centred(seeds[11], (E, MODEL_WIDTH, FFE), MODEL_WIDTH ** -0.5, 0.15625, ((1, 16), (2, 2)))
    down_weight = centred(seeds[12], (E, FFE, MODEL_WIDTH), (FFE // 4) ** -0.5, 0.4375, ((1, 2), (2, 16)))
    cotangent = centred(seeds[13], (TOKENS, MODEL_WIDTH), 1.0, 6.0, ((0, 32),))
    return {"hidden_in": hidden_in, "segments": segments, "routes": routes, "attention_gain": attention_gain, "query_weight": query_weight, "key_matrix": key_matrix, "value_matrix": value_matrix, "output_weight": output_weight, "expert_gain": expert_gain, "router_weight": router_weight, "gate_weight": gate_weight, "up_weight": up_weight, "down_weight": down_weight, "cotangent": cotangent}


EPSILON = 1e-06
ROPE_BASE = 1000000.0
MASKED = -1e+30

@jax.custom_vjp
def low(v):
    return lax.optimization_barrier(v.astype(jnp.bfloat16)).astype(jnp.float32)

@jax.custom_vjp
def low_back(v):
    return v

def low_keep(v):
    return (low(v), None)

def low_pass(kept, grad):
    return (grad,)

def back_keep(v):
    return (v, None)

def back_low(kept, grad):
    return (low(grad),)
low.defvjp(low_keep, low_pass)
low_back.defvjp(back_keep, back_low)

def precise_product(left_side, right_side):
    return jnp.dot(left_side, right_side, precision=lax.Precision.HIGHEST)

def rms_scaled(values, gain_vector):
    return values * lax.rsqrt(lax.optimization_barrier(jnp.mean(values * values, axis=-1, keepdims=True)) + EPSILON) * gain_vector

def positions(segment_ids):
    total_length = segment_ids.shape[0]
    token_index = jnp.arange(total_length, dtype=jnp.int32)
    change = jnp.concatenate([jnp.ones((1,), jnp.bool_), segment_ids[1:] != segment_ids[:-1]])
    first_index = lax.cummax(jnp.where(change, token_index, jnp.zeros_like(token_index)), axis=0)
    return token_index - first_index

def apply_rotary(values, places):
    half_size = values.shape[-1] // 2
    frequency = ROPE_BASE ** (-2.0 * jnp.arange(half_size, dtype=jnp.float32) / values.shape[-1])
    angles = places.astype(jnp.float32)[:, None] * frequency[None, :]
    cosine_part = jnp.cos(angles)[:, None, :]
    sine_part = jnp.sin(angles)[:, None, :]
    first_half = values[..., :half_size]
    second_half = values[..., half_size:]
    return jnp.concatenate([first_half * cosine_part - second_half * sine_part, second_half * cosine_part + first_half * sine_part], axis=-1)

def slot_tables(route_ids, capacity):
    flat_ids = route_ids.reshape(-1)
    expert_ids = jnp.arange(E, dtype=jnp.int32)
    onehot = (flat_ids[:, None] == expert_ids[None, :]).astype(jnp.int32)
    rank_ids = lax.optimization_barrier(jnp.sum((jnp.cumsum(onehot, axis=0, dtype=jnp.int32) - 1) * onehot, axis=1, dtype=jnp.int32))
    pair_slot = (flat_ids * capacity + rank_ids).astype(jnp.int32)
    owners = jnp.arange(flat_ids.shape[0], dtype=jnp.int32) // route_ids.shape[1]
    token_of = jnp.zeros((E * capacity,), jnp.int32).at[pair_slot].set(owners)
    filled = jnp.zeros((E * capacity,), jnp.int32).at[pair_slot].set(jnp.ones_like(owners))
    return (pair_slot, token_of, filled)

def head_attention(allowed, operands):
    queries, key_row_block, value_row_block = operands
    scores = low_back(precise_product(queries, key_row_block.T) * HEAD_SIZE ** (-0.5))
    scores = jnp.where(allowed, scores, MASKED)
    highest = lax.optimization_barrier(jnp.max(scores, axis=-1, keepdims=True))
    exponent = jnp.exp(scores - highest)
    weights_full = exponent / lax.optimization_barrier(jnp.sum(exponent, axis=-1, keepdims=True))
    return precise_product(low(weights_full), value_row_block)

def sequence(params, operands):
    gain_first, query_full, gathered_keys, gathered_values, output_full, gain_second, router_full, gate_full, up_full, down_full = params
    tokens_in, segment_ids, route_ids = operands
    total_length = tokens_in.shape[0]
    places = positions(segment_ids)
    token_index = jnp.arange(total_length, dtype=jnp.int32)
    allowed = (segment_ids[:, None] == segment_ids[None, :]) & (token_index[None, :] <= token_index[:, None])
    normalized_input = low(rms_scaled(tokens_in, gain_first))
    query_raw = low_back(precise_product(normalized_input, query_full)).reshape(total_length, QUERY_HEADS, HEAD_SIZE)
    unrotated_keys = low_back(precise_product(normalized_input, gathered_keys)).reshape(total_length, KEY_VALUE_HEADS, HEAD_SIZE)
    values_reduced = low(low_back(precise_product(normalized_input, gathered_values))).reshape(total_length, KEY_VALUE_HEADS, HEAD_SIZE)
    query_low = low(apply_rotary(query_raw, places))
    key_low = low(apply_rotary(unrotated_keys, places))
    heads_per_group = QUERY_HEADS // KEY_VALUE_HEADS
    key_heads = jnp.repeat(key_low, heads_per_group, axis=1).transpose(1, 0, 2)
    value_heads = jnp.repeat(values_reduced, heads_per_group, axis=1).transpose(1, 0, 2)
    mixed_heads = lax.map(jax.checkpoint(partial(head_attention, allowed)), (query_low.transpose(1, 0, 2), key_heads, value_heads))
    attended = low(low_back(mixed_heads.transpose(1, 0, 2).reshape(total_length, QUERY_HEADS * HEAD_SIZE)))
    branch = low_back(precise_product(attended, output_full))
    hidden_mid = tokens_in + branch
    normed_mid = low(rms_scaled(hidden_mid, gain_second))
    logits = low_back(precise_product(normed_mid, router_full))
    chosen = jnp.take_along_axis(logits, route_ids, axis=1)
    chosen_top = lax.optimization_barrier(jnp.max(chosen, axis=-1, keepdims=True))
    exponent = jnp.exp(chosen - chosen_top)
    route_gates = exponent / lax.optimization_barrier(jnp.sum(exponent, axis=-1, keepdims=True))
    pair_slot, token_of, filled = slot_tables(route_ids, CAP)
    expert_in = (normed_mid[token_of] * filled[:, None].astype(jnp.float32)).reshape(E, CAP, MODEL_WIDTH)
    gate_value = low_back(jnp.einsum('ecd,edf->ecf', expert_in, gate_full, precision=lax.Precision.HIGHEST))
    up_value = low_back(jnp.einsum('ecd,edf->ecf', expert_in, up_full, precision=lax.Precision.HIGHEST))
    activation = low(jax.nn.silu(gate_value) * up_value)
    expert_out = low_back(jnp.einsum('ecf,efd->ecd', activation, down_full, precision=lax.Precision.HIGHEST)).reshape(E * CAP, MODEL_WIDTH)
    picked = expert_out[pair_slot].reshape(total_length, TOPK, MODEL_WIDTH)
    return hidden_mid + lax.optimization_barrier(jnp.sum(route_gates[:, :, None] * picked, axis=1))

def reference(hidden_in, segments, routes, attention_gain, query_weight, key_matrix, value_matrix, output_weight, expert_gain, router_weight, gate_weight, up_weight, down_weight, cotangent):
    params = tuple((weight_arg.astype(jnp.float32) for weight_arg in (attention_gain, query_weight, key_matrix, value_matrix, output_weight, expert_gain, router_weight, gate_weight, up_weight, down_weight)))
    tokens = hidden_in.astype(jnp.float32).reshape(SEQS, TOK_DEV, MODEL_WIDTH)
    route_blocks = routes.reshape(SEQS, TOK_DEV, TOPK)

    def forward(params, tokens):
        sequence_step = jax.checkpoint(partial(sequence, params))
        return lax.map(sequence_step, (tokens, segments, route_blocks))
    result, pullback = jax.vjp(forward, params, tokens)
    weight_grads, grad_tokens = pullback(cotangent.astype(jnp.float32).reshape(SEQS, TOK_DEV, MODEL_WIDTH))
    return (result.reshape(TOKENS, MODEL_WIDTH).astype(jnp.bfloat16), grad_tokens.reshape(TOKENS, MODEL_WIDTH), weight_grads[0], weight_grads[1], weight_grads[2], weight_grads[3], weight_grads[4], weight_grads[5], weight_grads[6], weight_grads[7], weight_grads[8], weight_grads[9])
```

```python
import jax
import jax.numpy as jnp
from jax import lax
from jax.sharding import PartitionSpec as P

MODEL_WIDTH = 1536
QUERY_HEADS = 12
KEY_VALUE_HEADS = 2
HEAD_SIZE = 128
E = 32
TOPK = 4


EPSILON = 1e-06
ROPE_BASE = 1000000.0
MASKED = -1e30


def positions(segment_ids):
    total_length = segment_ids.shape[0]
    token_index = jnp.arange(total_length, dtype=jnp.int32)
    earlier = (segment_ids[:, None] == segment_ids[None, :]) & (
        token_index[None, :] < token_index[:, None]
    )
    return jnp.sum(earlier.astype(jnp.int32), axis=1)


def apply_rotary(values, places, direction):
    half_size = values.shape[-1] // 2
    frequency = ROPE_BASE ** (-2.0 * jnp.arange(half_size, dtype=jnp.float32) / values.shape[-1])
    angles = places.astype(jnp.float32)[:, None] * frequency[None, :]
    cosine_part = jnp.cos(angles)[:, None, :]
    sine_part = direction * jnp.sin(angles)[:, None, :]
    first_half = values[..., :half_size]
    second_half = values[..., half_size:]
    return jnp.concatenate(
        [
            first_half * cosine_part - second_half * sine_part,
            second_half * cosine_part + first_half * sine_part,
        ],
        axis=-1,
    )


def slot_ranks(route_ids):
    total_length = route_ids.shape[0]
    token_index = jnp.arange(total_length, dtype=jnp.int32)
    expert_ids = jnp.arange(E, dtype=jnp.int32)
    named = jnp.any(route_ids[:, :, None] == expert_ids[None, None, :], axis=1)
    before = (token_index[None, :] < token_index[:, None]).astype(jnp.bfloat16)
    counts = jnp.dot(before, named.astype(jnp.bfloat16), preferred_element_type=jnp.float32)
    return (named, counts.astype(jnp.int32))


def slot_tables(route_ids, experts, capacity):
    flat_ids = route_ids.reshape(-1)
    named, counts = slot_ranks(route_ids)
    rank_ids = jnp.sum(
        jnp.where(
            route_ids[:, :, None] == jnp.arange(experts, dtype=jnp.int32)[None, None, :],
            counts[:, None, :],
            0,
        ),
        axis=-1,
    ).reshape(-1)
    pair_slot = flat_ids * capacity + rank_ids
    owners = jnp.arange(flat_ids.shape[0], dtype=jnp.int32) // route_ids.shape[1]
    token_of = jnp.zeros((experts * capacity,), jnp.int32).at[pair_slot].set(owners)
    filled = jnp.zeros((experts * capacity,), jnp.int32).at[pair_slot].set(1)
    return (pair_slot, token_of, filled)


def masked_scores(queries, key_row_block, allowed, scaling):
    scores = (
        jnp.einsum("gqd,kd->gqk", queries, key_row_block, preferred_element_type=jnp.float32)
        * scaling
    )
    return jnp.where(allowed[None], scores, MASKED)


def attend_group(operands, allowed, scaling):
    queries, key_row_block, value_row_block = operands
    scores = masked_scores(queries, key_row_block, allowed, scaling)
    highest = jnp.max(scores, axis=-1, keepdims=True)
    exponent = jnp.exp(scores - highest)
    summed = jnp.sum(exponent, axis=-1, keepdims=True)
    weights_low = (exponent / summed).astype(jnp.bfloat16)
    result = jnp.einsum(
        "gqk,kd->gqd", weights_low, value_row_block, preferred_element_type=jnp.float32
    )
    return (result, highest + jnp.log(summed))


def attend_back(operands, allowed, scaling):
    queries, key_row_block, value_row_block, log_total, grad_result = operands
    scores = masked_scores(queries, key_row_block, allowed, scaling)
    weights_full = jnp.where(allowed[None], jnp.exp(scores - log_total), 0.0)
    weights_low = weights_full.astype(jnp.bfloat16)
    grad_values = jnp.einsum(
        "gqk,gqd->kd", weights_low, grad_result, preferred_element_type=jnp.float32
    )
    grad_weights = jnp.einsum(
        "gqd,kd->gqk", grad_result, value_row_block, preferred_element_type=jnp.float32
    )
    centre = jnp.sum(weights_full * grad_weights, axis=-1, keepdims=True)
    grad_scores = (weights_full * (grad_weights - centre)).astype(jnp.bfloat16)
    grad_queries = (
        jnp.einsum("gqk,kd->gqd", grad_scores, key_row_block, preferred_element_type=jnp.float32)
        * scaling
    )
    grad_keys = (
        jnp.einsum("gqk,gqd->kd", grad_scores, queries, preferred_element_type=jnp.float32)
        * scaling
    )
    return (grad_queries, grad_keys, grad_values)


def weights_move(
    hidden_in,
    segments,
    routes,
    attention_gain,
    query_weight,
    key_matrix,
    value_matrix,
    output_weight,
    expert_gain,
    router_weight,
    gate_weight,
    up_weight,
    down_weight,
    cotangent,
):
    gain_first, query_cols, key_cols, value_cols, output_rows = (
        lax.all_gather(attention_gain, "row", axis=0, tiled=True),
        lax.all_gather(query_weight, "row", axis=0, tiled=True),
        lax.all_gather(key_matrix, "row", axis=0, tiled=True),
        lax.all_gather(value_matrix, "row", axis=0, tiled=True),
        lax.all_gather(output_weight, "row", axis=1, tiled=True),
    )
    query_full, gathered_keys, gathered_values, output_full = (
        lax.all_gather(query_cols, "col", axis=1, tiled=True),
        lax.all_gather(key_cols, "col", axis=1, tiled=True),
        lax.all_gather(value_cols, "col", axis=1, tiled=True),
        lax.all_gather(output_rows, "col", axis=0, tiled=True),
    )
    gain_second, router_full, gate_full, up_full, down_full = (
        lax.all_gather(expert_gain, "row", axis=0, tiled=True),
        lax.all_gather(router_weight, "row", axis=0, tiled=True),
        lax.all_gather(gate_weight, "row", axis=1, tiled=True),
        lax.all_gather(up_weight, "row", axis=1, tiled=True),
        lax.all_gather(down_weight, "row", axis=2, tiled=True),
    )
    local_row_block = hidden_in.shape[0]
    sequence_span_length = segments.shape[1]
    first_row = lax.axis_index("col") * local_row_block
    segment_ids = segments[0]
    places_all = positions(segment_ids)
    local_positions = lax.dynamic_slice_in_dim(places_all, first_row, local_row_block)
    own_segments = lax.dynamic_slice_in_dim(segment_ids, first_row, local_row_block)
    query_index = first_row + jnp.arange(local_row_block, dtype=jnp.int32)
    key_index = jnp.arange(sequence_span_length, dtype=jnp.int32)
    allowed = (own_segments[:, None] == segment_ids[None, :]) & (
        key_index[None, :] <= query_index[:, None]
    )
    tokens_in = hidden_in.astype(jnp.float32)
    scale_first = lax.rsqrt(jnp.mean(tokens_in * tokens_in, axis=-1, keepdims=True) + EPSILON)
    unit_first = tokens_in * scale_first
    normed_first = (unit_first * gain_first.astype(jnp.float32)).astype(jnp.bfloat16)
    query_raw = jnp.dot(normed_first, query_full, preferred_element_type=jnp.float32).reshape(
        local_row_block, QUERY_HEADS, HEAD_SIZE
    )
    unrotated_keys = jnp.dot(
        normed_first, gathered_keys, preferred_element_type=jnp.float32
    ).reshape(local_row_block, KEY_VALUE_HEADS, HEAD_SIZE)
    values_reduced = jnp.dot(
        normed_first, gathered_values, preferred_element_type=jnp.float32
    ).astype(jnp.bfloat16)
    rotated_queries = apply_rotary(query_raw, local_positions, 1.0).astype(jnp.bfloat16)
    rotated_keys = (
        apply_rotary(unrotated_keys, local_positions, 1.0)
        .astype(jnp.bfloat16)
        .reshape(local_row_block, KEY_VALUE_HEADS * HEAD_SIZE)
    )
    key_row_block, value_row_block = (
        lax.all_gather(rotated_keys, "col", axis=0, tiled=True),
        lax.all_gather(values_reduced, "col", axis=0, tiled=True),
    )
    heads_per_group = QUERY_HEADS // KEY_VALUE_HEADS
    scaling = HEAD_SIZE ** (-0.5)
    grouped_queries = rotated_queries.reshape(
        local_row_block, KEY_VALUE_HEADS, heads_per_group, HEAD_SIZE
    ).transpose(1, 2, 0, 3)
    grouped_keys = key_row_block.reshape(
        sequence_span_length, KEY_VALUE_HEADS, HEAD_SIZE
    ).transpose(1, 0, 2)
    grouped_values = value_row_block.reshape(
        sequence_span_length, KEY_VALUE_HEADS, HEAD_SIZE
    ).transpose(1, 0, 2)
    attended, log_total = lax.map(
        lambda operands: attend_group(operands, allowed, scaling),
        (grouped_queries, grouped_keys, grouped_values),
    )
    attended_low = (
        attended.transpose(2, 0, 1, 3)
        .reshape(local_row_block, QUERY_HEADS * HEAD_SIZE)
        .astype(jnp.bfloat16)
    )
    branch = jnp.dot(attended_low, output_full, preferred_element_type=jnp.float32)
    hidden_mid = tokens_in + branch
    scale_second = lax.rsqrt(jnp.mean(hidden_mid * hidden_mid, axis=-1, keepdims=True) + EPSILON)
    unit_second = hidden_mid * scale_second
    normed_second = (unit_second * gain_second.astype(jnp.float32)).astype(jnp.bfloat16)
    normed_all, upstream_all = (
        lax.all_gather(normed_second, "col", axis=0, tiled=True),
        lax.all_gather(cotangent, "col", axis=0, tiled=True),
    )
    logits = jnp.dot(normed_all, router_full, preferred_element_type=jnp.float32)
    expert_ids = jnp.arange(E, dtype=jnp.int32)
    chosen_mask = routes[:, :, None] == expert_ids[None, None, :]
    chosen = jnp.sum(jnp.where(chosen_mask, logits[:, None, :], 0.0), axis=-1)
    exponent = jnp.exp(chosen - jnp.max(chosen, axis=-1, keepdims=True))
    route_gates = exponent / jnp.sum(exponent, axis=-1, keepdims=True)
    group_width = 4
    capacity = max(2, 3 * sequence_span_length * TOPK // (2 * E))
    pair_slot, token_of, filled = slot_tables(routes, E, capacity)
    slot_gate = jnp.zeros((E * capacity,), jnp.float32).at[pair_slot].set(route_gates.reshape(-1))
    group_rows = group_width * capacity

    def expert_step(accumulated, group_index):
        mixture_sum, input_sum = accumulated
        offset = group_index * group_rows
        row_ids = lax.dynamic_slice_in_dim(token_of, offset, group_rows)
        occupied = lax.dynamic_slice_in_dim(filled, offset, group_rows) > 0
        slot_weight = lax.dynamic_slice_in_dim(slot_gate, offset, group_rows)
        first_expert = group_index * group_width
        gate_block = lax.dynamic_slice_in_dim(gate_full, first_expert, group_width, 0)
        up_block = lax.dynamic_slice_in_dim(up_full, first_expert, group_width, 0)
        down_block = lax.dynamic_slice_in_dim(down_full, first_expert, group_width, 0)
        inputs = jnp.where(
            occupied[:, None], normed_all[row_ids], jnp.zeros((), jnp.bfloat16)
        ).reshape(group_width, capacity, MODEL_WIDTH)
        upstream = upstream_all[row_ids].astype(jnp.float32)
        gate_value = jnp.einsum(
            "ecd,edf->ecf", inputs, gate_block, preferred_element_type=jnp.float32
        )
        up_value = jnp.einsum("ecd,edf->ecf", inputs, up_block, preferred_element_type=jnp.float32)
        sigmoid_gate = jax.nn.sigmoid(gate_value)
        silu_gate = gate_value * sigmoid_gate
        activation = (silu_gate * up_value).astype(jnp.bfloat16)
        partial_out = jnp.einsum(
            "ecf,efd->ecd", activation, down_block, preferred_element_type=jnp.float32
        ).reshape(group_rows, MODEL_WIDTH)
        mixture_sum = mixture_sum.at[row_ids].add(partial_out * slot_weight[:, None])
        slot_grad = jnp.sum(partial_out * upstream, axis=-1)
        grad_expert = (
            (upstream * slot_weight[:, None])
            .astype(jnp.bfloat16)
            .reshape(group_width, capacity, MODEL_WIDTH)
        )
        grad_act = jnp.einsum(
            "ecd,efd->ecf", grad_expert, down_block, preferred_element_type=jnp.float32
        )
        slope = sigmoid_gate * (1.0 + gate_value * (1.0 - sigmoid_gate))
        grad_gate = (grad_act * up_value * slope).astype(jnp.bfloat16)
        grad_up = (grad_act * silu_gate).astype(jnp.bfloat16)
        grad_inputs = jnp.einsum(
            "ecf,edf->ecd", grad_gate, gate_block, preferred_element_type=jnp.float32
        )
        grad_inputs = grad_inputs + jnp.einsum(
            "ecf,edf->ecd", grad_up, up_block, preferred_element_type=jnp.float32
        )
        input_sum = input_sum.at[row_ids].add(grad_inputs.reshape(group_rows, MODEL_WIDTH))
        gate_piece = jnp.einsum(
            "ecd,ecf->edf", inputs, grad_gate, preferred_element_type=jnp.float32
        )
        up_piece = jnp.einsum("ecd,ecf->edf", inputs, grad_up, preferred_element_type=jnp.float32)
        down_piece = jnp.einsum(
            "ecf,ecd->efd", activation, grad_expert, preferred_element_type=jnp.float32
        )
        return ((mixture_sum, input_sum), (slot_grad, gate_piece, up_piece, down_piece))

    initial = (
        jnp.zeros((sequence_span_length, MODEL_WIDTH), jnp.float32),
        jnp.zeros((sequence_span_length, MODEL_WIDTH), jnp.float32),
    )
    sums_out, pieces = lax.scan(expert_step, initial, jnp.arange(E // group_width, dtype=jnp.int32))
    mixture_part, input_part = sums_out
    slot_grads, gate_pieces, up_pieces, down_pieces = pieces
    hidden_cols = gate_full.shape[2]
    gate_grad = gate_pieces.reshape(E, MODEL_WIDTH, hidden_cols)
    up_grad = up_pieces.reshape(E, MODEL_WIDTH, hidden_cols)
    down_grad = down_pieces.reshape(E, hidden_cols, MODEL_WIDTH)
    pick_grads = slot_grads.reshape(-1)[pair_slot].reshape(sequence_span_length, TOPK)
    mixture_own, input_own, pick_own = (
        lax.psum_scatter(mixture_part, "col", scatter_dimension=0, tiled=True),
        lax.psum_scatter(input_part, "col", scatter_dimension=0, tiled=True),
        lax.psum_scatter(pick_grads, "col", scatter_dimension=0, tiled=True),
    )
    block_out = (hidden_mid + mixture_own).astype(jnp.bfloat16)
    own_gates = lax.dynamic_slice_in_dim(route_gates, first_row, local_row_block)
    own_mask = lax.dynamic_slice_in_dim(chosen_mask, first_row, local_row_block)
    centred = own_gates * (pick_own - jnp.sum(own_gates * pick_own, axis=-1, keepdims=True))
    grad_logits = jnp.sum(jnp.where(own_mask, centred[:, :, None], 0.0), axis=1).astype(
        jnp.bfloat16
    )
    grad_normed = input_own + jnp.dot(
        grad_logits, router_full.T, preferred_element_type=jnp.float32
    )
    router_grad = jnp.dot(normed_second.T, grad_logits, preferred_element_type=jnp.float32)
    tilted_second = grad_normed * gain_second.astype(jnp.float32)
    gain_second_grad = jnp.sum(grad_normed * unit_second, axis=0)
    grad_hidden = cotangent.astype(jnp.float32) + scale_second * (
        tilted_second - unit_second * jnp.mean(tilted_second * unit_second, axis=-1, keepdims=True)
    )
    grad_branch = grad_hidden.astype(jnp.bfloat16)
    output_grad = jnp.dot(attended_low.T, grad_branch, preferred_element_type=jnp.float32)
    attended_gradient = jnp.dot(
        grad_branch, output_full.T, preferred_element_type=jnp.float32
    ).astype(jnp.bfloat16)
    grouped_gradient = attended_gradient.reshape(
        local_row_block, KEY_VALUE_HEADS, heads_per_group, HEAD_SIZE
    ).transpose(1, 2, 0, 3)
    grad_query_groups, key_gradient_grouped, value_gradient_grouped = lax.map(
        lambda operands: attend_back(operands, allowed, scaling),
        (grouped_queries, grouped_keys, grouped_values, log_total, grouped_gradient),
    )
    grad_query_rot = grad_query_groups.transpose(2, 0, 1, 3).reshape(
        local_row_block, QUERY_HEADS, HEAD_SIZE
    )
    key_gradient_total = key_gradient_grouped.transpose(1, 0, 2).reshape(
        sequence_span_length, KEY_VALUE_HEADS * HEAD_SIZE
    )
    value_gradient_total = value_gradient_grouped.transpose(1, 0, 2).reshape(
        sequence_span_length, KEY_VALUE_HEADS * HEAD_SIZE
    )
    local_keys, value_own = (
        lax.psum_scatter(
            key_gradient_total.astype(jnp.bfloat16), "col", scatter_dimension=0, tiled=True
        ).astype(jnp.float32),
        lax.psum_scatter(
            value_gradient_total.astype(jnp.bfloat16), "col", scatter_dimension=0, tiled=True
        ).astype(jnp.float32),
    )
    grad_query_low = (
        apply_rotary(grad_query_rot, local_positions, -1.0)
        .reshape(local_row_block, QUERY_HEADS * HEAD_SIZE)
        .astype(jnp.bfloat16)
    )
    grad_key_low = (
        apply_rotary(
            local_keys.reshape(local_row_block, KEY_VALUE_HEADS, HEAD_SIZE), local_positions, -1.0
        )
        .reshape(local_row_block, KEY_VALUE_HEADS * HEAD_SIZE)
        .astype(jnp.bfloat16)
    )
    grad_value_low = value_own.astype(jnp.bfloat16)
    grad_normed_first = jnp.dot(grad_query_low, query_full.T, preferred_element_type=jnp.float32)
    grad_normed_first = grad_normed_first + jnp.dot(
        grad_key_low, gathered_keys.T, preferred_element_type=jnp.float32
    )
    grad_normed_first = grad_normed_first + jnp.dot(
        grad_value_low, gathered_values.T, preferred_element_type=jnp.float32
    )
    query_grad = jnp.dot(normed_first.T, grad_query_low, preferred_element_type=jnp.float32)
    key_grad = jnp.dot(normed_first.T, grad_key_low, preferred_element_type=jnp.float32)
    value_grad = jnp.dot(normed_first.T, grad_value_low, preferred_element_type=jnp.float32)
    tilted_first = grad_normed_first * gain_first.astype(jnp.float32)
    gain_first_grad = jnp.sum(grad_normed_first * unit_first, axis=0)
    input_grad = grad_hidden + scale_first * (
        tilted_first - unit_first * jnp.mean(tilted_first * unit_first, axis=-1, keepdims=True)
    )
    query_part, key_part, value_part, output_part = (
        lax.psum_scatter(
            query_grad.astype(jnp.bfloat16), "col", scatter_dimension=1, tiled=True
        ).astype(jnp.float32),
        lax.psum_scatter(
            key_grad.astype(jnp.bfloat16), "col", scatter_dimension=1, tiled=True
        ).astype(jnp.float32),
        lax.psum_scatter(
            value_grad.astype(jnp.bfloat16), "col", scatter_dimension=1, tiled=True
        ).astype(jnp.float32),
        lax.psum_scatter(
            output_grad.astype(jnp.bfloat16), "col", scatter_dimension=0, tiled=True
        ).astype(jnp.float32),
    )
    small_total = lax.psum((gain_first_grad, gain_second_grad, router_grad), ("row", "col"))
    query_out, key_out, value_out, output_out, gate_out, up_out, down_out = (
        lax.psum_scatter(
            query_part.astype(jnp.bfloat16), "row", scatter_dimension=0, tiled=True
        ).astype(jnp.float32),
        lax.psum_scatter(
            key_part.astype(jnp.bfloat16), "row", scatter_dimension=0, tiled=True
        ).astype(jnp.float32),
        lax.psum_scatter(
            value_part.astype(jnp.bfloat16), "row", scatter_dimension=0, tiled=True
        ).astype(jnp.float32),
        lax.psum_scatter(
            output_part.astype(jnp.bfloat16), "row", scatter_dimension=1, tiled=True
        ).astype(jnp.float32),
        lax.psum_scatter(
            gate_grad.astype(jnp.bfloat16), "row", scatter_dimension=1, tiled=True
        ).astype(jnp.float32),
        lax.psum_scatter(
            up_grad.astype(jnp.bfloat16), "row", scatter_dimension=1, tiled=True
        ).astype(jnp.float32),
        lax.psum_scatter(
            down_grad.astype(jnp.bfloat16), "row", scatter_dimension=2, tiled=True
        ).astype(jnp.float32),
    )
    row_block = attention_gain.shape[0]
    row_start = lax.axis_index("row") * row_block
    gain_first_out = lax.dynamic_slice_in_dim(small_total[0], row_start, row_block)
    gain_second_out = lax.dynamic_slice_in_dim(small_total[1], row_start, row_block)
    router_out = lax.dynamic_slice_in_dim(small_total[2], row_start, row_block, 0)
    return (
        block_out,
        input_grad,
        gain_first_out,
        query_out,
        key_out,
        value_out,
        output_out,
        gain_second_out,
        router_out,
        gate_out,
        up_out,
        down_out,
    )


GRID = ("row", "col")


def swap_cores(block):
    return lax.ppermute(block, "col", [(0, 1), (1, 0)])


def both_cores(own, core):
    other = swap_cores(own)
    return jnp.where(
        core == 0,
        jnp.concatenate([own, other], axis=0),
        jnp.concatenate([other, own], axis=0),
    )


def sum_cores(partial, core):
    half = partial.shape[0] // 2
    away = lax.dynamic_slice_in_dim(partial, (1 - core) * half, half)
    kept = lax.dynamic_slice_in_dim(partial, core * half, half)
    return kept + swap_cores(away)


def exchange(block):
    return lax.all_to_all(block, GRID, split_axis=0, concat_axis=0, tiled=True)


def tokens_move(
    hidden_in,
    segments,
    routes,
    attention_gain,
    query_weight,
    key_matrix,
    value_matrix,
    output_weight,
    expert_gain,
    router_weight,
    gate_weight,
    up_weight,
    down_weight,
    cotangent,
):
    bf16, f32 = jnp.bfloat16, jnp.float32
    core = lax.axis_index("col")
    local = hidden_in.shape[0]
    span = segments.shape[1]
    rows = MODEL_WIDTH // query_weight.shape[0]
    row_block = query_weight.shape[0]
    hidden_block = gate_weight.shape[2]
    ffe = 2 * hidden_block
    capacity = max(2, 3 * span * TOPK // (2 * E))
    share = capacity // 2
    head_cols = query_weight.shape[1]
    kv_cols = key_matrix.shape[1]
    heads = head_cols // HEAD_SIZE

    packed = jnp.concatenate(
        [
            query_weight,
            key_matrix,
            value_matrix,
            output_weight.T,
            router_weight,
            attention_gain[:, None],
            expert_gain[:, None],
            jnp.zeros((row_block, 128 - E - 2), bf16),
        ],
        axis=1,
    )
    packed_full = lax.all_gather(packed, "row", axis=0, tiled=True)
    o0 = head_cols + 2 * kv_cols
    o1 = o0 + head_cols
    query_cols = packed_full[:, :head_cols]
    qkv_cols = packed_full[:, :o0]
    output_t = packed_full[:, o0:o1]
    router_full = packed_full[:, o1 : o1 + E]
    gain_first = packed_full[:, o1 + E].astype(f32)
    gain_second = packed_full[:, o1 + E + 1].astype(f32)

    named, counts = slot_ranks(routes)
    slot_of = jnp.where(named, counts, -1).T
    share_slots = core * share + jnp.arange(share, dtype=jnp.int32)
    pick = (slot_of[:, None, :] == share_slots[None, :, None]).astype(bf16)
    pick = pick.reshape(E * share, span)

    cotangent_all = both_cores(cotangent, core)
    cot_share = jnp.dot(pick, cotangent_all, preferred_element_type=f32).astype(bf16)
    upstream = exchange(cot_share)
    gate_e = exchange(gate_weight)
    up_e = exchange(up_weight)
    down_e = exchange(down_weight.transpose(0, 2, 1))

    def whole_weight(blocks):
        return (
            blocks.reshape(rows, 2, row_block, hidden_block)
            .transpose(0, 2, 1, 3)
            .reshape(MODEL_WIDTH, ffe)
        )

    hidden_all = both_cores(hidden_in, core)
    tokens_all = hidden_all.astype(f32)
    scale_all = lax.rsqrt(jnp.mean(tokens_all * tokens_all, axis=-1, keepdims=True) + EPSILON)
    normed_all = (tokens_all * scale_all * gain_first).astype(bf16)
    segment_ids = segments[0]
    places = positions(segment_ids)
    token_index = jnp.arange(span, dtype=jnp.int32)
    allowed = (segment_ids[:, None] == segment_ids[None, :]) & (
        token_index[None, :] <= token_index[:, None]
    )
    raw = jnp.dot(normed_all, qkv_cols, preferred_element_type=f32)
    queries = apply_rotary(raw[:, :head_cols].reshape(span, heads, HEAD_SIZE), places, 1.0)
    queries = queries.astype(bf16).transpose(1, 0, 2)
    keys = apply_rotary(
        raw[:, head_cols : head_cols + kv_cols].reshape(span, 1, HEAD_SIZE), places, 1.0
    ).astype(bf16)[:, 0]
    values = raw[:, head_cols + kv_cols :].astype(bf16)
    scaling = HEAD_SIZE ** (-0.5)
    attended, log_total = attend_group((queries, keys, values), allowed, scaling)
    attended_low = attended.transpose(1, 0, 2).reshape(span, head_cols).astype(bf16)
    branch_part = lax.dot_general(
        attended_low, output_t, (((1,), (1,)), ((), ())), preferred_element_type=f32
    )
    tokens_in = hidden_in.astype(f32)
    hidden_mid = tokens_in + sum_cores(branch_part, core)
    scale_second = lax.rsqrt(jnp.mean(hidden_mid * hidden_mid, axis=-1, keepdims=True) + EPSILON)
    unit_second = hidden_mid * scale_second
    normed_second = (unit_second * gain_second).astype(bf16)
    second_all = both_cores(normed_second, core)

    logits = jnp.dot(second_all, router_full, preferred_element_type=f32)
    masked = jnp.where(named, logits, MASKED)
    exponent = jnp.where(named, jnp.exp(masked - jnp.max(masked, axis=-1, keepdims=True)), 0.0)
    gates = exponent / jnp.sum(exponent, axis=-1, keepdims=True)

    expert_in = exchange(jnp.dot(pick, second_all, preferred_element_type=f32).astype(bf16))
    pick3 = pick.reshape(E, share, span)
    slot_gate = jnp.sum(pick3.astype(f32) * gates.T[:, None, :], axis=-1)
    slot_gate = exchange(slot_gate).reshape(-1, 1)

    gate_w, up_w, down_t = whole_weight(gate_e), whole_weight(up_e), whole_weight(down_e)
    nt = (((1,), (1,)), ((), ()))
    tn = (((0,), (0,)), ((), ()))
    gate_value = jnp.dot(expert_in, gate_w, preferred_element_type=f32)
    up_value = jnp.dot(expert_in, up_w, preferred_element_type=f32)
    sigmoid_gate = jax.nn.sigmoid(gate_value)
    silu_gate = gate_value * sigmoid_gate
    activation = (silu_gate * up_value).astype(bf16)
    expert_out = lax.dot_general(activation, down_t, nt, preferred_element_type=f32)
    up32 = upstream.astype(f32)
    slot_grad = jnp.sum(expert_out * up32, axis=-1)
    returned = exchange((expert_out * slot_gate).astype(bf16))
    grad_expert = (up32 * slot_gate).astype(bf16)
    grad_act = jnp.dot(grad_expert, down_t, preferred_element_type=f32)
    slope = sigmoid_gate * (1.0 + gate_value * (1.0 - sigmoid_gate))
    grad_gate = (grad_act * up_value * slope).astype(bf16)
    grad_up = (grad_act * silu_gate).astype(bf16)
    grad_in = lax.dot_general(grad_gate, gate_w, nt, preferred_element_type=f32)
    grad_in = grad_in + lax.dot_general(grad_up, up_w, nt, preferred_element_type=f32)
    grad_back = exchange(grad_in.astype(bf16))
    slot_grad = exchange(slot_grad.reshape(E, share))

    def shard_grad(left, right):
        full = lax.dot_general(left, right, tn, preferred_element_type=f32).astype(bf16)
        blocks = full.reshape(rows, row_block, 2, hidden_block).transpose(0, 2, 1, 3)
        return exchange(blocks.reshape(E, row_block, hidden_block)).astype(f32)

    def combine(slots):
        return sum_cores(lax.dot_general(pick, slots, tn, preferred_element_type=f32), core)

    input_own = combine(grad_back.reshape(E * share, MODEL_WIDTH))
    pick_part = jnp.sum(pick3.astype(f32) * slot_grad[:, :, None], axis=1).T
    pick_own = sum_cores(pick_part, core)
    own_gates = lax.dynamic_slice_in_dim(gates, core * local, local)
    centred = own_gates * (pick_own - jnp.sum(own_gates * pick_own, axis=-1, keepdims=True))
    grad_logits = centred.astype(bf16)
    grad_normed = input_own + lax.dot_general(
        grad_logits, router_full, nt, preferred_element_type=f32
    )
    router_grad = lax.dot_general(normed_second, grad_logits, tn, preferred_element_type=f32)
    tilted = grad_normed * gain_second
    gain_second_grad = jnp.sum(grad_normed * unit_second, axis=0)
    grad_hidden = cotangent.astype(f32) + scale_second * (
        tilted - unit_second * jnp.mean(tilted * unit_second, axis=-1, keepdims=True)
    )
    branch_all = both_cores(grad_hidden.astype(bf16), core)

    output_t_grad = lax.dot_general(branch_all, attended_low, tn, preferred_element_type=f32)
    grad_attended = jnp.dot(branch_all, output_t, preferred_element_type=f32).astype(bf16)
    grad_attended = grad_attended.reshape(span, heads, HEAD_SIZE).transpose(1, 0, 2)
    grad_queries, grad_keys, grad_values = attend_back(
        (queries, keys, values, log_total, grad_attended), allowed, scaling
    )
    grad_query_low = (
        apply_rotary(grad_queries.transpose(1, 0, 2), places, -1.0)
        .reshape(span, head_cols)
        .astype(bf16)
    )
    grad_key_low = apply_rotary(grad_keys[:, None], places, -1.0)[:, 0].astype(bf16)
    grad_qkv = jnp.concatenate([grad_query_low, grad_key_low, grad_values.astype(bf16)], axis=1)
    first_part = lax.dot_general(grad_qkv, qkv_cols, nt, preferred_element_type=f32)
    qkv_grad = lax.dot_general(normed_all, grad_qkv, tn, preferred_element_type=f32)
    grad_first = sum_cores(first_part, core)
    scale_first = lax.dynamic_slice_in_dim(scale_all, core * local, local)
    unit_first = tokens_in * scale_first
    tilted_first = grad_first * gain_first
    gain_first_grad = jnp.sum(grad_first * unit_first, axis=0)
    input_grad = grad_hidden + scale_first * (
        tilted_first - unit_first * jnp.mean(tilted_first * unit_first, axis=-1, keepdims=True)
    )
    block_out = (hidden_mid + combine(returned.reshape(E * share, MODEL_WIDTH))).astype(bf16)

    gate_out = shard_grad(expert_in, grad_gate)
    up_out = shard_grad(expert_in, grad_up)
    down_out = shard_grad(grad_expert, activation).transpose(0, 2, 1)
    packed_grad = jnp.concatenate([qkv_grad, output_t_grad], axis=1).astype(bf16)
    packed_own = lax.psum_scatter(packed_grad, "row", scatter_dimension=0, tiled=True).astype(f32)
    small = jnp.concatenate(
        [router_grad, gain_first_grad[:, None], gain_second_grad[:, None]], axis=1
    )
    small = lax.psum(small, GRID)
    small_own = lax.dynamic_slice_in_dim(small, lax.axis_index("row") * row_block, row_block)
    return (
        block_out,
        input_grad,
        small_own[:, E],
        packed_own[:, :head_cols],
        packed_own[:, head_cols : head_cols + kv_cols],
        packed_own[:, head_cols + kv_cols : o0],
        packed_own[:, o0:].T,
        small_own[:, E + 1],
        small_own[:, :E],
        gate_out,
        up_out,
        down_out,
    )


def solution(mesh):
    in_specs = (
        P(("row", "col"), None),
        P("row", None),
        P("row", None),
        P("row"),
        P("row", "col"),
        P("row", "col"),
        P("row", "col"),
        P("col", "row"),
        P("row"),
        P("row", None),
        P(None, "row", "col"),
        P(None, "row", "col"),
        P(None, "col", "row"),
        P(("row", "col"), None),
    )
    out_specs = (
        P(("row", "col"), None),
        P(("row", "col"), None),
        P("row"),
        P("row", "col"),
        P("row", "col"),
        P("row", "col"),
        P("col", "row"),
        P("row"),
        P("row", None),
        P(None, "row", "col"),
        P(None, "row", "col"),
        P(None, "col", "row"),
    )
    rows, cols = mesh.shape["row"], mesh.shape["col"]
    one_each = rows * cols == E and cols == KEY_VALUE_HEADS
    return jax.shard_map(
        tokens_move if one_each else weights_move, mesh=mesh,
        in_specs=in_specs,
        out_specs=out_specs,
        check_vma=False,
    )
```

```python
import jax
import jax.numpy as jnp
from jax import lax
from jax.experimental import pallas as pl
from jax.experimental.pallas import tpu as pltpu
from jax.sharding import PartitionSpec as P

MODEL_WIDTH = 1536
QUERY_HEADS = 12
KEY_VALUE_HEADS = 2
HEAD_SIZE = 128
E = 32
TOPK = 4


EPSILON = 1e-06
ROPE_BASE = 1000000.0
MASKED = -1e30


def positions(segment_ids):
    total_length = segment_ids.shape[0]
    token_index = jnp.arange(total_length, dtype=jnp.int32)
    earlier = (segment_ids[:, None] == segment_ids[None, :]) & (
        token_index[None, :] < token_index[:, None]
    )
    return jnp.sum(earlier.astype(jnp.int32), axis=1)


def apply_rotary(values, places, direction):
    half_size = values.shape[-1] // 2
    frequency = ROPE_BASE ** (-2.0 * jnp.arange(half_size, dtype=jnp.float32) / values.shape[-1])
    angles = places.astype(jnp.float32)[:, None] * frequency[None, :]
    cosine_part = jnp.cos(angles)[:, None, :]
    sine_part = direction * jnp.sin(angles)[:, None, :]
    first_half = values[..., :half_size]
    second_half = values[..., half_size:]
    return jnp.concatenate(
        [
            first_half * cosine_part - second_half * sine_part,
            second_half * cosine_part + first_half * sine_part,
        ],
        axis=-1,
    )


def slot_ranks(route_ids):
    total_length = route_ids.shape[0]
    token_index = jnp.arange(total_length, dtype=jnp.int32)
    expert_ids = jnp.arange(E, dtype=jnp.int32)
    named = jnp.any(route_ids[:, :, None] == expert_ids[None, None, :], axis=1)
    before = (token_index[None, :] < token_index[:, None]).astype(jnp.bfloat16)
    counts = jnp.dot(before, named.astype(jnp.bfloat16), preferred_element_type=jnp.float32)
    return (named, counts.astype(jnp.int32))


def slot_tables(route_ids, experts, capacity):
    flat_ids = route_ids.reshape(-1)
    named, counts = slot_ranks(route_ids)
    rank_ids = jnp.sum(
        jnp.where(
            route_ids[:, :, None] == jnp.arange(experts, dtype=jnp.int32)[None, None, :],
            counts[:, None, :],
            0,
        ),
        axis=-1,
    ).reshape(-1)
    pair_slot = flat_ids * capacity + rank_ids
    owners = jnp.arange(flat_ids.shape[0], dtype=jnp.int32) // route_ids.shape[1]
    token_of = jnp.zeros((experts * capacity,), jnp.int32).at[pair_slot].set(owners)
    filled = jnp.zeros((experts * capacity,), jnp.int32).at[pair_slot].set(1)
    return (pair_slot, token_of, filled)


def masked_scores(queries, key_row_block, allowed, scaling):
    scores = (
        jnp.einsum("gqd,kd->gqk", queries, key_row_block, preferred_element_type=jnp.float32)
        * scaling
    )
    return jnp.where(allowed[None], scores, MASKED)


def attend_group(operands, allowed, scaling):
    queries, key_row_block, value_row_block = operands
    scores = masked_scores(queries, key_row_block, allowed, scaling)
    highest = jnp.max(scores, axis=-1, keepdims=True)
    exponent = jnp.exp(scores - highest)
    summed = jnp.sum(exponent, axis=-1, keepdims=True)
    weights_low = (exponent / summed).astype(jnp.bfloat16)
    result = jnp.einsum(
        "gqk,kd->gqd", weights_low, value_row_block, preferred_element_type=jnp.float32
    )
    return (result, highest + jnp.log(summed))


def attend_back(operands, allowed, scaling):
    queries, key_row_block, value_row_block, log_total, grad_result = operands
    scores = masked_scores(queries, key_row_block, allowed, scaling)
    weights_full = jnp.where(allowed[None], jnp.exp(scores - log_total), 0.0)
    weights_low = weights_full.astype(jnp.bfloat16)
    grad_values = jnp.einsum(
        "gqk,gqd->kd", weights_low, grad_result, preferred_element_type=jnp.float32
    )
    grad_weights = jnp.einsum(
        "gqd,kd->gqk", grad_result, value_row_block, preferred_element_type=jnp.float32
    )
    centre = jnp.sum(weights_full * grad_weights, axis=-1, keepdims=True)
    grad_scores = (weights_full * (grad_weights - centre)).astype(jnp.bfloat16)
    grad_queries = (
        jnp.einsum("gqk,kd->gqd", grad_scores, key_row_block, preferred_element_type=jnp.float32)
        * scaling
    )
    grad_keys = (
        jnp.einsum("gqk,gqd->kd", grad_scores, queries, preferred_element_type=jnp.float32)
        * scaling
    )
    return (grad_queries, grad_keys, grad_values)


def weights_move(
    hidden_in,
    segments,
    routes,
    attention_gain,
    query_weight,
    key_matrix,
    value_matrix,
    output_weight,
    expert_gain,
    router_weight,
    gate_weight,
    up_weight,
    down_weight,
    cotangent,
):
    gain_first, query_cols, key_cols, value_cols, output_rows = (
        lax.all_gather(attention_gain, "row", axis=0, tiled=True),
        lax.all_gather(query_weight, "row", axis=0, tiled=True),
        lax.all_gather(key_matrix, "row", axis=0, tiled=True),
        lax.all_gather(value_matrix, "row", axis=0, tiled=True),
        lax.all_gather(output_weight, "row", axis=1, tiled=True),
    )
    query_full, gathered_keys, gathered_values, output_full = (
        lax.all_gather(query_cols, "col", axis=1, tiled=True),
        lax.all_gather(key_cols, "col", axis=1, tiled=True),
        lax.all_gather(value_cols, "col", axis=1, tiled=True),
        lax.all_gather(output_rows, "col", axis=0, tiled=True),
    )
    gain_second, router_full, gate_full, up_full, down_full = (
        lax.all_gather(expert_gain, "row", axis=0, tiled=True),
        lax.all_gather(router_weight, "row", axis=0, tiled=True),
        lax.all_gather(gate_weight, "row", axis=1, tiled=True),
        lax.all_gather(up_weight, "row", axis=1, tiled=True),
        lax.all_gather(down_weight, "row", axis=2, tiled=True),
    )
    local_row_block = hidden_in.shape[0]
    sequence_span_length = segments.shape[1]
    first_row = lax.axis_index("col") * local_row_block
    segment_ids = segments[0]
    places_all = positions(segment_ids)
    local_positions = lax.dynamic_slice_in_dim(places_all, first_row, local_row_block)
    own_segments = lax.dynamic_slice_in_dim(segment_ids, first_row, local_row_block)
    query_index = first_row + jnp.arange(local_row_block, dtype=jnp.int32)
    key_index = jnp.arange(sequence_span_length, dtype=jnp.int32)
    allowed = (own_segments[:, None] == segment_ids[None, :]) & (
        key_index[None, :] <= query_index[:, None]
    )
    tokens_in = hidden_in.astype(jnp.float32)
    scale_first = lax.rsqrt(jnp.mean(tokens_in * tokens_in, axis=-1, keepdims=True) + EPSILON)
    unit_first = tokens_in * scale_first
    normed_first = (unit_first * gain_first.astype(jnp.float32)).astype(jnp.bfloat16)
    query_raw = jnp.dot(normed_first, query_full, preferred_element_type=jnp.float32).reshape(
        local_row_block, QUERY_HEADS, HEAD_SIZE
    )
    unrotated_keys = jnp.dot(
        normed_first, gathered_keys, preferred_element_type=jnp.float32
    ).reshape(local_row_block, KEY_VALUE_HEADS, HEAD_SIZE)
    values_reduced = jnp.dot(
        normed_first, gathered_values, preferred_element_type=jnp.float32
    ).astype(jnp.bfloat16)
    rotated_queries = apply_rotary(query_raw, local_positions, 1.0).astype(jnp.bfloat16)
    rotated_keys = (
        apply_rotary(unrotated_keys, local_positions, 1.0)
        .astype(jnp.bfloat16)
        .reshape(local_row_block, KEY_VALUE_HEADS * HEAD_SIZE)
    )
    key_row_block, value_row_block = (
        lax.all_gather(rotated_keys, "col", axis=0, tiled=True),
        lax.all_gather(values_reduced, "col", axis=0, tiled=True),
    )
    heads_per_group = QUERY_HEADS // KEY_VALUE_HEADS
    scaling = HEAD_SIZE ** (-0.5)
    grouped_queries = rotated_queries.reshape(
        local_row_block, KEY_VALUE_HEADS, heads_per_group, HEAD_SIZE
    ).transpose(1, 2, 0, 3)
    grouped_keys = key_row_block.reshape(
        sequence_span_length, KEY_VALUE_HEADS, HEAD_SIZE
    ).transpose(1, 0, 2)
    grouped_values = value_row_block.reshape(
        sequence_span_length, KEY_VALUE_HEADS, HEAD_SIZE
    ).transpose(1, 0, 2)
    attended, log_total = lax.map(
        lambda operands: attend_group(operands, allowed, scaling),
        (grouped_queries, grouped_keys, grouped_values),
    )
    attended_low = (
        attended.transpose(2, 0, 1, 3)
        .reshape(local_row_block, QUERY_HEADS * HEAD_SIZE)
        .astype(jnp.bfloat16)
    )
    branch = jnp.dot(attended_low, output_full, preferred_element_type=jnp.float32)
    hidden_mid = tokens_in + branch
    scale_second = lax.rsqrt(jnp.mean(hidden_mid * hidden_mid, axis=-1, keepdims=True) + EPSILON)
    unit_second = hidden_mid * scale_second
    normed_second = (unit_second * gain_second.astype(jnp.float32)).astype(jnp.bfloat16)
    normed_all, upstream_all = (
        lax.all_gather(normed_second, "col", axis=0, tiled=True),
        lax.all_gather(cotangent, "col", axis=0, tiled=True),
    )
    logits = jnp.dot(normed_all, router_full, preferred_element_type=jnp.float32)
    expert_ids = jnp.arange(E, dtype=jnp.int32)
    chosen_mask = routes[:, :, None] == expert_ids[None, None, :]
    chosen = jnp.sum(jnp.where(chosen_mask, logits[:, None, :], 0.0), axis=-1)
    exponent = jnp.exp(chosen - jnp.max(chosen, axis=-1, keepdims=True))
    route_gates = exponent / jnp.sum(exponent, axis=-1, keepdims=True)
    group_width = 4
    capacity = max(2, 3 * sequence_span_length * TOPK // (2 * E))
    pair_slot, token_of, filled = slot_tables(routes, E, capacity)
    slot_gate = jnp.zeros((E * capacity,), jnp.float32).at[pair_slot].set(route_gates.reshape(-1))
    group_rows = group_width * capacity

    def expert_step(accumulated, group_index):
        mixture_sum, input_sum = accumulated
        offset = group_index * group_rows
        row_ids = lax.dynamic_slice_in_dim(token_of, offset, group_rows)
        occupied = lax.dynamic_slice_in_dim(filled, offset, group_rows) > 0
        slot_weight = lax.dynamic_slice_in_dim(slot_gate, offset, group_rows)
        first_expert = group_index * group_width
        gate_block = lax.dynamic_slice_in_dim(gate_full, first_expert, group_width, 0)
        up_block = lax.dynamic_slice_in_dim(up_full, first_expert, group_width, 0)
        down_block = lax.dynamic_slice_in_dim(down_full, first_expert, group_width, 0)
        inputs = jnp.where(
            occupied[:, None], normed_all[row_ids], jnp.zeros((), jnp.bfloat16)
        ).reshape(group_width, capacity, MODEL_WIDTH)
        upstream = upstream_all[row_ids].astype(jnp.float32)
        gate_value = jnp.einsum(
            "ecd,edf->ecf", inputs, gate_block, preferred_element_type=jnp.float32
        )
        up_value = jnp.einsum("ecd,edf->ecf", inputs, up_block, preferred_element_type=jnp.float32)
        sigmoid_gate = jax.nn.sigmoid(gate_value)
        silu_gate = gate_value * sigmoid_gate
        activation = (silu_gate * up_value).astype(jnp.bfloat16)
        partial_out = jnp.einsum(
            "ecf,efd->ecd", activation, down_block, preferred_element_type=jnp.float32
        ).reshape(group_rows, MODEL_WIDTH)
        mixture_sum = mixture_sum.at[row_ids].add(partial_out * slot_weight[:, None])
        slot_grad = jnp.sum(partial_out * upstream, axis=-1)
        grad_expert = (
            (upstream * slot_weight[:, None])
            .astype(jnp.bfloat16)
            .reshape(group_width, capacity, MODEL_WIDTH)
        )
        grad_act = jnp.einsum(
            "ecd,efd->ecf", grad_expert, down_block, preferred_element_type=jnp.float32
        )
        slope = sigmoid_gate * (1.0 + gate_value * (1.0 - sigmoid_gate))
        grad_gate = (grad_act * up_value * slope).astype(jnp.bfloat16)
        grad_up = (grad_act * silu_gate).astype(jnp.bfloat16)
        grad_inputs = jnp.einsum(
            "ecf,edf->ecd", grad_gate, gate_block, preferred_element_type=jnp.float32
        )
        grad_inputs = grad_inputs + jnp.einsum(
            "ecf,edf->ecd", grad_up, up_block, preferred_element_type=jnp.float32
        )
        input_sum = input_sum.at[row_ids].add(grad_inputs.reshape(group_rows, MODEL_WIDTH))
        gate_piece = jnp.einsum(
            "ecd,ecf->edf", inputs, grad_gate, preferred_element_type=jnp.float32
        )
        up_piece = jnp.einsum("ecd,ecf->edf", inputs, grad_up, preferred_element_type=jnp.float32)
        down_piece = jnp.einsum(
            "ecf,ecd->efd", activation, grad_expert, preferred_element_type=jnp.float32
        )
        return ((mixture_sum, input_sum), (slot_grad, gate_piece, up_piece, down_piece))

    initial = (
        jnp.zeros((sequence_span_length, MODEL_WIDTH), jnp.float32),
        jnp.zeros((sequence_span_length, MODEL_WIDTH), jnp.float32),
    )
    sums_out, pieces = lax.scan(expert_step, initial, jnp.arange(E // group_width, dtype=jnp.int32))
    mixture_part, input_part = sums_out
    slot_grads, gate_pieces, up_pieces, down_pieces = pieces
    hidden_cols = gate_full.shape[2]
    gate_grad = gate_pieces.reshape(E, MODEL_WIDTH, hidden_cols)
    up_grad = up_pieces.reshape(E, MODEL_WIDTH, hidden_cols)
    down_grad = down_pieces.reshape(E, hidden_cols, MODEL_WIDTH)
    pick_grads = slot_grads.reshape(-1)[pair_slot].reshape(sequence_span_length, TOPK)
    mixture_own, input_own, pick_own = (
        lax.psum_scatter(mixture_part, "col", scatter_dimension=0, tiled=True),
        lax.psum_scatter(input_part, "col", scatter_dimension=0, tiled=True),
        lax.psum_scatter(pick_grads, "col", scatter_dimension=0, tiled=True),
    )
    block_out = (hidden_mid + mixture_own).astype(jnp.bfloat16)
    own_gates = lax.dynamic_slice_in_dim(route_gates, first_row, local_row_block)
    own_mask = lax.dynamic_slice_in_dim(chosen_mask, first_row, local_row_block)
    centred = own_gates * (pick_own - jnp.sum(own_gates * pick_own, axis=-1, keepdims=True))
    grad_logits = jnp.sum(jnp.where(own_mask, centred[:, :, None], 0.0), axis=1).astype(
        jnp.bfloat16
    )
    grad_normed = input_own + jnp.dot(
        grad_logits, router_full.T, preferred_element_type=jnp.float32
    )
    router_grad = jnp.dot(normed_second.T, grad_logits, preferred_element_type=jnp.float32)
    tilted_second = grad_normed * gain_second.astype(jnp.float32)
    gain_second_grad = jnp.sum(grad_normed * unit_second, axis=0)
    grad_hidden = cotangent.astype(jnp.float32) + scale_second * (
        tilted_second - unit_second * jnp.mean(tilted_second * unit_second, axis=-1, keepdims=True)
    )
    grad_branch = grad_hidden.astype(jnp.bfloat16)
    output_grad = jnp.dot(attended_low.T, grad_branch, preferred_element_type=jnp.float32)
    attended_gradient = jnp.dot(
        grad_branch, output_full.T, preferred_element_type=jnp.float32
    ).astype(jnp.bfloat16)
    grouped_gradient = attended_gradient.reshape(
        local_row_block, KEY_VALUE_HEADS, heads_per_group, HEAD_SIZE
    ).transpose(1, 2, 0, 3)
    grad_query_groups, key_gradient_grouped, value_gradient_grouped = lax.map(
        lambda operands: attend_back(operands, allowed, scaling),
        (grouped_queries, grouped_keys, grouped_values, log_total, grouped_gradient),
    )
    grad_query_rot = grad_query_groups.transpose(2, 0, 1, 3).reshape(
        local_row_block, QUERY_HEADS, HEAD_SIZE
    )
    key_gradient_total = key_gradient_grouped.transpose(1, 0, 2).reshape(
        sequence_span_length, KEY_VALUE_HEADS * HEAD_SIZE
    )
    value_gradient_total = value_gradient_grouped.transpose(1, 0, 2).reshape(
        sequence_span_length, KEY_VALUE_HEADS * HEAD_SIZE
    )
    local_keys, value_own = (
        lax.psum_scatter(
            key_gradient_total.astype(jnp.bfloat16), "col", scatter_dimension=0, tiled=True
        ).astype(jnp.float32),
        lax.psum_scatter(
            value_gradient_total.astype(jnp.bfloat16), "col", scatter_dimension=0, tiled=True
        ).astype(jnp.float32),
    )
    grad_query_low = (
        apply_rotary(grad_query_rot, local_positions, -1.0)
        .reshape(local_row_block, QUERY_HEADS * HEAD_SIZE)
        .astype(jnp.bfloat16)
    )
    grad_key_low = (
        apply_rotary(
            local_keys.reshape(local_row_block, KEY_VALUE_HEADS, HEAD_SIZE), local_positions, -1.0
        )
        .reshape(local_row_block, KEY_VALUE_HEADS * HEAD_SIZE)
        .astype(jnp.bfloat16)
    )
    grad_value_low = value_own.astype(jnp.bfloat16)
    grad_normed_first = jnp.dot(grad_query_low, query_full.T, preferred_element_type=jnp.float32)
    grad_normed_first = grad_normed_first + jnp.dot(
        grad_key_low, gathered_keys.T, preferred_element_type=jnp.float32
    )
    grad_normed_first = grad_normed_first + jnp.dot(
        grad_value_low, gathered_values.T, preferred_element_type=jnp.float32
    )
    query_grad = jnp.dot(normed_first.T, grad_query_low, preferred_element_type=jnp.float32)
    key_grad = jnp.dot(normed_first.T, grad_key_low, preferred_element_type=jnp.float32)
    value_grad = jnp.dot(normed_first.T, grad_value_low, preferred_element_type=jnp.float32)
    tilted_first = grad_normed_first * gain_first.astype(jnp.float32)
    gain_first_grad = jnp.sum(grad_normed_first * unit_first, axis=0)
    input_grad = grad_hidden + scale_first * (
        tilted_first - unit_first * jnp.mean(tilted_first * unit_first, axis=-1, keepdims=True)
    )
    query_part, key_part, value_part, output_part = (
        lax.psum_scatter(
            query_grad.astype(jnp.bfloat16), "col", scatter_dimension=1, tiled=True
        ).astype(jnp.float32),
        lax.psum_scatter(
            key_grad.astype(jnp.bfloat16), "col", scatter_dimension=1, tiled=True
        ).astype(jnp.float32),
        lax.psum_scatter(
            value_grad.astype(jnp.bfloat16), "col", scatter_dimension=1, tiled=True
        ).astype(jnp.float32),
        lax.psum_scatter(
            output_grad.astype(jnp.bfloat16), "col", scatter_dimension=0, tiled=True
        ).astype(jnp.float32),
    )
    small_total = lax.psum((gain_first_grad, gain_second_grad, router_grad), ("row", "col"))
    query_out, key_out, value_out, output_out, gate_out, up_out, down_out = (
        lax.psum_scatter(
            query_part.astype(jnp.bfloat16), "row", scatter_dimension=0, tiled=True
        ).astype(jnp.float32),
        lax.psum_scatter(
            key_part.astype(jnp.bfloat16), "row", scatter_dimension=0, tiled=True
        ).astype(jnp.float32),
        lax.psum_scatter(
            value_part.astype(jnp.bfloat16), "row", scatter_dimension=0, tiled=True
        ).astype(jnp.float32),
        lax.psum_scatter(
            output_part.astype(jnp.bfloat16), "row", scatter_dimension=1, tiled=True
        ).astype(jnp.float32),
        lax.psum_scatter(
            gate_grad.astype(jnp.bfloat16), "row", scatter_dimension=1, tiled=True
        ).astype(jnp.float32),
        lax.psum_scatter(
            up_grad.astype(jnp.bfloat16), "row", scatter_dimension=1, tiled=True
        ).astype(jnp.float32),
        lax.psum_scatter(
            down_grad.astype(jnp.bfloat16), "row", scatter_dimension=2, tiled=True
        ).astype(jnp.float32),
    )
    row_block = attention_gain.shape[0]
    row_start = lax.axis_index("row") * row_block
    gain_first_out = lax.dynamic_slice_in_dim(small_total[0], row_start, row_block)
    gain_second_out = lax.dynamic_slice_in_dim(small_total[1], row_start, row_block)
    router_out = lax.dynamic_slice_in_dim(small_total[2], row_start, row_block, 0)
    return (
        block_out,
        input_grad,
        gain_first_out,
        query_out,
        key_out,
        value_out,
        output_out,
        gain_second_out,
        router_out,
        gate_out,
        up_out,
        down_out,
    )


GRID = ("row", "col")
PLANE = 4
LINE = 4


def nothing(*refs):
    pass


def after(block, *others):
    anywhere = pl.BlockSpec(memory_space=pl.ANY)
    return pl.pallas_call(
        nothing,
        out_shape=jax.ShapeDtypeStruct(block.shape, block.dtype),
        in_specs=[anywhere] * (1 + len(others)),
        out_specs=anywhere,
        input_output_aliases={0: 0},
        name="after",
    )(block, *others)


def swap_cores(block):
    return lax.ppermute(block, "col", [(0, 1), (1, 0)])


def both_cores(own):
    return jnp.concatenate([own, swap_cores(own)], axis=0)


def sum_cores(partial, kind):
    half = partial.shape[0] // 2
    away = partial[half:].astype(kind)
    return partial[:half] + swap_cores(away).astype(partial.dtype)


def own_first(table, core, axis):
    half = table.shape[axis] // 2
    mine = lax.dynamic_slice_in_dim(table, core * half, half, axis)
    theirs = lax.dynamic_slice_in_dim(table, (1 - core) * half, half, axis)
    return jnp.concatenate([mine, theirs], axis=axis)


def exchange(block):
    return lax.all_to_all(block, GRID, split_axis=0, concat_axis=0, tiled=True)


LINES = [[z * PLANE + p for z in range(LINE)] for p in range(PLANE)]


def line_shift(block, step):
    pairs = [
        (s * PLANE + p, (s + step) % LINE * PLANE + p) for s in range(LINE) for p in range(PLANE)
    ]
    return lax.ppermute(block, "row", pairs)


def plane_pairs(flip):
    return [(r, r ^ flip) for r in range(PLANE * LINE)]


def reorder(block, order, axis):
    picked = [lax.dynamic_index_in_dim(block, i, axis, True) for i in order]
    return jnp.concatenate(picked, axis=axis)


def row_gather(line, level, place):
    moved = [lax.ppermute(line, "row", plane_pairs(flip)) for flip in range(1, PLANE)]
    whole = jnp.concatenate([line, *moved], axis=0)
    order = [(place ^ p) * LINE + (level - z) % LINE for z in range(LINE) for p in range(PLANE)]
    return reorder(whole, order, 0).reshape(LINE * PLANE * line.shape[1], line.shape[2])


def row_reduce(total, flips, level, place, kind=jnp.bfloat16):
    block = total.shape[0] // (LINE * PLANE)
    parts = total.reshape(LINE, 2, 2, block, total.shape[1])
    for flip in flips:
        axis = min(3 - flip, parts.ndim - 3)
        bit = (place // flip) % 2
        kept = lax.dynamic_index_in_dim(parts, bit, axis, False)
        away = lax.dynamic_index_in_dim(parts, 1 - bit, axis, False).astype(kind)
        parts = kept + lax.ppermute(away, "row", plane_pairs(flip)).astype(jnp.float32)
    order = [(level + step) % LINE for step in range(LINE)]
    parts = [lax.dynamic_index_in_dim(parts, i, 0, False) for i in order]
    moved = [line_shift(parts[step].astype(kind), step) for step in range(1, LINE)]
    total = parts[0]
    for part in moved:
        total = total + part.astype(jnp.float32)
    return total


def line_gather(block):
    whole = lax.all_gather(block, "row", axis=0, tiled=False, axis_index_groups=LINES)
    return whole


def line_reduce(parts):
    return lax.psum_scatter(
        parts, "row", scatter_dimension=0, tiled=False, axis_index_groups=LINES
    )


def plane_exchange(block, mate):
    block = reorder(block, [mate ^ m for m in range(2 * PLANE)], 0)
    out = [block[0]]
    for move in range(1, 2 * PLANE):
        pairs = [(d, d ^ move) for d in range(2 * PLANE * LINE)]
        out.append(lax.ppermute(block[move], GRID, pairs))
    return reorder(jnp.stack(out), [mate ^ m for m in range(2 * PLANE)], 0)


def plane_all(block):
    groups = [[z * 2 * PLANE + d for d in range(2 * PLANE)] for z in range(LINE)]
    return lax.all_to_all(
        block, GRID, split_axis=0, concat_axis=0, tiled=True, axis_index_groups=groups
    )


def tokens_move(
    hidden_in,
    segments,
    routes,
    attention_gain,
    query_weight,
    key_matrix,
    value_matrix,
    output_weight,
    expert_gain,
    router_weight,
    gate_weight,
    up_weight,
    down_weight,
    cotangent,
):
    bf16, f32 = jnp.bfloat16, jnp.float32
    core, row = lax.axis_index("col"), lax.axis_index("row")
    level, place = row // PLANE, row % PLANE
    local = hidden_in.shape[0]
    span = segments.shape[1]
    row_block = query_weight.shape[0]
    rows = MODEL_WIDTH // row_block
    hidden_block = gate_weight.shape[2]
    ffe = 2 * hidden_block
    capacity = max(2, 3 * span * TOPK // (2 * E))
    share = capacity // 2
    head_cols = query_weight.shape[1]
    kv_cols = key_matrix.shape[1]
    heads = head_cols // HEAD_SIZE
    mates = 2 * PLANE
    my_expert = row * 2 + core
    nt = (((1,), (1,)), ((), ()))
    tn = (((0,), (0,)), ((), ()))

    packed = jnp.concatenate(
        [
            query_weight,
            key_matrix,
            value_matrix,
            output_weight.T,
            router_weight,
            attention_gain[:, None],
            expert_gain[:, None],
            jnp.zeros((row_block, 128 - E - 2), bf16),
        ],
        axis=1,
    )
    packed_line = jnp.stack([packed] + [line_shift(packed, step) for step in range(1, LINE)])
    routes_line = [routes.T] + [line_shift(routes.T, step) for step in range(1, LINE)]
    routes_line = reorder(jnp.stack(routes_line), [(level - z) % LINE for z in range(LINE)], 0)
    packed_line = after(packed_line, routes_line)
    packed_full = row_gather(packed_line, level, place)
    o0 = head_cols + 2 * kv_cols
    qkv_cols, out_full = packed_full[:, :o0], packed_full[:, o0:]
    output_t = out_full[:, :head_cols]
    router_full = out_full[:, head_cols : head_cols + E]
    gain_first = out_full[:, head_cols + E].astype(f32)
    gain_second = out_full[:, head_cols + E + 1].astype(f32)

    expert_ids = jnp.arange(E, dtype=jnp.int32)
    share_slots = core * share + jnp.arange(share, dtype=jnp.int32)
    picks, masks = [], []
    for i in range(LINE):
        named, counts = slot_ranks(routes_line[i].T)
        slot_of = jnp.where(named, counts, -1).T
        slot_of = lax.dynamic_slice_in_dim(own_first(slot_of, core, 1), level * mates, mates)
        pick = (slot_of[:, None, :] == share_slots[None, :, None]).astype(bf16)
        picks.append(pick.reshape(mates * share, span))
        masks.append(own_first(jnp.pad(named.astype(bf16), ((0, 0), (0, 128 - E))), core, 0))

    def send_rows(tables, chunks):
        sent = []
        for pick, chunk in zip(tables, chunks):
            part = jnp.dot(pick, chunk, preferred_element_type=f32).astype(bf16)
            sent.append(part.reshape(mates, 1, share, chunk.shape[1]))
        return jnp.concatenate(sent, axis=1)

    slots = LINE * share * mates

    gate_up = exchange(after(jnp.concatenate([gate_weight, up_weight], axis=2), packed_line))
    cot_line = line_gather(after(cotangent, packed_line))

    def whole_weight(blocks):
        return (
            blocks.reshape(rows, 2, row_block, hidden_block)
            .transpose(0, 2, 1, 3)
            .reshape(MODEL_WIDTH, ffe)
        )

    hidden_all = both_cores(hidden_in)
    tokens_all = hidden_all.astype(f32)
    scale_all = lax.rsqrt(jnp.mean(tokens_all * tokens_all, axis=-1, keepdims=True) + EPSILON)
    normed_all = (tokens_all * scale_all * gain_first).astype(bf16)
    places = own_first(positions(segments[0]), core, 0)
    segment_ids = own_first(segments[0], core, 0)
    token_index = own_first(jnp.arange(span, dtype=jnp.int32), core, 0)
    allowed = (segment_ids[:, None] == segment_ids[None, :]) & (
        token_index[None, :] <= token_index[:, None]
    )
    raw = jnp.dot(normed_all, qkv_cols, preferred_element_type=f32)
    queries = apply_rotary(raw[:, :head_cols].reshape(span, heads, HEAD_SIZE), places, 1.0)
    queries = queries.astype(bf16).transpose(1, 0, 2)
    keys = apply_rotary(
        raw[:, head_cols : head_cols + kv_cols].reshape(span, 1, HEAD_SIZE), places, 1.0
    ).astype(bf16)[:, 0]
    values = raw[:, head_cols + kv_cols :].astype(bf16)
    scaling = HEAD_SIZE ** (-0.5)
    attended, log_total = attend_group((queries, keys, values), allowed, scaling)
    attended_low = attended.transpose(1, 0, 2).reshape(span, head_cols).astype(bf16)
    branch_part = lax.dot_general(attended_low, output_t, nt, preferred_element_type=f32)
    tokens_in = hidden_in.astype(f32)
    hidden_mid = tokens_in + sum_cores(branch_part, f32)
    scale_second = lax.rsqrt(jnp.mean(hidden_mid * hidden_mid, axis=-1, keepdims=True) + EPSILON)
    unit_second = hidden_mid * scale_second
    normed_second = (unit_second * gain_second).astype(bf16)

    normed_line = line_gather(after(normed_second, gate_up))
    cot_line = after(cot_line, normed_second)
    cot_swap = swap_cores(cot_line)
    cot_rows = [
        jnp.concatenate([jnp.concatenate([cot_line[i], cot_swap[i]], axis=0), masks[i]], axis=1)
        for i in range(LINE)
    ]
    upstream_rows = plane_all(send_rows(picks, cot_rows))
    upstream = upstream_rows.reshape(slots, MODEL_WIDTH + 128)
    mask_rows = upstream[:, MODEL_WIDTH : MODEL_WIDTH + E] > 0
    upstream = upstream[:, :MODEL_WIDTH].astype(f32)

    normed_swap = swap_cores(normed_line)
    expert_in = plane_exchange(
        send_rows(
            picks,
            [jnp.concatenate([normed_line[i], normed_swap[i]], axis=0) for i in range(LINE)],
        ),
        place * 2 + core,
    ).reshape(slots, MODEL_WIDTH)
    down_e = exchange(after(down_weight.transpose(0, 2, 1), upstream_rows))

    logits = jnp.dot(expert_in, router_full, preferred_element_type=f32)
    top = jnp.max(jnp.where(mask_rows, logits, MASKED), axis=-1, keepdims=True)
    exponent = jnp.where(mask_rows, jnp.exp(logits - top), 0.0)
    gates = exponent / jnp.maximum(jnp.sum(exponent, axis=-1, keepdims=True), 1e-30)
    mine = (expert_ids == my_expert)[None, :]
    slot_gate = jnp.sum(jnp.where(mine, gates, 0.0), axis=-1, keepdims=True)
    gate_w = whole_weight(gate_up[:, :, :hidden_block])
    up_w = whole_weight(gate_up[:, :, hidden_block:])
    down_t = whole_weight(down_e)
    gate_value = jnp.dot(expert_in, gate_w, preferred_element_type=f32)
    up_value = jnp.dot(expert_in, up_w, preferred_element_type=f32)
    sigmoid_gate = jax.nn.sigmoid(gate_value)
    silu_gate = gate_value * sigmoid_gate
    activation = (silu_gate * up_value).astype(bf16)
    expert_out = lax.dot_general(activation, down_t, nt, preferred_element_type=f32)
    slot_grad = jnp.sum(expert_out * upstream, axis=-1, keepdims=True)
    pick_grad = slot_gate * slot_grad
    grad_logits = (pick_grad * (jnp.where(mine, 1.0, 0.0) - gates)).astype(bf16)
    grad_expert = (upstream * slot_gate).astype(bf16)
    grad_act = jnp.dot(grad_expert, down_t, preferred_element_type=f32)
    slope = sigmoid_gate * (1.0 + gate_value * (1.0 - sigmoid_gate))
    grad_gate = (grad_act * up_value * slope).astype(bf16)
    grad_up = (grad_act * silu_gate).astype(bf16)
    grad_in = lax.dot_general(grad_gate, gate_w, nt, preferred_element_type=f32)
    grad_in = grad_in + lax.dot_general(grad_up, up_w, nt, preferred_element_type=f32)
    grad_in = grad_in + lax.dot_general(grad_logits, router_full, nt, preferred_element_type=f32)

    def combine(got):
        parts = []
        for i, pick in enumerate(picks):
            part = got[:, i].reshape(mates * share, MODEL_WIDTH)
            parts.append(lax.dot_general(pick, part, tn, preferred_element_type=f32))
        parts = jnp.stack(parts)
        away = swap_cores(parts[:, local:].astype(bf16))
        parts = parts[:, :local] + away.astype(f32)
        return line_reduce(parts.astype(bf16)).astype(f32)

    shape = (mates, LINE, share, MODEL_WIDTH)
    grad_back = plane_all(grad_in.astype(bf16).reshape(shape))
    grad_normed = combine(grad_back)
    router_grad = lax.dot_general(expert_in, grad_logits, tn, preferred_element_type=f32)

    def shard_grad(left, right):
        full = lax.dot_general(left, right, tn, preferred_element_type=f32).astype(bf16)
        blocks = full.reshape(rows, row_block, 2, hidden_block).transpose(0, 2, 1, 3)
        return blocks.reshape(E, row_block, hidden_block)

    mixture = (expert_out * slot_gate).astype(bf16).reshape(shape)
    mixture = plane_all(after(mixture, grad_back))
    down_home = exchange(after(shard_grad(grad_expert, activation), mixture))
    gate_home = exchange(after(shard_grad(expert_in, grad_gate), down_home))
    up_home = exchange(after(shard_grad(expert_in, grad_up), gate_home))

    tilted = grad_normed * gain_second
    gain_second_grad = jnp.sum(grad_normed * unit_second, axis=0)
    grad_hidden = cotangent.astype(f32) + scale_second * (
        tilted - unit_second * jnp.mean(tilted * unit_second, axis=-1, keepdims=True)
    )
    branch_all = both_cores(grad_hidden.astype(bf16))

    output_t_grad = lax.dot_general(branch_all, attended_low, tn, preferred_element_type=f32)
    grad_attended = jnp.dot(branch_all, output_t, preferred_element_type=f32).astype(bf16)
    grad_attended = grad_attended.reshape(span, heads, HEAD_SIZE).transpose(1, 0, 2)
    grad_queries, grad_keys, grad_values = attend_back(
        (queries, keys, values, log_total, grad_attended), allowed, scaling
    )
    grad_query_low = (
        apply_rotary(grad_queries.transpose(1, 0, 2), places, -1.0)
        .reshape(span, head_cols)
        .astype(bf16)
    )
    grad_key_low = apply_rotary(grad_keys[:, None], places, -1.0)[:, 0].astype(bf16)
    grad_qkv = jnp.concatenate([grad_query_low, grad_key_low, grad_values.astype(bf16)], axis=1)
    qkv_grad = lax.dot_general(normed_all, grad_qkv, tn, preferred_element_type=f32)
    first_part = lax.dot_general(grad_qkv, qkv_cols, nt, preferred_element_type=f32)
    grad_first = sum_cores(first_part, f32)
    unit_first = tokens_in * scale_all[:local]
    tilted_first = grad_first * gain_first
    gain_first_grad = jnp.sum(grad_first * unit_first, axis=0)
    input_grad = grad_hidden + scale_all[:local] * (
        tilted_first - unit_first * jnp.mean(tilted_first * unit_first, axis=-1, keepdims=True)
    )
    mixture = combine(after(mixture, grad_qkv))
    block_out = (hidden_mid + mixture).astype(bf16)

    extra = jnp.concatenate(
        [
            router_grad,
            gain_second_grad[:, None],
            jnp.zeros((MODEL_WIDTH, 128 - E - 1), f32),
        ],
        axis=1,
    )
    half = head_cols // 2
    output_own = [
        row_reduce(output_t_grad[:, :half], (1, 2), level, place),
        row_reduce(
            jnp.concatenate([output_t_grad[:, half:], extra], axis=1), (2, 1), level, place
        ),
    ]
    output_own = jnp.concatenate(output_own, axis=1)
    small_own = output_own[:, head_cols:]
    small_own = small_own + swap_cores(small_own)
    qkv_grad = after(qkv_grad, gate_home)
    half = qkv_grad.shape[1] // 2
    qkv_own = jnp.concatenate(
        [
            row_reduce(qkv_grad[:, :half], (1, 2), level, place),
            row_reduce(qkv_grad[:, half:], (2, 1), level, place),
        ],
        axis=1,
    )
    gain_parts = gain_first_grad.reshape(rows, row_block)
    gain_first_own = row_reduce(gain_parts, (1, 2), level, place, f32)[0]
    gain_first_own = gain_first_own + swap_cores(gain_first_own)
    return (
        block_out,
        input_grad,
        gain_first_own,
        qkv_own[:, :head_cols],
        qkv_own[:, head_cols : head_cols + kv_cols],
        qkv_own[:, head_cols + kv_cols :],
        output_own[:, :head_cols].T,
        small_own[:, E],
        small_own[:, :E],
        gate_home.astype(f32),
        up_home.astype(f32),
        down_home.astype(f32).transpose(0, 2, 1),
    )


def solution(mesh):
    in_specs = (
        P(("row", "col"), None),
        P("row", None),
        P("row", None),
        P("row"),
        P("row", "col"),
        P("row", "col"),
        P("row", "col"),
        P("col", "row"),
        P("row"),
        P("row", None),
        P(None, "row", "col"),
        P(None, "row", "col"),
        P(None, "col", "row"),
        P(("row", "col"), None),
    )
    out_specs = (
        P(("row", "col"), None),
        P(("row", "col"), None),
        P("row"),
        P("row", "col"),
        P("row", "col"),
        P("row", "col"),
        P("col", "row"),
        P("row"),
        P("row", None),
        P(None, "row", "col"),
        P(None, "row", "col"),
        P(None, "col", "row"),
    )
    rows, cols = mesh.shape["row"], mesh.shape["col"]
    one_each = rows == 4 * PLANE and cols == KEY_VALUE_HEADS and rows * cols == E
    return jax.shard_map(
        tokens_move if one_each else weights_move, mesh=mesh,
        in_specs=in_specs,
        out_specs=out_specs,
        check_vma=False,
    )
```

```python
import jax
import jax.numpy as jnp
from jax import lax
from jax.experimental import pallas as pl
from jax.experimental.pallas import tpu as pltpu
from jax.sharding import PartitionSpec as P

MODEL_WIDTH = 1536
QUERY_HEADS = 12
KEY_VALUE_HEADS = 2
HEAD_SIZE = 128
E = 32
TOPK = 4


EPSILON = 1e-06
ROPE_BASE = 1000000.0
MASKED = -1e30


def positions(segment_ids):
    total_length = segment_ids.shape[0]
    token_index = jnp.arange(total_length, dtype=jnp.int32)
    earlier = (segment_ids[:, None] == segment_ids[None, :]) & (
        token_index[None, :] < token_index[:, None]
    )
    return jnp.sum(earlier.astype(jnp.int32), axis=1)


def apply_rotary(values, places, direction):
    half_size = values.shape[-1] // 2
    frequency = ROPE_BASE ** (-2.0 * jnp.arange(half_size, dtype=jnp.float32) / values.shape[-1])
    angles = places.astype(jnp.float32)[:, None] * frequency[None, :]
    cosine_part = jnp.cos(angles)[:, None, :]
    sine_part = direction * jnp.sin(angles)[:, None, :]
    first_half = values[..., :half_size]
    second_half = values[..., half_size:]
    return jnp.concatenate(
        [
            first_half * cosine_part - second_half * sine_part,
            second_half * cosine_part + first_half * sine_part,
        ],
        axis=-1,
    )


def slot_ranks(route_ids):
    total_length = route_ids.shape[0]
    token_index = jnp.arange(total_length, dtype=jnp.int32)
    expert_ids = jnp.arange(E, dtype=jnp.int32)
    named = jnp.any(route_ids[:, :, None] == expert_ids[None, None, :], axis=1)
    before = (token_index[None, :] < token_index[:, None]).astype(jnp.bfloat16)
    counts = jnp.dot(before, named.astype(jnp.bfloat16), preferred_element_type=jnp.float32)
    return (named, counts.astype(jnp.int32))


def slot_tables(route_ids, experts, capacity):
    flat_ids = route_ids.reshape(-1)
    named, counts = slot_ranks(route_ids)
    rank_ids = jnp.sum(
        jnp.where(
            route_ids[:, :, None] == jnp.arange(experts, dtype=jnp.int32)[None, None, :],
            counts[:, None, :],
            0,
        ),
        axis=-1,
    ).reshape(-1)
    pair_slot = flat_ids * capacity + rank_ids
    owners = jnp.arange(flat_ids.shape[0], dtype=jnp.int32) // route_ids.shape[1]
    token_of = jnp.zeros((experts * capacity,), jnp.int32).at[pair_slot].set(owners)
    filled = jnp.zeros((experts * capacity,), jnp.int32).at[pair_slot].set(1)
    return (pair_slot, token_of, filled)


def masked_scores(queries, key_row_block, allowed, scaling):
    scores = (
        jnp.einsum("gqd,kd->gqk", queries, key_row_block, preferred_element_type=jnp.float32)
        * scaling
    )
    return jnp.where(allowed[None], scores, MASKED)


def attend_group(operands, allowed, scaling):
    queries, key_row_block, value_row_block = operands
    scores = masked_scores(queries, key_row_block, allowed, scaling)
    highest = jnp.max(scores, axis=-1, keepdims=True)
    exponent = jnp.exp(scores - highest)
    summed = jnp.sum(exponent, axis=-1, keepdims=True)
    weights_low = (exponent / summed).astype(jnp.bfloat16)
    result = jnp.einsum(
        "gqk,kd->gqd", weights_low, value_row_block, preferred_element_type=jnp.float32
    )
    return (result, highest + jnp.log(summed))


def attend_back(operands, allowed, scaling):
    queries, key_row_block, value_row_block, log_total, grad_result = operands
    scores = masked_scores(queries, key_row_block, allowed, scaling)
    weights_full = jnp.where(allowed[None], jnp.exp(scores - log_total), 0.0)
    weights_low = weights_full.astype(jnp.bfloat16)
    grad_values = jnp.einsum(
        "gqk,gqd->kd", weights_low, grad_result, preferred_element_type=jnp.float32
    )
    grad_weights = jnp.einsum(
        "gqd,kd->gqk", grad_result, value_row_block, preferred_element_type=jnp.float32
    )
    centre = jnp.sum(weights_full * grad_weights, axis=-1, keepdims=True)
    grad_scores = (weights_full * (grad_weights - centre)).astype(jnp.bfloat16)
    grad_queries = (
        jnp.einsum("gqk,kd->gqd", grad_scores, key_row_block, preferred_element_type=jnp.float32)
        * scaling
    )
    grad_keys = (
        jnp.einsum("gqk,gqd->kd", grad_scores, queries, preferred_element_type=jnp.float32)
        * scaling
    )
    return (grad_queries, grad_keys, grad_values)


def weights_move(
    hidden_in,
    segments,
    routes,
    attention_gain,
    query_weight,
    key_matrix,
    value_matrix,
    output_weight,
    expert_gain,
    router_weight,
    gate_weight,
    up_weight,
    down_weight,
    cotangent,
):
    gain_first, query_cols, key_cols, value_cols, output_rows = (
        lax.all_gather(attention_gain, "row", axis=0, tiled=True),
        lax.all_gather(query_weight, "row", axis=0, tiled=True),
        lax.all_gather(key_matrix, "row", axis=0, tiled=True),
        lax.all_gather(value_matrix, "row", axis=0, tiled=True),
        lax.all_gather(output_weight, "row", axis=1, tiled=True),
    )
    query_full, gathered_keys, gathered_values, output_full = (
        lax.all_gather(query_cols, "col", axis=1, tiled=True),
        lax.all_gather(key_cols, "col", axis=1, tiled=True),
        lax.all_gather(value_cols, "col", axis=1, tiled=True),
        lax.all_gather(output_rows, "col", axis=0, tiled=True),
    )
    gain_second, router_full, gate_full, up_full, down_full = (
        lax.all_gather(expert_gain, "row", axis=0, tiled=True),
        lax.all_gather(router_weight, "row", axis=0, tiled=True),
        lax.all_gather(gate_weight, "row", axis=1, tiled=True),
        lax.all_gather(up_weight, "row", axis=1, tiled=True),
        lax.all_gather(down_weight, "row", axis=2, tiled=True),
    )
    local_row_block = hidden_in.shape[0]
    sequence_span_length = segments.shape[1]
    first_row = lax.axis_index("col") * local_row_block
    segment_ids = segments[0]
    places_all = positions(segment_ids)
    local_positions = lax.dynamic_slice_in_dim(places_all, first_row, local_row_block)
    own_segments = lax.dynamic_slice_in_dim(segment_ids, first_row, local_row_block)
    query_index = first_row + jnp.arange(local_row_block, dtype=jnp.int32)
    key_index = jnp.arange(sequence_span_length, dtype=jnp.int32)
    allowed = (own_segments[:, None] == segment_ids[None, :]) & (
        key_index[None, :] <= query_index[:, None]
    )
    tokens_in = hidden_in.astype(jnp.float32)
    scale_first = lax.rsqrt(jnp.mean(tokens_in * tokens_in, axis=-1, keepdims=True) + EPSILON)
    unit_first = tokens_in * scale_first
    normed_first = (unit_first * gain_first.astype(jnp.float32)).astype(jnp.bfloat16)
    query_raw = jnp.dot(normed_first, query_full, preferred_element_type=jnp.float32).reshape(
        local_row_block, QUERY_HEADS, HEAD_SIZE
    )
    unrotated_keys = jnp.dot(
        normed_first, gathered_keys, preferred_element_type=jnp.float32
    ).reshape(local_row_block, KEY_VALUE_HEADS, HEAD_SIZE)
    values_reduced = jnp.dot(
        normed_first, gathered_values, preferred_element_type=jnp.float32
    ).astype(jnp.bfloat16)
    rotated_queries = apply_rotary(query_raw, local_positions, 1.0).astype(jnp.bfloat16)
    rotated_keys = (
        apply_rotary(unrotated_keys, local_positions, 1.0)
        .astype(jnp.bfloat16)
        .reshape(local_row_block, KEY_VALUE_HEADS * HEAD_SIZE)
    )
    key_row_block, value_row_block = (
        lax.all_gather(rotated_keys, "col", axis=0, tiled=True),
        lax.all_gather(values_reduced, "col", axis=0, tiled=True),
    )
    heads_per_group = QUERY_HEADS // KEY_VALUE_HEADS
    scaling = HEAD_SIZE ** (-0.5)
    grouped_queries = rotated_queries.reshape(
        local_row_block, KEY_VALUE_HEADS, heads_per_group, HEAD_SIZE
    ).transpose(1, 2, 0, 3)
    grouped_keys = key_row_block.reshape(
        sequence_span_length, KEY_VALUE_HEADS, HEAD_SIZE
    ).transpose(1, 0, 2)
    grouped_values = value_row_block.reshape(
        sequence_span_length, KEY_VALUE_HEADS, HEAD_SIZE
    ).transpose(1, 0, 2)
    attended, log_total = lax.map(
        lambda operands: attend_group(operands, allowed, scaling),
        (grouped_queries, grouped_keys, grouped_values),
    )
    attended_low = (
        attended.transpose(2, 0, 1, 3)
        .reshape(local_row_block, QUERY_HEADS * HEAD_SIZE)
        .astype(jnp.bfloat16)
    )
    branch = jnp.dot(attended_low, output_full, preferred_element_type=jnp.float32)
    hidden_mid = tokens_in + branch
    scale_second = lax.rsqrt(jnp.mean(hidden_mid * hidden_mid, axis=-1, keepdims=True) + EPSILON)
    unit_second = hidden_mid * scale_second
    normed_second = (unit_second * gain_second.astype(jnp.float32)).astype(jnp.bfloat16)
    normed_all, upstream_all = (
        lax.all_gather(normed_second, "col", axis=0, tiled=True),
        lax.all_gather(cotangent, "col", axis=0, tiled=True),
    )
    logits = jnp.dot(normed_all, router_full, preferred_element_type=jnp.float32)
    expert_ids = jnp.arange(E, dtype=jnp.int32)
    chosen_mask = routes[:, :, None] == expert_ids[None, None, :]
    chosen = jnp.sum(jnp.where(chosen_mask, logits[:, None, :], 0.0), axis=-1)
    exponent = jnp.exp(chosen - jnp.max(chosen, axis=-1, keepdims=True))
    route_gates = exponent / jnp.sum(exponent, axis=-1, keepdims=True)
    group_width = 4
    capacity = max(2, 3 * sequence_span_length * TOPK // (2 * E))
    pair_slot, token_of, filled = slot_tables(routes, E, capacity)
    slot_gate = jnp.zeros((E * capacity,), jnp.float32).at[pair_slot].set(route_gates.reshape(-1))
    group_rows = group_width * capacity

    def expert_step(accumulated, group_index):
        mixture_sum, input_sum = accumulated
        offset = group_index * group_rows
        row_ids = lax.dynamic_slice_in_dim(token_of, offset, group_rows)
        occupied = lax.dynamic_slice_in_dim(filled, offset, group_rows) > 0
        slot_weight = lax.dynamic_slice_in_dim(slot_gate, offset, group_rows)
        first_expert = group_index * group_width
        gate_block = lax.dynamic_slice_in_dim(gate_full, first_expert, group_width, 0)
        up_block = lax.dynamic_slice_in_dim(up_full, first_expert, group_width, 0)
        down_block = lax.dynamic_slice_in_dim(down_full, first_expert, group_width, 0)
        inputs = jnp.where(
            occupied[:, None], normed_all[row_ids], jnp.zeros((), jnp.bfloat16)
        ).reshape(group_width, capacity, MODEL_WIDTH)
        upstream = upstream_all[row_ids].astype(jnp.float32)
        gate_value = jnp.einsum(
            "ecd,edf->ecf", inputs, gate_block, preferred_element_type=jnp.float32
        )
        up_value = jnp.einsum("ecd,edf->ecf", inputs, up_block, preferred_element_type=jnp.float32)
        sigmoid_gate = jax.nn.sigmoid(gate_value)
        silu_gate = gate_value * sigmoid_gate
        activation = (silu_gate * up_value).astype(jnp.bfloat16)
        partial_out = jnp.einsum(
            "ecf,efd->ecd", activation, down_block, preferred_element_type=jnp.float32
        ).reshape(group_rows, MODEL_WIDTH)
        mixture_sum = mixture_sum.at[row_ids].add(partial_out * slot_weight[:, None])
        slot_grad = jnp.sum(partial_out * upstream, axis=-1)
        grad_expert = (
            (upstream * slot_weight[:, None])
            .astype(jnp.bfloat16)
            .reshape(group_width, capacity, MODEL_WIDTH)
        )
        grad_act = jnp.einsum(
            "ecd,efd->ecf", grad_expert, down_block, preferred_element_type=jnp.float32
        )
        slope = sigmoid_gate * (1.0 + gate_value * (1.0 - sigmoid_gate))
        grad_gate = (grad_act * up_value * slope).astype(jnp.bfloat16)
        grad_up = (grad_act * silu_gate).astype(jnp.bfloat16)
        grad_inputs = jnp.einsum(
            "ecf,edf->ecd", grad_gate, gate_block, preferred_element_type=jnp.float32
        )
        grad_inputs = grad_inputs + jnp.einsum(
            "ecf,edf->ecd", grad_up, up_block, preferred_element_type=jnp.float32
        )
        input_sum = input_sum.at[row_ids].add(grad_inputs.reshape(group_rows, MODEL_WIDTH))
        gate_piece = jnp.einsum(
            "ecd,ecf->edf", inputs, grad_gate, preferred_element_type=jnp.float32
        )
        up_piece = jnp.einsum("ecd,ecf->edf", inputs, grad_up, preferred_element_type=jnp.float32)
        down_piece = jnp.einsum(
            "ecf,ecd->efd", activation, grad_expert, preferred_element_type=jnp.float32
        )
        return ((mixture_sum, input_sum), (slot_grad, gate_piece, up_piece, down_piece))

    initial = (
        jnp.zeros((sequence_span_length, MODEL_WIDTH), jnp.float32),
        jnp.zeros((sequence_span_length, MODEL_WIDTH), jnp.float32),
    )
    sums_out, pieces = lax.scan(expert_step, initial, jnp.arange(E // group_width, dtype=jnp.int32))
    mixture_part, input_part = sums_out
    slot_grads, gate_pieces, up_pieces, down_pieces = pieces
    hidden_cols = gate_full.shape[2]
    gate_grad = gate_pieces.reshape(E, MODEL_WIDTH, hidden_cols)
    up_grad = up_pieces.reshape(E, MODEL_WIDTH, hidden_cols)
    down_grad = down_pieces.reshape(E, hidden_cols, MODEL_WIDTH)
    pick_grads = slot_grads.reshape(-1)[pair_slot].reshape(sequence_span_length, TOPK)
    mixture_own, input_own, pick_own = (
        lax.psum_scatter(mixture_part, "col", scatter_dimension=0, tiled=True),
        lax.psum_scatter(input_part, "col", scatter_dimension=0, tiled=True),
        lax.psum_scatter(pick_grads, "col", scatter_dimension=0, tiled=True),
    )
    block_out = (hidden_mid + mixture_own).astype(jnp.bfloat16)
    own_gates = lax.dynamic_slice_in_dim(route_gates, first_row, local_row_block)
    own_mask = lax.dynamic_slice_in_dim(chosen_mask, first_row, local_row_block)
    centred = own_gates * (pick_own - jnp.sum(own_gates * pick_own, axis=-1, keepdims=True))
    grad_logits = jnp.sum(jnp.where(own_mask, centred[:, :, None], 0.0), axis=1).astype(
        jnp.bfloat16
    )
    grad_normed = input_own + jnp.dot(
        grad_logits, router_full.T, preferred_element_type=jnp.float32
    )
    router_grad = jnp.dot(normed_second.T, grad_logits, preferred_element_type=jnp.float32)
    tilted_second = grad_normed * gain_second.astype(jnp.float32)
    gain_second_grad = jnp.sum(grad_normed * unit_second, axis=0)
    grad_hidden = cotangent.astype(jnp.float32) + scale_second * (
        tilted_second - unit_second * jnp.mean(tilted_second * unit_second, axis=-1, keepdims=True)
    )
    grad_branch = grad_hidden.astype(jnp.bfloat16)
    output_grad = jnp.dot(attended_low.T, grad_branch, preferred_element_type=jnp.float32)
    attended_gradient = jnp.dot(
        grad_branch, output_full.T, preferred_element_type=jnp.float32
    ).astype(jnp.bfloat16)
    grouped_gradient = attended_gradient.reshape(
        local_row_block, KEY_VALUE_HEADS, heads_per_group, HEAD_SIZE
    ).transpose(1, 2, 0, 3)
    grad_query_groups, key_gradient_grouped, value_gradient_grouped = lax.map(
        lambda operands: attend_back(operands, allowed, scaling),
        (grouped_queries, grouped_keys, grouped_values, log_total, grouped_gradient),
    )
    grad_query_rot = grad_query_groups.transpose(2, 0, 1, 3).reshape(
        local_row_block, QUERY_HEADS, HEAD_SIZE
    )
    key_gradient_total = key_gradient_grouped.transpose(1, 0, 2).reshape(
        sequence_span_length, KEY_VALUE_HEADS * HEAD_SIZE
    )
    value_gradient_total = value_gradient_grouped.transpose(1, 0, 2).reshape(
        sequence_span_length, KEY_VALUE_HEADS * HEAD_SIZE
    )
    local_keys, value_own = (
        lax.psum_scatter(
            key_gradient_total.astype(jnp.bfloat16), "col", scatter_dimension=0, tiled=True
        ).astype(jnp.float32),
        lax.psum_scatter(
            value_gradient_total.astype(jnp.bfloat16), "col", scatter_dimension=0, tiled=True
        ).astype(jnp.float32),
    )
    grad_query_low = (
        apply_rotary(grad_query_rot, local_positions, -1.0)
        .reshape(local_row_block, QUERY_HEADS * HEAD_SIZE)
        .astype(jnp.bfloat16)
    )
    grad_key_low = (
        apply_rotary(
            local_keys.reshape(local_row_block, KEY_VALUE_HEADS, HEAD_SIZE), local_positions, -1.0
        )
        .reshape(local_row_block, KEY_VALUE_HEADS * HEAD_SIZE)
        .astype(jnp.bfloat16)
    )
    grad_value_low = value_own.astype(jnp.bfloat16)
    grad_normed_first = jnp.dot(grad_query_low, query_full.T, preferred_element_type=jnp.float32)
    grad_normed_first = grad_normed_first + jnp.dot(
        grad_key_low, gathered_keys.T, preferred_element_type=jnp.float32
    )
    grad_normed_first = grad_normed_first + jnp.dot(
        grad_value_low, gathered_values.T, preferred_element_type=jnp.float32
    )
    query_grad = jnp.dot(normed_first.T, grad_query_low, preferred_element_type=jnp.float32)
    key_grad = jnp.dot(normed_first.T, grad_key_low, preferred_element_type=jnp.float32)
    value_grad = jnp.dot(normed_first.T, grad_value_low, preferred_element_type=jnp.float32)
    tilted_first = grad_normed_first * gain_first.astype(jnp.float32)
    gain_first_grad = jnp.sum(grad_normed_first * unit_first, axis=0)
    input_grad = grad_hidden + scale_first * (
        tilted_first - unit_first * jnp.mean(tilted_first * unit_first, axis=-1, keepdims=True)
    )
    query_part, key_part, value_part, output_part = (
        lax.psum_scatter(
            query_grad.astype(jnp.bfloat16), "col", scatter_dimension=1, tiled=True
        ).astype(jnp.float32),
        lax.psum_scatter(
            key_grad.astype(jnp.bfloat16), "col", scatter_dimension=1, tiled=True
        ).astype(jnp.float32),
        lax.psum_scatter(
            value_grad.astype(jnp.bfloat16), "col", scatter_dimension=1, tiled=True
        ).astype(jnp.float32),
        lax.psum_scatter(
            output_grad.astype(jnp.bfloat16), "col", scatter_dimension=0, tiled=True
        ).astype(jnp.float32),
    )
    small_total = lax.psum((gain_first_grad, gain_second_grad, router_grad), ("row", "col"))
    query_out, key_out, value_out, output_out, gate_out, up_out, down_out = (
        lax.psum_scatter(
            query_part.astype(jnp.bfloat16), "row", scatter_dimension=0, tiled=True
        ).astype(jnp.float32),
        lax.psum_scatter(
            key_part.astype(jnp.bfloat16), "row", scatter_dimension=0, tiled=True
        ).astype(jnp.float32),
        lax.psum_scatter(
            value_part.astype(jnp.bfloat16), "row", scatter_dimension=0, tiled=True
        ).astype(jnp.float32),
        lax.psum_scatter(
            output_part.astype(jnp.bfloat16), "row", scatter_dimension=1, tiled=True
        ).astype(jnp.float32),
        lax.psum_scatter(
            gate_grad.astype(jnp.bfloat16), "row", scatter_dimension=1, tiled=True
        ).astype(jnp.float32),
        lax.psum_scatter(
            up_grad.astype(jnp.bfloat16), "row", scatter_dimension=1, tiled=True
        ).astype(jnp.float32),
        lax.psum_scatter(
            down_grad.astype(jnp.bfloat16), "row", scatter_dimension=2, tiled=True
        ).astype(jnp.float32),
    )
    row_block = attention_gain.shape[0]
    row_start = lax.axis_index("row") * row_block
    gain_first_out = lax.dynamic_slice_in_dim(small_total[0], row_start, row_block)
    gain_second_out = lax.dynamic_slice_in_dim(small_total[1], row_start, row_block)
    router_out = lax.dynamic_slice_in_dim(small_total[2], row_start, row_block, 0)
    return (
        block_out,
        input_grad,
        gain_first_out,
        query_out,
        key_out,
        value_out,
        output_out,
        gain_second_out,
        router_out,
        gate_out,
        up_out,
        down_out,
    )


GRID = ("row", "col")
PLANE = 4
LINE = 4


def nothing(*refs):
    pass


def after(block, *others):
    anywhere = pl.BlockSpec(memory_space=pl.ANY)
    return pl.pallas_call(
        nothing,
        out_shape=jax.ShapeDtypeStruct(block.shape, block.dtype),
        in_specs=[anywhere] * (1 + len(others)),
        out_specs=anywhere,
        input_output_aliases={0: 0},
        name="after",
    )(block, *others)


def swap_cores(block):
    return lax.ppermute(block, "col", [(0, 1), (1, 0)])


def both_cores(own):
    return jnp.concatenate([own, swap_cores(own)], axis=0)


def sum_cores(partial, kind):
    half = partial.shape[0] // 2
    away = partial[half:].astype(kind)
    return partial[:half] + swap_cores(away).astype(partial.dtype)


def own_first(table, core, axis):
    half = table.shape[axis] // 2
    mine = lax.dynamic_slice_in_dim(table, core * half, half, axis)
    theirs = lax.dynamic_slice_in_dim(table, (1 - core) * half, half, axis)
    return jnp.concatenate([mine, theirs], axis=axis)


def exchange(block):
    return lax.all_to_all(block, GRID, split_axis=0, concat_axis=0, tiled=True)


LINES = [[z * PLANE + p for z in range(LINE)] for p in range(PLANE)]


def line_shift(block, step):
    pairs = [
        (s * PLANE + p, (s + step) % LINE * PLANE + p) for s in range(LINE) for p in range(PLANE)
    ]
    return lax.ppermute(block, "row", pairs)


def plane_pairs(flip):
    return [(r, r ^ flip) for r in range(PLANE * LINE)]


def reorder(block, order, axis):
    picked = [lax.dynamic_index_in_dim(block, i, axis, True) for i in order]
    return jnp.concatenate(picked, axis=axis)


def row_gather(line, level, place):
    moved = [lax.ppermute(line, "row", plane_pairs(flip)) for flip in range(1, PLANE)]
    whole = jnp.concatenate([line, *moved], axis=0)
    order = [(place ^ p) * LINE + (level - z) % LINE for z in range(LINE) for p in range(PLANE)]
    return reorder(whole, order, 0).reshape(LINE * PLANE * line.shape[1], line.shape[2])


def row_reduce(halves, level, place):
    block = halves[0].shape[0] // (LINE * PLANE)
    halves = [h.reshape(LINE, 2, 2, block, h.shape[1]) for h in halves]
    for flips in ((1, 2), (2, 1)):
        for i, flip in enumerate(flips):
            axis = min(3 - flip, halves[i].ndim - 3)
            bit = (place // flip) % 2
            kept = lax.dynamic_index_in_dim(halves[i], bit, axis, False)
            away = lax.dynamic_index_in_dim(halves[i], 1 - bit, axis, False)
            away = lax.ppermute(away.astype(jnp.bfloat16), "row", plane_pairs(flip))
            halves[i] = kept + away.astype(jnp.float32)
    order = [(level + step) % LINE for step in range(LINE)]
    parts = [
        jnp.concatenate([lax.dynamic_index_in_dim(h, i, 0, False) for h in halves], axis=1)
        for i in order
    ]
    moved = [line_shift(parts[step].astype(jnp.bfloat16), step) for step in range(1, LINE)]
    total = parts[0]
    for part in moved:
        total = total + part.astype(jnp.float32)
    return total


def line_gather(block):
    whole = lax.all_gather(block, "row", axis=0, tiled=False, axis_index_groups=LINES)
    return whole


def line_reduce(parts):
    return lax.psum_scatter(
        parts, "row", scatter_dimension=0, tiled=False, axis_index_groups=LINES
    )


def plane_move(block, move):
    return lax.ppermute(block, "row", plane_pairs(move))


def plane_exchange(block):
    far = swap_cores(block[1])
    pairs = [jnp.stack([block[0, m], far[m]]) for m in range(PLANE)]
    moved = {m: plane_move(pairs[m], m) for m in (1, 2, 3)}
    return [pairs[0], moved[1], moved[2], moved[3]]


def plane_all(block):
    groups = [[z * 2 * PLANE + d for d in range(2 * PLANE)] for z in range(LINE)]
    return lax.all_to_all(
        block, GRID, split_axis=0, concat_axis=0, tiled=True, axis_index_groups=groups
    )


def expert_body(
    where_ref,
    x_ref,
    cot_ref,
    weights_ref,
    router_ref,
    _,
    grad_in_ref,
    mix_ref,
    grad_expert_ref,
    act_ref,
    grad_gate_ref,
    grad_up_ref,
    grad_logits_ref,
):
    bf16, f32 = jnp.bfloat16, jnp.float32
    core, expert = where_ref[1], where_ref[2]
    nt = (((1,), (1,)), ((), ()))
    width = x_ref.shape[1]
    x = x_ref[...]
    half = x.shape[0] // 2
    there = jnp.concatenate([cot_ref[0, core], cot_ref[0, 1 - core]], axis=0)
    mask = there[:, width:].astype(f32) > 0
    upstream = there[:, :width].astype(f32)
    router = router_ref[...]
    logits = jnp.dot(x, router, preferred_element_type=f32)
    top = jnp.max(jnp.where(mask, logits, MASKED), axis=-1, keepdims=True)
    exponent = jnp.where(mask, jnp.exp(logits - top), 0.0)
    gates = exponent / jnp.maximum(jnp.sum(exponent, axis=-1, keepdims=True), 1e-30)
    mine = lax.broadcasted_iota(jnp.int32, gates.shape, 1) == expert
    slot_gate = jnp.sum(jnp.where(mine, gates, 0.0), axis=-1, keepdims=True)
    grad_expert = (upstream * slot_gate).astype(bf16)
    grad_expert_ref[...] = grad_expert
    cols = weights_ref.shape[3] // 3
    parts, out = [], None
    for side in range(2):
        gate_w = weights_ref[:, side, :, :cols].reshape(width, cols)
        up_w = weights_ref[:, side, :, cols : 2 * cols].reshape(width, cols)
        down_t = weights_ref[:, side, :, 2 * cols :].reshape(width, cols)
        gate_value = jnp.dot(x, gate_w, preferred_element_type=f32)
        up_value = jnp.dot(x, up_w, preferred_element_type=f32)
        sigmoid = 1.0 / (1.0 + jnp.exp(-gate_value))
        silu = gate_value * sigmoid
        act = (silu * up_value).astype(bf16)
        part = lax.dot_general(act, down_t, nt, preferred_element_type=f32)
        out = part if out is None else out + part
        grad_act = jnp.dot(grad_expert, down_t, preferred_element_type=f32)
        slope = sigmoid * (1.0 + gate_value * (1.0 - sigmoid))
        grad_gate = (grad_act * up_value * slope).astype(bf16)
        grad_up = (grad_act * silu).astype(bf16)
        act_ref[:, side * cols : (side + 1) * cols] = act
        grad_gate_ref[:, side * cols : (side + 1) * cols] = grad_gate
        grad_up_ref[:, side * cols : (side + 1) * cols] = grad_up
        parts.append((grad_gate, grad_up, gate_w, up_w))
    scaled = (out * slot_gate).astype(bf16)
    mix_ref[0, core] = scaled[:half]
    mix_ref[0, 1 - core] = scaled[half:]
    pick_grad = slot_gate * jnp.sum(out * upstream, axis=-1, keepdims=True)
    grad_logits = (pick_grad * (jnp.where(mine, 1.0, 0.0) - gates)).astype(bf16)
    grad_logits_ref[...] = grad_logits
    grad_in = lax.dot_general(grad_logits, router, nt, preferred_element_type=f32)
    for grad_gate, grad_up, gate_w, up_w in parts:
        grad_in += lax.dot_general(grad_gate, gate_w, nt, preferred_element_type=f32)
        grad_in += lax.dot_general(grad_up, up_w, nt, preferred_element_type=f32)
    grad_in_ref[...] = grad_in.astype(bf16)


def expert_rows(move, place, core, expert, x, cot, weights, router, mixture):
    slots, width = x.shape
    cols = weights.shape[3] // 3
    where = jnp.stack([place, core, expert]).astype(jnp.int32)

    def whole(shape):
        return pl.BlockSpec(shape, lambda i, w: (0,) * len(shape))

    outs = [width, width, width, 2 * cols, 2 * cols, 2 * cols, router.shape[1]]
    out_specs = [whole((slots, n)) for n in outs]
    out_shape = [jax.ShapeDtypeStruct((slots, n), jnp.bfloat16) for n in outs]
    mix_block = (1, 2, slots // 2, width)
    out_specs[1] = pl.BlockSpec(mix_block, lambda i, w: (w[0] ^ move, 0, 0, 0))
    out_shape[1] = jax.ShapeDtypeStruct((PLANE, *mix_block[1:]), jnp.bfloat16)
    resident = pl.BlockSpec(memory_space=pltpu.VMEM)
    first = mixture is None
    cot_spec = pl.BlockSpec((1, *cot.shape[1:]), lambda i, w: (w[0] ^ move, 0, 0, 0))
    anywhere = pl.BlockSpec(memory_space=pl.ANY)
    return pl.pallas_call(
        expert_body,
        grid_spec=pltpu.PrefetchScalarGridSpec(
            num_scalar_prefetch=1,
            grid=(1,),
            in_specs=[whole(x.shape), cot_spec, resident, resident, anywhere],
            out_specs=out_specs,
        ),
        out_shape=out_shape,
        input_output_aliases={} if first else {5: 1},
        compiler_params=pltpu.CompilerParams(vmem_limit_bytes=40 << 20),
        cost_estimate=pl.CostEstimate(
            flops=24 * slots * width * cols,
            bytes_accessed=2 * (5 * slots * width + 6 * slots * cols),
            transcendentals=slots * 2 * cols,
        ),
        name="expert_rows",
    )(where, x, cot, weights, router, x if first else mixture)


def picked(slots, share):
    ids = lax.broadcasted_iota(jnp.int32, (share, slots.shape[1]), 0)
    rows = [(slots[e : e + 1] == ids).astype(jnp.bfloat16) for e in range(slots.shape[0])]
    return jnp.concatenate(rows, axis=0)


def select_body(slots_ref, own_ref, other_ref, *rest):
    out_ref = rest[-1]
    share = out_ref.shape[3]
    pick = picked(slots_ref[0], share)
    half, width = own_ref.shape[1], own_ref.shape[2]
    rows = jnp.dot(pick[:, :half], own_ref[0], preferred_element_type=jnp.float32)
    rows += jnp.dot(pick[:, half:], other_ref[0], preferred_element_type=jnp.float32)
    out_ref[:, :, 0, :, :width] = rows.astype(jnp.bfloat16).reshape(2, PLANE, share, width)
    if len(rest) == 2:
        extra = jnp.dot(pick, rest[0][0], preferred_element_type=jnp.float32)
        extra = extra.astype(jnp.bfloat16)
        out_ref[:, :, 0, :, width:] = extra.reshape(2, PLANE, share, extra.shape[1])


def select_rows(slots, own, other, share, extra=None):
    lines, mates, span = slots.shape
    half, width = own.shape[1:]
    wide = width + (0 if extra is None else extra.shape[2])
    parts = [slots, own, other] + ([] if extra is None else [extra])

    def block(shape):
        return pl.BlockSpec((1, *shape), lambda i: (i, 0, 0))

    specs = [block((mates, span)), block((half, width)), block((half, width))]
    if extra is not None:
        specs.append(block((span, extra.shape[2])))
    return pl.pallas_call(
        select_body,
        grid=(lines,),
        in_specs=specs,
        out_specs=pl.BlockSpec((2, PLANE, 1, share, wide), lambda i: (0, 0, i, 0, 0)),
        out_shape=jax.ShapeDtypeStruct((2, PLANE, lines, share, wide), jnp.bfloat16),
        compiler_params=pltpu.CompilerParams(vmem_limit_bytes=40 << 20),
        cost_estimate=pl.CostEstimate(
            flops=2 * lines * mates * share * span * wide,
            bytes_accessed=2 * lines * (span + mates * share) * wide,
            transcendentals=0,
        ),
        name="select_rows",
    )(*parts)


def combine_body(slots_ref, near_ref, far_ref, kept_ref, away_ref):
    chips, _, share, width = near_ref.shape
    half = kept_ref.shape[1]
    pick = picked(slots_ref[0], share).T
    near = near_ref[:, 0].reshape(chips * share, width)
    far = far_ref[:, 0].reshape(chips * share, width)
    total = jnp.dot(pick, jnp.concatenate([near, far]), preferred_element_type=jnp.float32)
    kept_ref[0] = total[:half].astype(kept_ref.dtype)
    away_ref[0] = total[half:].astype(away_ref.dtype)


def combine_rows(slots, near, far, far_block=0):
    lines, mates, span = slots.shape
    chips = mates // 2
    share, width = near.shape[2:]
    part = pl.BlockSpec((1, span // 2, width), lambda i: (i, 0, 0))
    shape = (lines, span // 2, width)
    return pl.pallas_call(
        combine_body,
        grid=(lines,),
        in_specs=[
            pl.BlockSpec((1, mates, span), lambda i: (i, 0, 0)),
            pl.BlockSpec((chips, 1, share, width), lambda i: (0, i, 0, 0)),
            pl.BlockSpec((chips, 1, share, width), lambda i: (far_block, i, 0, 0)),
        ],
        out_specs=[part, part],
        out_shape=[
            jax.ShapeDtypeStruct(shape, jnp.float32),
            jax.ShapeDtypeStruct(shape, jnp.bfloat16),
        ],
        compiler_params=pltpu.CompilerParams(vmem_limit_bytes=40 << 20),
        cost_estimate=pl.CostEstimate(
            flops=2 * lines * mates * share * span * width,
            bytes_accessed=2 * lines * (2 * span + mates * share) * width,
            transcendentals=0,
        ),
        name="combine_rows",
    )(slots, near, far)


def shard_body(pieces, left_refs, right_refs, out_ref):
    count, _, block, _ = out_ref.shape
    lefts = [ref[...].T for ref in left_refs]
    for i in range(len(right_refs) // pieces):
        rights = right_refs[i * pieces : (i + 1) * pieces]
        full = None
        for left, right in zip(lefts, rights):
            part = jnp.dot(left, right[...], preferred_element_type=jnp.float32)
            full = part if full is None else full + part
        full = full.astype(jnp.bfloat16)
        cols = full.shape[1] // 2
        for core in range(2):
            part = full[:, core * cols : (core + 1) * cols]
            out_ref[:, core, :, i * cols : (i + 1) * cols] = part.reshape(count, block, cols)


def shard_grad(lefts, rights, rows, count=4):
    pieces = len(lefts)
    slots, width = lefts[0].shape
    cols = rights[0].shape[1] // 2
    block = width // rows
    wide = cols * (len(rights) // pieces)

    def body(*refs):
        shard_body(pieces, refs[:pieces], refs[pieces:-1], refs[-1])

    out = pl.pallas_call(
        body,
        grid=(rows // count,),
        in_specs=[pl.BlockSpec((slots, count * block), lambda i: (0, i)) for _ in lefts]
        + [pl.BlockSpec((slots, 2 * cols), lambda i: (0, 0)) for _ in rights],
        out_specs=pl.BlockSpec((count, 2, block, wide), lambda i: (i, 0, 0, 0)),
        out_shape=jax.ShapeDtypeStruct((rows, 2, block, wide), jnp.bfloat16),
        compiler_params=pltpu.CompilerParams(vmem_limit_bytes=48 << 20),
        cost_estimate=pl.CostEstimate(
            flops=4 * pieces * slots * width * wide,
            bytes_accessed=2 * (pieces * slots * (width + 2 * wide) + 2 * width * wide),
            transcendentals=0,
        ),
        name="shard_grad",
    )(*lefts, *rights)
    return out.reshape(2 * rows, block, wide)


def tokens_move(
    hidden_in,
    segments,
    routes,
    attention_gain,
    query_weight,
    key_matrix,
    value_matrix,
    output_weight,
    expert_gain,
    router_weight,
    gate_weight,
    up_weight,
    down_weight,
    cotangent,
):
    bf16, f32 = jnp.bfloat16, jnp.float32
    core, row = lax.axis_index("col"), lax.axis_index("row")
    level, place = row // PLANE, row % PLANE
    local = hidden_in.shape[0]
    span = segments.shape[1]
    row_block = query_weight.shape[0]
    rows = MODEL_WIDTH // row_block
    hidden_block = gate_weight.shape[2]
    ffe = 2 * hidden_block
    capacity = max(2, 3 * span * TOPK // (2 * E))
    share = capacity // 2
    head_cols = query_weight.shape[1]
    kv_cols = key_matrix.shape[1]
    heads = head_cols // HEAD_SIZE
    mates = 2 * PLANE
    my_expert = row * 2 + core
    relative = [(place * 2 + core) ^ (2 * m + k) for k in range(2) for m in range(PLANE)]
    nt = (((1,), (1,)), ((), ()))
    tn = (((0,), (0,)), ((), ()))

    packed = jnp.concatenate(
        [
            query_weight,
            key_matrix,
            value_matrix,
            output_weight.T,
            router_weight,
            attention_gain[:, None],
            expert_gain[:, None],
            jnp.zeros((row_block, 128 - E - 2), bf16),
        ],
        axis=1,
    )
    packed_line = jnp.stack([packed] + [line_shift(packed, step) for step in range(1, LINE)])
    routes_own = after(routes.T, packed)
    routes_line = [routes_own] + [line_shift(routes_own, step) for step in range(1, LINE)]
    routes_line = reorder(jnp.stack(routes_line), [(level - z) % LINE for z in range(LINE)], 0)
    packed_full = row_gather(packed_line, level, place)
    o0 = head_cols + 2 * kv_cols
    qkv_cols, out_full = packed_full[:, :o0], packed_full[:, o0:]
    output_t = out_full[:, :head_cols]
    router_full = out_full[:, head_cols : head_cols + E]
    gain_first = out_full[:, head_cols + E].astype(f32)
    gain_second = out_full[:, head_cols + E + 1].astype(f32)

    expert_ids = jnp.arange(E, dtype=jnp.int32)
    slot_near, slot_there, masks = [], [], []
    for i in range(LINE):
        named, counts = slot_ranks(routes_line[i].T)
        slot_of = jnp.where(named, counts - core * share, -1).T
        slot_of = lax.dynamic_slice_in_dim(own_first(slot_of, core, 1), level * mates, mates)
        slot_there.append(slot_of)
        slot_near.append(reorder(slot_of, relative, 0))
        masks.append(own_first(jnp.pad(named.astype(bf16), ((0, 0), (0, 128 - E))), core, 0))
    slot_near, slot_there, mask_line = [jnp.stack(t) for t in (slot_near, slot_there, masks)]

    slots = LINE * share * mates

    nil = packed_line[0, 0, 0] * 0
    weights = jnp.concatenate(
        [gate_weight, up_weight, down_weight.transpose(0, 2, 1) + nil], axis=2
    )
    weights = exchange(after(weights, routes_line))
    cot_line = line_gather(after(cotangent, packed_line))

    hidden_all = both_cores(hidden_in)
    tokens_all = hidden_all.astype(f32)
    scale_all = lax.rsqrt(jnp.mean(tokens_all * tokens_all, axis=-1, keepdims=True) + EPSILON)
    normed_all = (tokens_all * scale_all * gain_first).astype(bf16)
    places = own_first(positions(segments[0]), core, 0)
    segment_ids = own_first(segments[0], core, 0)
    token_index = own_first(jnp.arange(span, dtype=jnp.int32), core, 0)
    allowed = (segment_ids[:, None] == segment_ids[None, :]) & (
        token_index[None, :] <= token_index[:, None]
    )
    raw = jnp.dot(normed_all, qkv_cols, preferred_element_type=f32)
    queries = apply_rotary(raw[:, :head_cols].reshape(span, heads, HEAD_SIZE), places, 1.0)
    queries = queries.astype(bf16).transpose(1, 0, 2)
    keys = apply_rotary(
        raw[:, head_cols : head_cols + kv_cols].reshape(span, 1, HEAD_SIZE), places, 1.0
    ).astype(bf16)[:, 0]
    values = raw[:, head_cols + kv_cols :].astype(bf16)
    scaling = HEAD_SIZE ** (-0.5)
    attended, log_total = attend_group((queries, keys, values), allowed, scaling)
    attended_low = attended.transpose(1, 0, 2).reshape(span, head_cols).astype(bf16)
    branch_part = lax.dot_general(attended_low, output_t, nt, preferred_element_type=f32)
    tokens_in = hidden_in.astype(f32)
    hidden_mid = tokens_in + sum_cores(branch_part, f32)
    scale_second = lax.rsqrt(jnp.mean(hidden_mid * hidden_mid, axis=-1, keepdims=True) + EPSILON)
    unit_second = hidden_mid * scale_second
    normed_second = (unit_second * gain_second).astype(bf16)

    cot_line = after(cot_line, normed_second)
    cot_swap = swap_cores(cot_line)
    cot_rows = select_rows(slot_there, cot_line, cot_swap, share, mask_line)
    normed_line = line_gather(after(normed_second, weights, cot_rows))
    cot_rows = plane_all(cot_rows.reshape(mates, LINE, share, MODEL_WIDTH + 128))
    normed_swap = swap_cores(normed_line)
    normed_rows = select_rows(slot_near, after(normed_line, cot_rows), normed_swap, share)
    pieces = plane_exchange(normed_rows)

    pieces = [p.reshape(2 * LINE * share, MODEL_WIDTH) for p in pieces]
    cot_rows = cot_rows.reshape(PLANE, 2, LINE * share, MODEL_WIDTH + 128)
    weights = weights.reshape(rows, 2, row_block, 3 * hidden_block)
    done, mixture, back = [], None, []
    for move in range(PLANE):
        if move == 3:
            pieces[3] = after(pieces[3], back[1])
        found = expert_rows(
            move, place, core, my_expert, pieces[move], cot_rows, weights, out_full[:, head_cols:], mixture
        )
        mixture = found[1]
        done.append(found)
        back.append(plane_move(found[0], move) if move else found[0])
    _, _, grad_expert, activation, grad_gate, grad_up, grad_logits = [
        list(a) for a in zip(*done)
    ]

    def combine(table, near, far, far_block=0):
        kept, away = combine_rows(table, near, far, far_block)
        return (kept + swap_cores(away).astype(f32)).astype(bf16)

    shape = (2, LINE, share, MODEL_WIDTH)
    back = [b.reshape(shape) for b in back]
    grad_expert[3] = after(grad_expert[3], back[2])
    down_home = exchange(after(shard_grad(grad_expert, activation, rows), back[3]))
    far = swap_cores(after(jnp.stack([b[1] for b in back]), down_home))
    grad_parts = combine(slot_near, jnp.stack([b[0] for b in back]), far)
    grad_normed = line_reduce(grad_parts).astype(f32)
    router_grad = sum(
        lax.dot_general(g, p, tn, preferred_element_type=f32) for g, p in zip(grad_logits, pieces)
    )
    router_grad = router_grad[:E].T
    mixture = mixture.reshape(mates, LINE, share, MODEL_WIDTH)
    mixture = plane_all(after(mixture, down_home))
    mixture_there = after(mixture, grad_parts)
    mixture_parts = combine(slot_there, mixture_there, mixture_there, 1)
    mixture_own = line_reduce(mixture_parts).astype(f32)
    gate_up_home = shard_grad(pieces, grad_gate + grad_up, rows)
    gate_up_home = exchange(after(gate_up_home, mixture))

    grad_normed = after(grad_normed, mixture_parts)
    tilted = grad_normed * gain_second
    gain_second_grad = jnp.sum(grad_normed * unit_second, axis=0)
    grad_hidden = cotangent.astype(f32) + scale_second * (
        tilted - unit_second * jnp.mean(tilted * unit_second, axis=-1, keepdims=True)
    )
    branch_all = both_cores(grad_hidden.astype(bf16))

    output_t_grad = lax.dot_general(branch_all, attended_low, tn, preferred_element_type=f32)
    grad_attended = jnp.dot(branch_all, output_t, preferred_element_type=f32).astype(bf16)
    grad_attended = grad_attended.reshape(span, heads, HEAD_SIZE).transpose(1, 0, 2)
    grad_queries, grad_keys, grad_values = attend_back(
        (queries, keys, values, log_total, grad_attended), allowed, scaling
    )
    grad_query_low = (
        apply_rotary(grad_queries.transpose(1, 0, 2), places, -1.0)
        .reshape(span, head_cols)
        .astype(bf16)
    )
    grad_key_low = apply_rotary(grad_keys[:, None], places, -1.0)[:, 0].astype(bf16)
    grad_qkv = jnp.concatenate([grad_query_low, grad_key_low, grad_values.astype(bf16)], axis=1)
    qkv_grad = lax.dot_general(normed_all, grad_qkv, tn, preferred_element_type=f32)
    first_part = lax.dot_general(grad_qkv, qkv_cols, nt, preferred_element_type=f32)
    unit_all = tokens_all * scale_all
    gain_first_grad = jnp.sum(first_part * unit_all, axis=0)
    grad_first = sum_cores(first_part, f32)
    unit_first = tokens_in * scale_all[:local]
    tilted_first = grad_first * gain_first
    input_grad = grad_hidden + scale_all[:local] * (
        tilted_first - unit_first * jnp.mean(tilted_first * unit_first, axis=-1, keepdims=True)
    )
    block_out = (hidden_mid + mixture_own).astype(bf16)

    extra = jnp.concatenate(
        [
            router_grad,
            gain_second_grad[:, None],
            jnp.zeros((MODEL_WIDTH, 128 - E - 1), f32),
        ],
        axis=1,
    )
    down_home = after(down_home, grad_qkv)
    pad = jnp.zeros((MODEL_WIDTH, 127), f32)
    owned = row_reduce(
        [
            jnp.concatenate([output_t_grad, extra], axis=1),
            jnp.concatenate([qkv_grad, gain_first_grad[:, None], pad], axis=1),
        ],
        level,
        place,
    )
    output_own, owned = owned[:, :head_cols], owned[:, head_cols:]
    small_own, qkv_own = owned[:, :128], owned[:, 128 : 128 + o0]
    small_own = jnp.concatenate([small_own[:, : E + 1], owned[:, 128 + o0 : 129 + o0]], axis=1)
    small_own = small_own + swap_cores(small_own)
    gate_up_home = after(gate_up_home, small_own)
    return (
        block_out,
        input_grad,
        small_own[:, E + 1],
        qkv_own[:, :head_cols],
        qkv_own[:, head_cols : head_cols + kv_cols],
        qkv_own[:, head_cols + kv_cols :],
        output_own[:, :head_cols].T,
        small_own[:, E],
        small_own[:, :E],
        gate_up_home[:, :, :hidden_block].astype(f32),
        gate_up_home[:, :, hidden_block:].astype(f32),
        down_home.astype(f32).transpose(0, 2, 1),
    )


def solution(mesh):
    in_specs = (
        P(("row", "col"), None),
        P("row", None),
        P("row", None),
        P("row"),
        P("row", "col"),
        P("row", "col"),
        P("row", "col"),
        P("col", "row"),
        P("row"),
        P("row", None),
        P(None, "row", "col"),
        P(None, "row", "col"),
        P(None, "col", "row"),
        P(("row", "col"), None),
    )
    out_specs = (
        P(("row", "col"), None),
        P(("row", "col"), None),
        P("row"),
        P("row", "col"),
        P("row", "col"),
        P("row", "col"),
        P("col", "row"),
        P("row"),
        P("row", None),
        P(None, "row", "col"),
        P(None, "row", "col"),
        P(None, "col", "row"),
    )
    rows, cols = mesh.shape["row"], mesh.shape["col"]
    one_each = rows == 4 * PLANE and cols == KEY_VALUE_HEADS and rows * cols == E
    return jax.shard_map(
        tokens_move if one_each else weights_move, mesh=mesh,
        in_specs=in_specs,
        out_specs=out_specs,
        check_vma=False,
    )
```

```python
import jax
import jax.numpy as jnp
from jax import lax
from jax.experimental import pallas as pl
from jax.experimental.pallas import tpu as pltpu
from jax.sharding import PartitionSpec as P

MODEL_WIDTH = 1536
QUERY_HEADS = 12
KEY_VALUE_HEADS = 2
HEAD_SIZE = 128
E = 32
TOPK = 4


EPSILON = 1e-06
ROPE_BASE = 1000000.0
MASKED = -1e30


def positions(segment_ids):
    total_length = segment_ids.shape[0]
    token_index = jnp.arange(total_length, dtype=jnp.int32)
    earlier = (segment_ids[:, None] == segment_ids[None, :]) & (
        token_index[None, :] < token_index[:, None]
    )
    return jnp.sum(earlier.astype(jnp.int32), axis=1)


def apply_rotary(values, places, direction):
    half_size = values.shape[-1] // 2
    frequency = ROPE_BASE ** (-2.0 * jnp.arange(half_size, dtype=jnp.float32) / values.shape[-1])
    angles = places.astype(jnp.float32)[:, None] * frequency[None, :]
    cosine_part = jnp.cos(angles)[:, None, :]
    sine_part = direction * jnp.sin(angles)[:, None, :]
    first_half = values[..., :half_size]
    second_half = values[..., half_size:]
    return jnp.concatenate(
        [
            first_half * cosine_part - second_half * sine_part,
            second_half * cosine_part + first_half * sine_part,
        ],
        axis=-1,
    )


def slot_ranks(route_ids):
    total_length = route_ids.shape[0]
    token_index = jnp.arange(total_length, dtype=jnp.int32)
    expert_ids = jnp.arange(E, dtype=jnp.int32)
    named = jnp.any(route_ids[:, :, None] == expert_ids[None, None, :], axis=1)
    before = (token_index[None, :] < token_index[:, None]).astype(jnp.bfloat16)
    counts = jnp.dot(before, named.astype(jnp.bfloat16), preferred_element_type=jnp.float32)
    return (named, counts.astype(jnp.int32))


def slot_tables(route_ids, experts, capacity):
    flat_ids = route_ids.reshape(-1)
    named, counts = slot_ranks(route_ids)
    rank_ids = jnp.sum(
        jnp.where(
            route_ids[:, :, None] == jnp.arange(experts, dtype=jnp.int32)[None, None, :],
            counts[:, None, :],
            0,
        ),
        axis=-1,
    ).reshape(-1)
    pair_slot = flat_ids * capacity + rank_ids
    owners = jnp.arange(flat_ids.shape[0], dtype=jnp.int32) // route_ids.shape[1]
    token_of = jnp.zeros((experts * capacity,), jnp.int32).at[pair_slot].set(owners)
    filled = jnp.zeros((experts * capacity,), jnp.int32).at[pair_slot].set(1)
    return (pair_slot, token_of, filled)


def masked_scores(queries, key_row_block, allowed, scaling):
    scores = (
        jnp.einsum("gqd,kd->gqk", queries, key_row_block, preferred_element_type=jnp.float32)
        * scaling
    )
    return jnp.where(allowed[None], scores, MASKED)


def attend_group(operands, allowed, scaling):
    queries, key_row_block, value_row_block = operands
    scores = masked_scores(queries, key_row_block, allowed, scaling)
    highest = jnp.max(scores, axis=-1, keepdims=True)
    exponent = jnp.exp(scores - highest)
    summed = jnp.sum(exponent, axis=-1, keepdims=True)
    weights_low = (exponent / summed).astype(jnp.bfloat16)
    result = jnp.einsum(
        "gqk,kd->gqd", weights_low, value_row_block, preferred_element_type=jnp.float32
    )
    return (result, highest + jnp.log(summed))


def attend_back(operands, allowed, scaling):
    queries, key_row_block, value_row_block, log_total, grad_result = operands
    scores = masked_scores(queries, key_row_block, allowed, scaling)
    weights_full = jnp.where(allowed[None], jnp.exp(scores - log_total), 0.0)
    weights_low = weights_full.astype(jnp.bfloat16)
    grad_values = jnp.einsum(
        "gqk,gqd->kd", weights_low, grad_result, preferred_element_type=jnp.float32
    )
    grad_weights = jnp.einsum(
        "gqd,kd->gqk", grad_result, value_row_block, preferred_element_type=jnp.float32
    )
    centre = jnp.sum(weights_full * grad_weights, axis=-1, keepdims=True)
    grad_scores = (weights_full * (grad_weights - centre)).astype(jnp.bfloat16)
    grad_queries = (
        jnp.einsum("gqk,kd->gqd", grad_scores, key_row_block, preferred_element_type=jnp.float32)
        * scaling
    )
    grad_keys = (
        jnp.einsum("gqk,gqd->kd", grad_scores, queries, preferred_element_type=jnp.float32)
        * scaling
    )
    return (grad_queries, grad_keys, grad_values)


def weights_move(
    hidden_in,
    segments,
    routes,
    attention_gain,
    query_weight,
    key_matrix,
    value_matrix,
    output_weight,
    expert_gain,
    router_weight,
    gate_weight,
    up_weight,
    down_weight,
    cotangent,
):
    gain_first, query_cols, key_cols, value_cols, output_rows = (
        lax.all_gather(attention_gain, "row", axis=0, tiled=True),
        lax.all_gather(query_weight, "row", axis=0, tiled=True),
        lax.all_gather(key_matrix, "row", axis=0, tiled=True),
        lax.all_gather(value_matrix, "row", axis=0, tiled=True),
        lax.all_gather(output_weight, "row", axis=1, tiled=True),
    )
    query_full, gathered_keys, gathered_values, output_full = (
        lax.all_gather(query_cols, "col", axis=1, tiled=True),
        lax.all_gather(key_cols, "col", axis=1, tiled=True),
        lax.all_gather(value_cols, "col", axis=1, tiled=True),
        lax.all_gather(output_rows, "col", axis=0, tiled=True),
    )
    gain_second, router_full, gate_full, up_full, down_full = (
        lax.all_gather(expert_gain, "row", axis=0, tiled=True),
        lax.all_gather(router_weight, "row", axis=0, tiled=True),
        lax.all_gather(gate_weight, "row", axis=1, tiled=True),
        lax.all_gather(up_weight, "row", axis=1, tiled=True),
        lax.all_gather(down_weight, "row", axis=2, tiled=True),
    )
    local_row_block = hidden_in.shape[0]
    sequence_span_length = segments.shape[1]
    first_row = lax.axis_index("col") * local_row_block
    segment_ids = segments[0]
    places_all = positions(segment_ids)
    local_positions = lax.dynamic_slice_in_dim(places_all, first_row, local_row_block)
    own_segments = lax.dynamic_slice_in_dim(segment_ids, first_row, local_row_block)
    query_index = first_row + jnp.arange(local_row_block, dtype=jnp.int32)
    key_index = jnp.arange(sequence_span_length, dtype=jnp.int32)
    allowed = (own_segments[:, None] == segment_ids[None, :]) & (
        key_index[None, :] <= query_index[:, None]
    )
    tokens_in = hidden_in.astype(jnp.float32)
    scale_first = lax.rsqrt(jnp.mean(tokens_in * tokens_in, axis=-1, keepdims=True) + EPSILON)
    unit_first = tokens_in * scale_first
    normed_first = (unit_first * gain_first.astype(jnp.float32)).astype(jnp.bfloat16)
    query_raw = jnp.dot(normed_first, query_full, preferred_element_type=jnp.float32).reshape(
        local_row_block, QUERY_HEADS, HEAD_SIZE
    )
    unrotated_keys = jnp.dot(
        normed_first, gathered_keys, preferred_element_type=jnp.float32
    ).reshape(local_row_block, KEY_VALUE_HEADS, HEAD_SIZE)
    values_reduced = jnp.dot(
        normed_first, gathered_values, preferred_element_type=jnp.float32
    ).astype(jnp.bfloat16)
    rotated_queries = apply_rotary(query_raw, local_positions, 1.0).astype(jnp.bfloat16)
    rotated_keys = (
        apply_rotary(unrotated_keys, local_positions, 1.0)
        .astype(jnp.bfloat16)
        .reshape(local_row_block, KEY_VALUE_HEADS * HEAD_SIZE)
    )
    key_row_block, value_row_block = (
        lax.all_gather(rotated_keys, "col", axis=0, tiled=True),
        lax.all_gather(values_reduced, "col", axis=0, tiled=True),
    )
    heads_per_group = QUERY_HEADS // KEY_VALUE_HEADS
    scaling = HEAD_SIZE ** (-0.5)
    grouped_queries = rotated_queries.reshape(
        local_row_block, KEY_VALUE_HEADS, heads_per_group, HEAD_SIZE
    ).transpose(1, 2, 0, 3)
    grouped_keys = key_row_block.reshape(
        sequence_span_length, KEY_VALUE_HEADS, HEAD_SIZE
    ).transpose(1, 0, 2)
    grouped_values = value_row_block.reshape(
        sequence_span_length, KEY_VALUE_HEADS, HEAD_SIZE
    ).transpose(1, 0, 2)
    attended, log_total = lax.map(
        lambda operands: attend_group(operands, allowed, scaling),
        (grouped_queries, grouped_keys, grouped_values),
    )
    attended_low = (
        attended.transpose(2, 0, 1, 3)
        .reshape(local_row_block, QUERY_HEADS * HEAD_SIZE)
        .astype(jnp.bfloat16)
    )
    branch = jnp.dot(attended_low, output_full, preferred_element_type=jnp.float32)
    hidden_mid = tokens_in + branch
    scale_second = lax.rsqrt(jnp.mean(hidden_mid * hidden_mid, axis=-1, keepdims=True) + EPSILON)
    unit_second = hidden_mid * scale_second
    normed_second = (unit_second * gain_second.astype(jnp.float32)).astype(jnp.bfloat16)
    normed_all, upstream_all = (
        lax.all_gather(normed_second, "col", axis=0, tiled=True),
        lax.all_gather(cotangent, "col", axis=0, tiled=True),
    )
    logits = jnp.dot(normed_all, router_full, preferred_element_type=jnp.float32)
    expert_ids = jnp.arange(E, dtype=jnp.int32)
    chosen_mask = routes[:, :, None] == expert_ids[None, None, :]
    chosen = jnp.sum(jnp.where(chosen_mask, logits[:, None, :], 0.0), axis=-1)
    exponent = jnp.exp(chosen - jnp.max(chosen, axis=-1, keepdims=True))
    route_gates = exponent / jnp.sum(exponent, axis=-1, keepdims=True)
    group_width = 4
    capacity = max(2, 3 * sequence_span_length * TOPK // (2 * E))
    pair_slot, token_of, filled = slot_tables(routes, E, capacity)
    slot_gate = jnp.zeros((E * capacity,), jnp.float32).at[pair_slot].set(route_gates.reshape(-1))
    group_rows = group_width * capacity

    def expert_step(accumulated, group_index):
        mixture_sum, input_sum = accumulated
        offset = group_index * group_rows
        row_ids = lax.dynamic_slice_in_dim(token_of, offset, group_rows)
        occupied = lax.dynamic_slice_in_dim(filled, offset, group_rows) > 0
        slot_weight = lax.dynamic_slice_in_dim(slot_gate, offset, group_rows)
        first_expert = group_index * group_width
        gate_block = lax.dynamic_slice_in_dim(gate_full, first_expert, group_width, 0)
        up_block = lax.dynamic_slice_in_dim(up_full, first_expert, group_width, 0)
        down_block = lax.dynamic_slice_in_dim(down_full, first_expert, group_width, 0)
        inputs = jnp.where(
            occupied[:, None], normed_all[row_ids], jnp.zeros((), jnp.bfloat16)
        ).reshape(group_width, capacity, MODEL_WIDTH)
        upstream = upstream_all[row_ids].astype(jnp.float32)
        gate_value = jnp.einsum(
            "ecd,edf->ecf", inputs, gate_block, preferred_element_type=jnp.float32
        )
        up_value = jnp.einsum("ecd,edf->ecf", inputs, up_block, preferred_element_type=jnp.float32)
        sigmoid_gate = jax.nn.sigmoid(gate_value)
        silu_gate = gate_value * sigmoid_gate
        activation = (silu_gate * up_value).astype(jnp.bfloat16)
        partial_out = jnp.einsum(
            "ecf,efd->ecd", activation, down_block, preferred_element_type=jnp.float32
        ).reshape(group_rows, MODEL_WIDTH)
        mixture_sum = mixture_sum.at[row_ids].add(partial_out * slot_weight[:, None])
        slot_grad = jnp.sum(partial_out * upstream, axis=-1)
        grad_expert = (
            (upstream * slot_weight[:, None])
            .astype(jnp.bfloat16)
            .reshape(group_width, capacity, MODEL_WIDTH)
        )
        grad_act = jnp.einsum(
            "ecd,efd->ecf", grad_expert, down_block, preferred_element_type=jnp.float32
        )
        slope = sigmoid_gate * (1.0 + gate_value * (1.0 - sigmoid_gate))
        grad_gate = (grad_act * up_value * slope).astype(jnp.bfloat16)
        grad_up = (grad_act * silu_gate).astype(jnp.bfloat16)
        grad_inputs = jnp.einsum(
            "ecf,edf->ecd", grad_gate, gate_block, preferred_element_type=jnp.float32
        )
        grad_inputs = grad_inputs + jnp.einsum(
            "ecf,edf->ecd", grad_up, up_block, preferred_element_type=jnp.float32
        )
        input_sum = input_sum.at[row_ids].add(grad_inputs.reshape(group_rows, MODEL_WIDTH))
        gate_piece = jnp.einsum(
            "ecd,ecf->edf", inputs, grad_gate, preferred_element_type=jnp.float32
        )
        up_piece = jnp.einsum("ecd,ecf->edf", inputs, grad_up, preferred_element_type=jnp.float32)
        down_piece = jnp.einsum(
            "ecf,ecd->efd", activation, grad_expert, preferred_element_type=jnp.float32
        )
        return ((mixture_sum, input_sum), (slot_grad, gate_piece, up_piece, down_piece))

    initial = (
        jnp.zeros((sequence_span_length, MODEL_WIDTH), jnp.float32),
        jnp.zeros((sequence_span_length, MODEL_WIDTH), jnp.float32),
    )
    sums_out, pieces = lax.scan(expert_step, initial, jnp.arange(E // group_width, dtype=jnp.int32))
    mixture_part, input_part = sums_out
    slot_grads, gate_pieces, up_pieces, down_pieces = pieces
    hidden_cols = gate_full.shape[2]
    gate_grad = gate_pieces.reshape(E, MODEL_WIDTH, hidden_cols)
    up_grad = up_pieces.reshape(E, MODEL_WIDTH, hidden_cols)
    down_grad = down_pieces.reshape(E, hidden_cols, MODEL_WIDTH)
    pick_grads = slot_grads.reshape(-1)[pair_slot].reshape(sequence_span_length, TOPK)
    mixture_own, input_own, pick_own = (
        lax.psum_scatter(mixture_part, "col", scatter_dimension=0, tiled=True),
        lax.psum_scatter(input_part, "col", scatter_dimension=0, tiled=True),
        lax.psum_scatter(pick_grads, "col", scatter_dimension=0, tiled=True),
    )
    block_out = (hidden_mid + mixture_own).astype(jnp.bfloat16)
    own_gates = lax.dynamic_slice_in_dim(route_gates, first_row, local_row_block)
    own_mask = lax.dynamic_slice_in_dim(chosen_mask, first_row, local_row_block)
    centred = own_gates * (pick_own - jnp.sum(own_gates * pick_own, axis=-1, keepdims=True))
    grad_logits = jnp.sum(jnp.where(own_mask, centred[:, :, None], 0.0), axis=1).astype(
        jnp.bfloat16
    )
    grad_normed = input_own + jnp.dot(
        grad_logits, router_full.T, preferred_element_type=jnp.float32
    )
    router_grad = jnp.dot(normed_second.T, grad_logits, preferred_element_type=jnp.float32)
    tilted_second = grad_normed * gain_second.astype(jnp.float32)
    gain_second_grad = jnp.sum(grad_normed * unit_second, axis=0)
    grad_hidden = cotangent.astype(jnp.float32) + scale_second * (
        tilted_second - unit_second * jnp.mean(tilted_second * unit_second, axis=-1, keepdims=True)
    )
    grad_branch = grad_hidden.astype(jnp.bfloat16)
    output_grad = jnp.dot(attended_low.T, grad_branch, preferred_element_type=jnp.float32)
    attended_gradient = jnp.dot(
        grad_branch, output_full.T, preferred_element_type=jnp.float32
    ).astype(jnp.bfloat16)
    grouped_gradient = attended_gradient.reshape(
        local_row_block, KEY_VALUE_HEADS, heads_per_group, HEAD_SIZE
    ).transpose(1, 2, 0, 3)
    grad_query_groups, key_gradient_grouped, value_gradient_grouped = lax.map(
        lambda operands: attend_back(operands, allowed, scaling),
        (grouped_queries, grouped_keys, grouped_values, log_total, grouped_gradient),
    )
    grad_query_rot = grad_query_groups.transpose(2, 0, 1, 3).reshape(
        local_row_block, QUERY_HEADS, HEAD_SIZE
    )
    key_gradient_total = key_gradient_grouped.transpose(1, 0, 2).reshape(
        sequence_span_length, KEY_VALUE_HEADS * HEAD_SIZE
    )
    value_gradient_total = value_gradient_grouped.transpose(1, 0, 2).reshape(
        sequence_span_length, KEY_VALUE_HEADS * HEAD_SIZE
    )
    local_keys, value_own = (
        lax.psum_scatter(
            key_gradient_total.astype(jnp.bfloat16), "col", scatter_dimension=0, tiled=True
        ).astype(jnp.float32),
        lax.psum_scatter(
            value_gradient_total.astype(jnp.bfloat16), "col", scatter_dimension=0, tiled=True
        ).astype(jnp.float32),
    )
    grad_query_low = (
        apply_rotary(grad_query_rot, local_positions, -1.0)
        .reshape(local_row_block, QUERY_HEADS * HEAD_SIZE)
        .astype(jnp.bfloat16)
    )
    grad_key_low = (
        apply_rotary(
            local_keys.reshape(local_row_block, KEY_VALUE_HEADS, HEAD_SIZE), local_positions, -1.0
        )
        .reshape(local_row_block, KEY_VALUE_HEADS * HEAD_SIZE)
        .astype(jnp.bfloat16)
    )
    grad_value_low = value_own.astype(jnp.bfloat16)
    grad_normed_first = jnp.dot(grad_query_low, query_full.T, preferred_element_type=jnp.float32)
    grad_normed_first = grad_normed_first + jnp.dot(
        grad_key_low, gathered_keys.T, preferred_element_type=jnp.float32
    )
    grad_normed_first = grad_normed_first + jnp.dot(
        grad_value_low, gathered_values.T, preferred_element_type=jnp.float32
    )
    query_grad = jnp.dot(normed_first.T, grad_query_low, preferred_element_type=jnp.float32)
    key_grad = jnp.dot(normed_first.T, grad_key_low, preferred_element_type=jnp.float32)
    value_grad = jnp.dot(normed_first.T, grad_value_low, preferred_element_type=jnp.float32)
    tilted_first = grad_normed_first * gain_first.astype(jnp.float32)
    gain_first_grad = jnp.sum(grad_normed_first * unit_first, axis=0)
    input_grad = grad_hidden + scale_first * (
        tilted_first - unit_first * jnp.mean(tilted_first * unit_first, axis=-1, keepdims=True)
    )
    query_part, key_part, value_part, output_part = (
        lax.psum_scatter(
            query_grad.astype(jnp.bfloat16), "col", scatter_dimension=1, tiled=True
        ).astype(jnp.float32),
        lax.psum_scatter(
            key_grad.astype(jnp.bfloat16), "col", scatter_dimension=1, tiled=True
        ).astype(jnp.float32),
        lax.psum_scatter(
            value_grad.astype(jnp.bfloat16), "col", scatter_dimension=1, tiled=True
        ).astype(jnp.float32),
        lax.psum_scatter(
            output_grad.astype(jnp.bfloat16), "col", scatter_dimension=0, tiled=True
        ).astype(jnp.float32),
    )
    small_total = lax.psum((gain_first_grad, gain_second_grad, router_grad), ("row", "col"))
    query_out, key_out, value_out, output_out, gate_out, up_out, down_out = (
        lax.psum_scatter(
            query_part.astype(jnp.bfloat16), "row", scatter_dimension=0, tiled=True
        ).astype(jnp.float32),
        lax.psum_scatter(
            key_part.astype(jnp.bfloat16), "row", scatter_dimension=0, tiled=True
        ).astype(jnp.float32),
        lax.psum_scatter(
            value_part.astype(jnp.bfloat16), "row", scatter_dimension=0, tiled=True
        ).astype(jnp.float32),
        lax.psum_scatter(
            output_part.astype(jnp.bfloat16), "row", scatter_dimension=1, tiled=True
        ).astype(jnp.float32),
        lax.psum_scatter(
            gate_grad.astype(jnp.bfloat16), "row", scatter_dimension=1, tiled=True
        ).astype(jnp.float32),
        lax.psum_scatter(
            up_grad.astype(jnp.bfloat16), "row", scatter_dimension=1, tiled=True
        ).astype(jnp.float32),
        lax.psum_scatter(
            down_grad.astype(jnp.bfloat16), "row", scatter_dimension=2, tiled=True
        ).astype(jnp.float32),
    )
    row_block = attention_gain.shape[0]
    row_start = lax.axis_index("row") * row_block
    gain_first_out = lax.dynamic_slice_in_dim(small_total[0], row_start, row_block)
    gain_second_out = lax.dynamic_slice_in_dim(small_total[1], row_start, row_block)
    router_out = lax.dynamic_slice_in_dim(small_total[2], row_start, row_block, 0)
    return (
        block_out,
        input_grad,
        gain_first_out,
        query_out,
        key_out,
        value_out,
        output_out,
        gain_second_out,
        router_out,
        gate_out,
        up_out,
        down_out,
    )


GRID = ("row", "col")
PLANE = 4
LINE = 4


def nothing(*refs):
    pass


def after(block, *others):
    anywhere = pl.BlockSpec(memory_space=pl.ANY)
    return pl.pallas_call(
        nothing,
        out_shape=jax.ShapeDtypeStruct(block.shape, block.dtype),
        in_specs=[anywhere] * (1 + len(others)),
        out_specs=anywhere,
        input_output_aliases={0: 0},
        name="after",
    )(block, *others)


def swap_cores(block):
    return lax.ppermute(block, "col", [(0, 1), (1, 0)])


def both_cores(own):
    return jnp.concatenate([own, swap_cores(own)], axis=0)


def sum_cores(partial, kind):
    half = partial.shape[0] // 2
    away = partial[half:].astype(kind)
    return partial[:half] + swap_cores(away).astype(partial.dtype)


def own_first(table, core, axis):
    half = table.shape[axis] // 2
    mine = lax.dynamic_slice_in_dim(table, core * half, half, axis)
    theirs = lax.dynamic_slice_in_dim(table, (1 - core) * half, half, axis)
    return jnp.concatenate([mine, theirs], axis=axis)


def exchange(block):
    return lax.all_to_all(block, GRID, split_axis=0, concat_axis=0, tiled=True)


LINES = [[z * PLANE + p for z in range(LINE)] for p in range(PLANE)]


def line_shift(block, step):
    pairs = [
        (s * PLANE + p, (s + step) % LINE * PLANE + p) for s in range(LINE) for p in range(PLANE)
    ]
    return lax.ppermute(block, "row", pairs)


def plane_pairs(flip):
    return [(r, r ^ flip) for r in range(PLANE * LINE)]


def reorder(block, order, axis):
    picked = [lax.dynamic_index_in_dim(block, i, axis, True) for i in order]
    return jnp.concatenate(picked, axis=axis)


def row_gather(line, level, place):
    moved = [lax.ppermute(line, "row", plane_pairs(flip)) for flip in range(1, PLANE)]
    whole = jnp.concatenate([line, *moved], axis=0)
    order = [(place ^ p) * LINE + (level - z) % LINE for z in range(LINE) for p in range(PLANE)]
    return reorder(whole, order, 0).reshape(LINE * PLANE * line.shape[1], line.shape[2])


def row_reduce(halves, level, place):
    block = halves[0].shape[0] // (LINE * PLANE)
    halves = [h.reshape(LINE, 2, 2, block, h.shape[1]) for h in halves]
    marks = []
    for flips in ((1, 2), (2, 1)):
        for i, flip in enumerate(flips):
            axis = min(3 - flip, halves[i].ndim - 3)
            bit = (place // flip) % 2
            kept = lax.dynamic_index_in_dim(halves[i], bit, axis, False)
            away = lax.dynamic_index_in_dim(halves[i], 1 - bit, axis, False)
            away = lax.ppermute(away.astype(jnp.bfloat16), "row", plane_pairs(flip))
            halves[i] = kept + away.astype(jnp.float32)
            marks.append(halves[i])
    order = [(level + step) % LINE for step in range(LINE)]
    parts = [
        jnp.concatenate([lax.dynamic_index_in_dim(h, i, 0, False) for h in halves], axis=1)
        for i in order
    ]
    moved = [line_shift(parts[step].astype(jnp.bfloat16), step) for step in range(1, LINE)]
    total = parts[0]
    for part in moved:
        total = total + part.astype(jnp.float32)
    return total, marks[2:]


def line_gather(block):
    whole = lax.all_gather(block, "row", axis=0, tiled=False, axis_index_groups=LINES)
    return whole


def line_reduce(parts):
    return lax.psum_scatter(
        parts, "row", scatter_dimension=0, tiled=False, axis_index_groups=LINES
    )


def plane_move(block, move):
    return lax.ppermute(block, "row", plane_pairs(move))


def plane_exchange(block):
    far = swap_cores(block[1])
    pairs = [jnp.stack([block[0, m], far[m]]) for m in range(PLANE)]
    moved = {m: plane_move(pairs[m], m) for m in (1, 2, 3)}
    return [pairs[0], moved[1], moved[2], moved[3]]


def plane_all(block):
    groups = [[z * 2 * PLANE + d for d in range(2 * PLANE)] for z in range(LINE)]
    return lax.all_to_all(
        block, GRID, split_axis=0, concat_axis=0, tiled=True, axis_index_groups=groups
    )


def expert_body(
    where_ref,
    x_ref,
    cot_ref,
    weights_ref,
    router_ref,
    _,
    grad_in_ref,
    mix_ref,
    grad_expert_ref,
    act_ref,
    grad_gate_ref,
    grad_up_ref,
    grad_logits_ref,
):
    bf16, f32 = jnp.bfloat16, jnp.float32
    core, expert = where_ref[1], where_ref[2]
    nt = (((1,), (1,)), ((), ()))
    width = x_ref.shape[1]
    x = x_ref[...]
    half = x.shape[0] // 2
    there = jnp.concatenate([cot_ref[0, core], cot_ref[0, 1 - core]], axis=0)
    mask = there[:, width:].astype(f32) > 0
    upstream = there[:, :width].astype(f32)
    router = router_ref[...]
    logits = jnp.dot(x, router, preferred_element_type=f32)
    top = jnp.max(jnp.where(mask, logits, MASKED), axis=-1, keepdims=True)
    exponent = jnp.where(mask, jnp.exp(logits - top), 0.0)
    gates = exponent / jnp.maximum(jnp.sum(exponent, axis=-1, keepdims=True), 1e-30)
    mine = lax.broadcasted_iota(jnp.int32, gates.shape, 1) == expert
    slot_gate = jnp.sum(jnp.where(mine, gates, 0.0), axis=-1, keepdims=True)
    grad_expert = (upstream * slot_gate).astype(bf16)
    grad_expert_ref[...] = grad_expert
    cols = weights_ref.shape[3] // 3
    parts, out = [], None
    for side in range(2):
        gate_w = weights_ref[:, side, :, :cols].reshape(width, cols)
        up_w = weights_ref[:, side, :, cols : 2 * cols].reshape(width, cols)
        down_t = weights_ref[:, side, :, 2 * cols :].reshape(width, cols)
        gate_value = jnp.dot(x, gate_w, preferred_element_type=f32)
        up_value = jnp.dot(x, up_w, preferred_element_type=f32)
        sigmoid = 1.0 / (1.0 + jnp.exp(-gate_value))
        silu = gate_value * sigmoid
        act = (silu * up_value).astype(bf16)
        part = lax.dot_general(act, down_t, nt, preferred_element_type=f32)
        out = part if out is None else out + part
        grad_act = jnp.dot(grad_expert, down_t, preferred_element_type=f32)
        slope = sigmoid * (1.0 + gate_value * (1.0 - sigmoid))
        grad_gate = (grad_act * up_value * slope).astype(bf16)
        grad_up = (grad_act * silu).astype(bf16)
        act_ref[:, side * cols : (side + 1) * cols] = act
        grad_gate_ref[:, side * cols : (side + 1) * cols] = grad_gate
        grad_up_ref[:, side * cols : (side + 1) * cols] = grad_up
        parts.append((grad_gate, grad_up, gate_w, up_w))
    scaled = (out * slot_gate).astype(bf16)
    mix_ref[0, core] = scaled[:half]
    mix_ref[0, 1 - core] = scaled[half:]
    pick_grad = slot_gate * jnp.sum(out * upstream, axis=-1, keepdims=True)
    grad_logits = (pick_grad * (jnp.where(mine, 1.0, 0.0) - gates)).astype(bf16)
    grad_logits_ref[...] = grad_logits
    grad_in = lax.dot_general(grad_logits, router, nt, preferred_element_type=f32)
    for grad_gate, grad_up, gate_w, up_w in parts:
        grad_in += lax.dot_general(grad_gate, gate_w, nt, preferred_element_type=f32)
        grad_in += lax.dot_general(grad_up, up_w, nt, preferred_element_type=f32)
    grad_in_ref[...] = grad_in.astype(bf16)


def expert_rows(move, place, core, expert, x, cot, weights, router, mixture):
    slots, width = x.shape
    cols = weights.shape[3] // 3
    where = jnp.stack([place, core, expert]).astype(jnp.int32)

    def whole(shape):
        return pl.BlockSpec(shape, lambda i, w: (0,) * len(shape))

    outs = [width, width, width, 2 * cols, 2 * cols, 2 * cols, router.shape[1]]
    out_specs = [whole((slots, n)) for n in outs]
    out_shape = [jax.ShapeDtypeStruct((slots, n), jnp.bfloat16) for n in outs]
    mix_block = (1, 2, slots // 2, width)
    out_specs[1] = pl.BlockSpec(mix_block, lambda i, w: (w[0] ^ move, 0, 0, 0))
    out_shape[1] = jax.ShapeDtypeStruct((PLANE, *mix_block[1:]), jnp.bfloat16)
    resident = pl.BlockSpec(memory_space=pltpu.VMEM)
    first = mixture is None
    cot_spec = pl.BlockSpec((1, *cot.shape[1:]), lambda i, w: (w[0] ^ move, 0, 0, 0))
    anywhere = pl.BlockSpec(memory_space=pl.ANY)
    return pl.pallas_call(
        expert_body,
        grid_spec=pltpu.PrefetchScalarGridSpec(
            num_scalar_prefetch=1,
            grid=(1,),
            in_specs=[whole(x.shape), cot_spec, resident, resident, anywhere],
            out_specs=out_specs,
        ),
        out_shape=out_shape,
        input_output_aliases={} if first else {5: 1},
        compiler_params=pltpu.CompilerParams(vmem_limit_bytes=40 << 20),
        cost_estimate=pl.CostEstimate(
            flops=24 * slots * width * cols,
            bytes_accessed=2 * (5 * slots * width + 6 * slots * cols),
            transcendentals=slots * 2 * cols,
        ),
        name="expert_rows",
    )(where, x, cot, weights, router, x if first else mixture)


def picked(slots, share):
    ids = lax.broadcasted_iota(jnp.int32, (share, slots.shape[1]), 0)
    rows = [(slots[e : e + 1] == ids).astype(jnp.bfloat16) for e in range(slots.shape[0])]
    return jnp.concatenate(rows, axis=0)


def select_body(slots_ref, own_ref, other_ref, *rest):
    out_ref = rest[-1]
    share = out_ref.shape[3]
    pick = picked(slots_ref[0], share)
    half, width = own_ref.shape[1], own_ref.shape[2]
    rows = jnp.dot(pick[:, :half], own_ref[0], preferred_element_type=jnp.float32)
    rows += jnp.dot(pick[:, half:], other_ref[0], preferred_element_type=jnp.float32)
    out_ref[:, :, 0, :, :width] = rows.astype(jnp.bfloat16).reshape(2, PLANE, share, width)
    if len(rest) == 2:
        extra = jnp.dot(pick, rest[0][0], preferred_element_type=jnp.float32)
        extra = extra.astype(jnp.bfloat16)
        out_ref[:, :, 0, :, width:] = extra.reshape(2, PLANE, share, extra.shape[1])


def select_rows(slots, own, other, share, extra=None):
    lines, mates, span = slots.shape
    half, width = own.shape[1:]
    wide = width + (0 if extra is None else extra.shape[2])
    parts = [slots, own, other] + ([] if extra is None else [extra])

    def block(shape):
        return pl.BlockSpec((1, *shape), lambda i: (i, 0, 0))

    specs = [block((mates, span)), block((half, width)), block((half, width))]
    if extra is not None:
        specs.append(block((span, extra.shape[2])))
    return pl.pallas_call(
        select_body,
        grid=(lines,),
        in_specs=specs,
        out_specs=pl.BlockSpec((2, PLANE, 1, share, wide), lambda i: (0, 0, i, 0, 0)),
        out_shape=jax.ShapeDtypeStruct((2, PLANE, lines, share, wide), jnp.bfloat16),
        compiler_params=pltpu.CompilerParams(vmem_limit_bytes=40 << 20),
        cost_estimate=pl.CostEstimate(
            flops=2 * lines * mates * share * span * wide,
            bytes_accessed=2 * lines * (span + mates * share) * wide,
            transcendentals=0,
        ),
        name="select_rows",
    )(*parts)


def combine_body(slots_ref, near_ref, far_ref, kept_ref, away_ref):
    chips, _, share, width = near_ref.shape
    half = kept_ref.shape[1]
    pick = picked(slots_ref[0], share).T
    near = near_ref[:, 0].reshape(chips * share, width)
    far = far_ref[:, 0].reshape(chips * share, width)
    total = jnp.dot(pick, jnp.concatenate([near, far]), preferred_element_type=jnp.float32)
    kept_ref[0] = total[:half].astype(kept_ref.dtype)
    away_ref[0] = total[half:].astype(away_ref.dtype)


def combine_rows(slots, near, far, far_block=0):
    lines, mates, span = slots.shape
    chips = mates // 2
    share, width = near.shape[2:]
    part = pl.BlockSpec((1, span // 2, width), lambda i: (i, 0, 0))
    shape = (lines, span // 2, width)
    return pl.pallas_call(
        combine_body,
        grid=(lines,),
        in_specs=[
            pl.BlockSpec((1, mates, span), lambda i: (i, 0, 0)),
            pl.BlockSpec((chips, 1, share, width), lambda i: (0, i, 0, 0)),
            pl.BlockSpec((chips, 1, share, width), lambda i: (far_block, i, 0, 0)),
        ],
        out_specs=[part, part],
        out_shape=[
            jax.ShapeDtypeStruct(shape, jnp.bfloat16),
            jax.ShapeDtypeStruct(shape, jnp.bfloat16),
        ],
        compiler_params=pltpu.CompilerParams(vmem_limit_bytes=40 << 20),
        cost_estimate=pl.CostEstimate(
            flops=2 * lines * mates * share * span * width,
            bytes_accessed=2 * lines * (2 * span + mates * share) * width,
            transcendentals=0,
        ),
        name="combine_rows",
    )(slots, near, far)


def shard_body(pieces, left_refs, right_refs, out_ref):
    count, _, block, _ = out_ref.shape
    lefts = [ref[...].T for ref in left_refs]
    for i in range(len(right_refs) // pieces):
        rights = right_refs[i * pieces : (i + 1) * pieces]
        full = None
        for left, right in zip(lefts, rights):
            part = jnp.dot(left, right[...], preferred_element_type=jnp.float32)
            full = part if full is None else full + part
        full = full.astype(jnp.bfloat16)
        cols = full.shape[1] // 2
        for core in range(2):
            part = full[:, core * cols : (core + 1) * cols]
            out_ref[:, core, :, i * cols : (i + 1) * cols] = part.reshape(count, block, cols)


def shard_grad(lefts, rights, rows, count=4):
    pieces = len(lefts)
    slots, width = lefts[0].shape
    cols = rights[0].shape[1] // 2
    block = width // rows
    wide = cols * (len(rights) // pieces)

    def body(*refs):
        shard_body(pieces, refs[:pieces], refs[pieces:-1], refs[-1])

    out = pl.pallas_call(
        body,
        grid=(rows // count,),
        in_specs=[pl.BlockSpec((slots, count * block), lambda i: (0, i)) for _ in lefts]
        + [pl.BlockSpec((slots, 2 * cols), lambda i: (0, 0)) for _ in rights],
        out_specs=pl.BlockSpec((count, 2, block, wide), lambda i: (i, 0, 0, 0)),
        out_shape=jax.ShapeDtypeStruct((rows, 2, block, wide), jnp.bfloat16),
        compiler_params=pltpu.CompilerParams(vmem_limit_bytes=48 << 20),
        cost_estimate=pl.CostEstimate(
            flops=4 * pieces * slots * width * wide,
            bytes_accessed=2 * (pieces * slots * (width + 2 * wide) + 2 * width * wide),
            transcendentals=0,
        ),
        name="shard_grad",
    )(*lefts, *rights)
    return out.reshape(2 * rows, block, wide)


def tokens_move(
    hidden_in,
    segments,
    routes,
    attention_gain,
    query_weight,
    key_matrix,
    value_matrix,
    output_weight,
    expert_gain,
    router_weight,
    gate_weight,
    up_weight,
    down_weight,
    cotangent,
):
    bf16, f32 = jnp.bfloat16, jnp.float32
    core, row = lax.axis_index("col"), lax.axis_index("row")
    level, place = row // PLANE, row % PLANE
    local = hidden_in.shape[0]
    span = segments.shape[1]
    row_block = query_weight.shape[0]
    rows = MODEL_WIDTH // row_block
    hidden_block = gate_weight.shape[2]
    ffe = 2 * hidden_block
    capacity = max(2, 3 * span * TOPK // (2 * E))
    share = capacity // 2
    head_cols = query_weight.shape[1]
    kv_cols = key_matrix.shape[1]
    heads = head_cols // HEAD_SIZE
    mates = 2 * PLANE
    my_expert = row * 2 + core
    relative = [(place * 2 + core) ^ (2 * m + k) for k in range(2) for m in range(PLANE)]
    nt = (((1,), (1,)), ((), ()))
    tn = (((0,), (0,)), ((), ()))

    routes_rows = span * TOPK // 64
    routes_own = routes.T.astype(bf16).reshape(routes_rows, 64)
    routes_own = jnp.pad(routes_own, ((0, row_block - routes_rows), (0, 0)))
    packed = jnp.concatenate(
        [
            query_weight,
            key_matrix,
            value_matrix,
            output_weight.T,
            router_weight,
            attention_gain[:, None],
            expert_gain[:, None],
            routes_own,
            jnp.zeros((row_block, 126 - E - routes_own.shape[1]), bf16),
        ],
        axis=1,
    )
    packed_line = jnp.stack([packed] + [line_shift(packed, step) for step in range(1, LINE)])
    o0 = head_cols + 2 * kv_cols
    first = o0 + head_cols + E + 2
    routes_line = packed_line[:, :routes_rows, first : first + 64].reshape(LINE, TOPK, span)
    routes_line = reorder(routes_line, [(level - z) % LINE for z in range(LINE)], 0)
    routes_line = routes_line.astype(jnp.int32)
    packed_full = row_gather(packed_line, level, place)
    qkv_cols, out_full = packed_full[:, :o0], packed_full[:, o0:]
    output_t = out_full[:, :head_cols]
    router_full = out_full[:, head_cols : head_cols + E]
    gain_first = out_full[:, head_cols + E].astype(f32)
    gain_second = out_full[:, head_cols + E + 1].astype(f32)

    expert_ids = jnp.arange(E, dtype=jnp.int32)
    slot_near, slot_there, masks = [], [], []
    for i in range(LINE):
        named, counts = slot_ranks(routes_line[i].T)
        slot_of = jnp.where(named, counts - core * share, -1).T
        slot_of = lax.dynamic_slice_in_dim(own_first(slot_of, core, 1), level * mates, mates)
        slot_there.append(slot_of)
        slot_near.append(reorder(slot_of, relative, 0))
        masks.append(own_first(jnp.pad(named.astype(bf16), ((0, 0), (0, 128 - E))), core, 0))
    slot_near, slot_there, mask_line = [jnp.stack(t) for t in (slot_near, slot_there, masks)]

    slots = LINE * share * mates

    nil = packed_line[1, 0, 0] * 0
    weights = jnp.concatenate(
        [gate_weight, up_weight, down_weight.transpose(0, 2, 1) + nil], axis=2
    )
    weights = exchange(after(weights, packed_line))
    cot_line = line_gather(after(cotangent, packed_line))

    hidden_all = both_cores(hidden_in)
    tokens_all = hidden_all.astype(f32)
    scale_all = lax.rsqrt(jnp.mean(tokens_all * tokens_all, axis=-1, keepdims=True) + EPSILON)
    normed_all = (tokens_all * scale_all * gain_first).astype(bf16)
    places = own_first(positions(segments[0]), core, 0)
    segment_ids = own_first(segments[0], core, 0)
    token_index = own_first(jnp.arange(span, dtype=jnp.int32), core, 0)
    allowed = (segment_ids[:, None] == segment_ids[None, :]) & (
        token_index[None, :] <= token_index[:, None]
    )
    raw = jnp.dot(normed_all, qkv_cols, preferred_element_type=f32)
    queries = apply_rotary(raw[:, :head_cols].reshape(span, heads, HEAD_SIZE), places, 1.0)
    queries = queries.astype(bf16).transpose(1, 0, 2)
    keys = apply_rotary(
        raw[:, head_cols : head_cols + kv_cols].reshape(span, 1, HEAD_SIZE), places, 1.0
    ).astype(bf16)[:, 0]
    values = raw[:, head_cols + kv_cols :].astype(bf16)
    scaling = HEAD_SIZE ** (-0.5)
    attended, log_total = attend_group((queries, keys, values), allowed, scaling)
    attended_low = attended.transpose(1, 0, 2).reshape(span, head_cols).astype(bf16)
    branch_part = lax.dot_general(attended_low, output_t, nt, preferred_element_type=f32)
    tokens_in = hidden_in.astype(f32)
    hidden_mid = tokens_in + sum_cores(branch_part, f32)
    scale_second = lax.rsqrt(jnp.mean(hidden_mid * hidden_mid, axis=-1, keepdims=True) + EPSILON)
    unit_second = hidden_mid * scale_second
    normed_second = (unit_second * gain_second).astype(bf16)

    cot_line = after(cot_line, normed_second)
    cot_swap = swap_cores(cot_line)
    cot_rows = select_rows(slot_there, cot_line, cot_swap, share, mask_line)
    normed_line = line_gather(after(normed_second, weights, cot_rows))
    cot_rows = plane_all(cot_rows.reshape(mates, LINE, share, MODEL_WIDTH + 128))
    normed_swap = swap_cores(normed_line)
    normed_rows = select_rows(slot_near, after(normed_line, cot_rows), normed_swap, share)
    pieces = plane_exchange(normed_rows)

    pieces = [p.reshape(2 * LINE * share, MODEL_WIDTH) for p in pieces]
    cot_rows = cot_rows.reshape(PLANE, 2, LINE * share, MODEL_WIDTH + 128)
    weights = weights.reshape(rows, 2, row_block, 3 * hidden_block)
    done, mixture, back = [], None, []
    for move in range(PLANE):
        if move == 3:
            pieces[3] = after(pieces[3], back[1])
        found = expert_rows(
            move, place, core, my_expert, pieces[move], cot_rows, weights, out_full[:, head_cols:], mixture
        )
        mixture = found[1]
        done.append(found)
        back.append(plane_move(found[0], move) if move else found[0])
    _, _, grad_expert, activation, grad_gate, grad_up, grad_logits = [
        list(a) for a in zip(*done)
    ]

    def combine(table, near, far, far_block=0):
        kept, away = combine_rows(table, near, far, far_block)
        return (kept.astype(f32) + swap_cores(away).astype(f32)).astype(bf16)

    shape = (2, LINE, share, MODEL_WIDTH)
    back = [b.reshape(shape) for b in back]
    grad_expert[3] = after(grad_expert[3], back[2])
    down_home = exchange(after(shard_grad(grad_expert, activation, rows), back[3]))
    far = swap_cores(after(jnp.stack([b[1] for b in back]), down_home))
    grad_parts = combine(slot_near, jnp.stack([b[0] for b in back]), far)
    grad_normed = line_reduce(grad_parts).astype(f32)
    router_grad = sum(
        lax.dot_general(g, p, tn, preferred_element_type=f32) for g, p in zip(grad_logits, pieces)
    )
    router_grad = router_grad[:E].T
    mixture = mixture.reshape(mates, LINE, share, MODEL_WIDTH)
    mixture = plane_all(after(mixture, down_home))
    mixture_there = after(mixture, grad_parts)
    mixture_parts = combine(slot_there, mixture_there, mixture_there, 1)
    mixture_own = line_reduce(mixture_parts).astype(f32)
    gate_up_home = shard_grad(pieces, grad_gate + grad_up, rows)
    gate_up_home = exchange(after(gate_up_home, mixture))

    grad_normed = after(grad_normed, mixture_parts)
    tilted = grad_normed * gain_second
    gain_second_grad = jnp.sum(grad_normed * unit_second, axis=0)
    grad_hidden = cotangent.astype(f32) + scale_second * (
        tilted - unit_second * jnp.mean(tilted * unit_second, axis=-1, keepdims=True)
    )
    branch_all = both_cores(grad_hidden.astype(bf16))

    output_t_grad = lax.dot_general(branch_all, attended_low, tn, preferred_element_type=f32)
    grad_attended = jnp.dot(branch_all, output_t, preferred_element_type=f32).astype(bf16)
    grad_attended = grad_attended.reshape(span, heads, HEAD_SIZE).transpose(1, 0, 2)
    grad_queries, grad_keys, grad_values = attend_back(
        (queries, keys, values, log_total, grad_attended), allowed, scaling
    )
    grad_query_low = (
        apply_rotary(grad_queries.transpose(1, 0, 2), places, -1.0)
        .reshape(span, head_cols)
        .astype(bf16)
    )
    grad_key_low = apply_rotary(grad_keys[:, None], places, -1.0)[:, 0].astype(bf16)
    grad_qkv = jnp.concatenate([grad_query_low, grad_key_low, grad_values.astype(bf16)], axis=1)
    qkv_grad = lax.dot_general(normed_all, grad_qkv, tn, preferred_element_type=f32)
    first_part = lax.dot_general(grad_qkv, qkv_cols, nt, preferred_element_type=f32)
    unit_all = tokens_all * scale_all
    gain_first_grad = jnp.sum(first_part * unit_all, axis=0)
    grad_first = sum_cores(first_part, f32)
    unit_first = tokens_in * scale_all[:local]
    tilted_first = grad_first * gain_first
    input_grad = grad_hidden + scale_all[:local] * (
        tilted_first - unit_first * jnp.mean(tilted_first * unit_first, axis=-1, keepdims=True)
    )
    block_out = (hidden_mid + mixture_own).astype(bf16)

    extra = jnp.concatenate(
        [
            router_grad,
            gain_second_grad[:, None],
            gain_first_grad[:, None],
            jnp.zeros((MODEL_WIDTH, 128 - E - 2), f32),
        ],
        axis=1,
    )
    owned, marks = row_reduce(
        [jnp.concatenate([output_t_grad, extra], axis=1), qkv_grad], level, place
    )
    output_own, qkv_own = owned[:, :head_cols], owned[:, head_cols + 128 :]
    small_own = owned[:, head_cols : head_cols + 128]
    small_own = small_own + swap_cores(small_own)
    gate_up_home = after(gate_up_home, *marks)
    return (
        block_out,
        input_grad,
        small_own[:, E + 1],
        qkv_own[:, :head_cols],
        qkv_own[:, head_cols : head_cols + kv_cols],
        qkv_own[:, head_cols + kv_cols :],
        output_own[:, :head_cols].T,
        small_own[:, E],
        small_own[:, :E],
        gate_up_home[:, :, :hidden_block].astype(f32),
        gate_up_home[:, :, hidden_block:].astype(f32),
        down_home.astype(f32).transpose(0, 2, 1),
    )


def solution(mesh):
    in_specs = (
        P(("row", "col"), None),
        P("row", None),
        P("row", None),
        P("row"),
        P("row", "col"),
        P("row", "col"),
        P("row", "col"),
        P("col", "row"),
        P("row"),
        P("row", None),
        P(None, "row", "col"),
        P(None, "row", "col"),
        P(None, "col", "row"),
        P(("row", "col"), None),
    )
    out_specs = (
        P(("row", "col"), None),
        P(("row", "col"), None),
        P("row"),
        P("row", "col"),
        P("row", "col"),
        P("row", "col"),
        P("col", "row"),
        P("row"),
        P("row", None),
        P(None, "row", "col"),
        P(None, "row", "col"),
        P(None, "col", "row"),
    )
    rows, cols = mesh.shape["row"], mesh.shape["col"]
    one_each = rows == 4 * PLANE and cols == KEY_VALUE_HEADS and rows * cols == E
    return jax.shard_map(
        tokens_move if one_each else weights_move, mesh=mesh,
        in_specs=in_specs,
        out_specs=out_specs,
        check_vma=False,
    )
```

```python
import jax
import jax.numpy as jnp
from jax import lax
from jax.experimental import pallas as pl
from jax.experimental.pallas import tpu as pltpu
from jax.sharding import PartitionSpec as P

MODEL_WIDTH = 1536
QUERY_HEADS = 12
KEY_VALUE_HEADS = 2
HEAD_SIZE = 128
E = 32
TOPK = 4


EPSILON = 1e-06
ROPE_BASE = 1000000.0
MASKED = -1e30


def positions(segment_ids):
    total_length = segment_ids.shape[0]
    token_index = jnp.arange(total_length, dtype=jnp.int32)
    earlier = (segment_ids[:, None] == segment_ids[None, :]) & (
        token_index[None, :] < token_index[:, None]
    )
    return jnp.sum(earlier.astype(jnp.int32), axis=1)


def apply_rotary(values, places, direction):
    half_size = values.shape[-1] // 2
    frequency = ROPE_BASE ** (-2.0 * jnp.arange(half_size, dtype=jnp.float32) / values.shape[-1])
    angles = places.astype(jnp.float32)[:, None] * frequency[None, :]
    cosine_part = jnp.cos(angles)[:, None, :]
    sine_part = direction * jnp.sin(angles)[:, None, :]
    first_half = values[..., :half_size]
    second_half = values[..., half_size:]
    return jnp.concatenate(
        [
            first_half * cosine_part - second_half * sine_part,
            second_half * cosine_part + first_half * sine_part,
        ],
        axis=-1,
    )


def slot_ranks(route_ids):
    total_length = route_ids.shape[0]
    token_index = jnp.arange(total_length, dtype=jnp.int32)
    expert_ids = jnp.arange(E, dtype=jnp.int32)
    named = jnp.any(route_ids[:, :, None] == expert_ids[None, None, :], axis=1)
    before = (token_index[None, :] < token_index[:, None]).astype(jnp.bfloat16)
    counts = jnp.dot(before, named.astype(jnp.bfloat16), preferred_element_type=jnp.float32)
    return (named, counts.astype(jnp.int32))


def slot_tables(route_ids, experts, capacity):
    flat_ids = route_ids.reshape(-1)
    named, counts = slot_ranks(route_ids)
    rank_ids = jnp.sum(
        jnp.where(
            route_ids[:, :, None] == jnp.arange(experts, dtype=jnp.int32)[None, None, :],
            counts[:, None, :],
            0,
        ),
        axis=-1,
    ).reshape(-1)
    pair_slot = flat_ids * capacity + rank_ids
    owners = jnp.arange(flat_ids.shape[0], dtype=jnp.int32) // route_ids.shape[1]
    token_of = jnp.zeros((experts * capacity,), jnp.int32).at[pair_slot].set(owners)
    filled = jnp.zeros((experts * capacity,), jnp.int32).at[pair_slot].set(1)
    return (pair_slot, token_of, filled)


def masked_scores(queries, key_row_block, allowed, scaling):
    scores = (
        jnp.einsum("gqd,kd->gqk", queries, key_row_block, preferred_element_type=jnp.float32)
        * scaling
    )
    return jnp.where(allowed[None], scores, MASKED)


def attend_group(operands, allowed, scaling):
    queries, key_row_block, value_row_block = operands
    scores = masked_scores(queries, key_row_block, allowed, scaling)
    highest = jnp.max(scores, axis=-1, keepdims=True)
    exponent = jnp.exp(scores - highest)
    summed = jnp.sum(exponent, axis=-1, keepdims=True)
    weights_low = (exponent / summed).astype(jnp.bfloat16)
    result = jnp.einsum(
        "gqk,kd->gqd", weights_low, value_row_block, preferred_element_type=jnp.float32
    )
    return (result, highest + jnp.log(summed))


def attend_back(operands, allowed, scaling):
    queries, key_row_block, value_row_block, log_total, grad_result = operands
    scores = masked_scores(queries, key_row_block, allowed, scaling)
    weights_full = jnp.where(allowed[None], jnp.exp(scores - log_total), 0.0)
    weights_low = weights_full.astype(jnp.bfloat16)
    grad_values = jnp.einsum(
        "gqk,gqd->kd", weights_low, grad_result, preferred_element_type=jnp.float32
    )
    grad_weights = jnp.einsum(
        "gqd,kd->gqk", grad_result, value_row_block, preferred_element_type=jnp.float32
    )
    centre = jnp.sum(weights_full * grad_weights, axis=-1, keepdims=True)
    grad_scores = (weights_full * (grad_weights - centre)).astype(jnp.bfloat16)
    grad_queries = (
        jnp.einsum("gqk,kd->gqd", grad_scores, key_row_block, preferred_element_type=jnp.float32)
        * scaling
    )
    grad_keys = (
        jnp.einsum("gqk,gqd->kd", grad_scores, queries, preferred_element_type=jnp.float32)
        * scaling
    )
    return (grad_queries, grad_keys, grad_values)


def weights_move(
    hidden_in,
    segments,
    routes,
    attention_gain,
    query_weight,
    key_matrix,
    value_matrix,
    output_weight,
    expert_gain,
    router_weight,
    gate_weight,
    up_weight,
    down_weight,
    cotangent,
):
    gain_first, query_cols, key_cols, value_cols, output_rows = (
        lax.all_gather(attention_gain, "row", axis=0, tiled=True),
        lax.all_gather(query_weight, "row", axis=0, tiled=True),
        lax.all_gather(key_matrix, "row", axis=0, tiled=True),
        lax.all_gather(value_matrix, "row", axis=0, tiled=True),
        lax.all_gather(output_weight, "row", axis=1, tiled=True),
    )
    query_full, gathered_keys, gathered_values, output_full = (
        lax.all_gather(query_cols, "col", axis=1, tiled=True),
        lax.all_gather(key_cols, "col", axis=1, tiled=True),
        lax.all_gather(value_cols, "col", axis=1, tiled=True),
        lax.all_gather(output_rows, "col", axis=0, tiled=True),
    )
    gain_second, router_full, gate_full, up_full, down_full = (
        lax.all_gather(expert_gain, "row", axis=0, tiled=True),
        lax.all_gather(router_weight, "row", axis=0, tiled=True),
        lax.all_gather(gate_weight, "row", axis=1, tiled=True),
        lax.all_gather(up_weight, "row", axis=1, tiled=True),
        lax.all_gather(down_weight, "row", axis=2, tiled=True),
    )
    local_row_block = hidden_in.shape[0]
    sequence_span_length = segments.shape[1]
    first_row = lax.axis_index("col") * local_row_block
    segment_ids = segments[0]
    places_all = positions(segment_ids)
    local_positions = lax.dynamic_slice_in_dim(places_all, first_row, local_row_block)
    own_segments = lax.dynamic_slice_in_dim(segment_ids, first_row, local_row_block)
    query_index = first_row + jnp.arange(local_row_block, dtype=jnp.int32)
    key_index = jnp.arange(sequence_span_length, dtype=jnp.int32)
    allowed = (own_segments[:, None] == segment_ids[None, :]) & (
        key_index[None, :] <= query_index[:, None]
    )
    tokens_in = hidden_in.astype(jnp.float32)
    scale_first = lax.rsqrt(jnp.mean(tokens_in * tokens_in, axis=-1, keepdims=True) + EPSILON)
    unit_first = tokens_in * scale_first
    normed_first = (unit_first * gain_first.astype(jnp.float32)).astype(jnp.bfloat16)
    query_raw = jnp.dot(normed_first, query_full, preferred_element_type=jnp.float32).reshape(
        local_row_block, QUERY_HEADS, HEAD_SIZE
    )
    unrotated_keys = jnp.dot(
        normed_first, gathered_keys, preferred_element_type=jnp.float32
    ).reshape(local_row_block, KEY_VALUE_HEADS, HEAD_SIZE)
    values_reduced = jnp.dot(
        normed_first, gathered_values, preferred_element_type=jnp.float32
    ).astype(jnp.bfloat16)
    rotated_queries = apply_rotary(query_raw, local_positions, 1.0).astype(jnp.bfloat16)
    rotated_keys = (
        apply_rotary(unrotated_keys, local_positions, 1.0)
        .astype(jnp.bfloat16)
        .reshape(local_row_block, KEY_VALUE_HEADS * HEAD_SIZE)
    )
    key_row_block, value_row_block = (
        lax.all_gather(rotated_keys, "col", axis=0, tiled=True),
        lax.all_gather(values_reduced, "col", axis=0, tiled=True),
    )
    heads_per_group = QUERY_HEADS // KEY_VALUE_HEADS
    scaling = HEAD_SIZE ** (-0.5)
    grouped_queries = rotated_queries.reshape(
        local_row_block, KEY_VALUE_HEADS, heads_per_group, HEAD_SIZE
    ).transpose(1, 2, 0, 3)
    grouped_keys = key_row_block.reshape(
        sequence_span_length, KEY_VALUE_HEADS, HEAD_SIZE
    ).transpose(1, 0, 2)
    grouped_values = value_row_block.reshape(
        sequence_span_length, KEY_VALUE_HEADS, HEAD_SIZE
    ).transpose(1, 0, 2)
    attended, log_total = lax.map(
        lambda operands: attend_group(operands, allowed, scaling),
        (grouped_queries, grouped_keys, grouped_values),
    )
    attended_low = (
        attended.transpose(2, 0, 1, 3)
        .reshape(local_row_block, QUERY_HEADS * HEAD_SIZE)
        .astype(jnp.bfloat16)
    )
    branch = jnp.dot(attended_low, output_full, preferred_element_type=jnp.float32)
    hidden_mid = tokens_in + branch
    scale_second = lax.rsqrt(jnp.mean(hidden_mid * hidden_mid, axis=-1, keepdims=True) + EPSILON)
    unit_second = hidden_mid * scale_second
    normed_second = (unit_second * gain_second.astype(jnp.float32)).astype(jnp.bfloat16)
    normed_all, upstream_all = (
        lax.all_gather(normed_second, "col", axis=0, tiled=True),
        lax.all_gather(cotangent, "col", axis=0, tiled=True),
    )
    logits = jnp.dot(normed_all, router_full, preferred_element_type=jnp.float32)
    expert_ids = jnp.arange(E, dtype=jnp.int32)
    chosen_mask = routes[:, :, None] == expert_ids[None, None, :]
    chosen = jnp.sum(jnp.where(chosen_mask, logits[:, None, :], 0.0), axis=-1)
    exponent = jnp.exp(chosen - jnp.max(chosen, axis=-1, keepdims=True))
    route_gates = exponent / jnp.sum(exponent, axis=-1, keepdims=True)
    group_width = 4
    capacity = max(2, 3 * sequence_span_length * TOPK // (2 * E))
    pair_slot, token_of, filled = slot_tables(routes, E, capacity)
    slot_gate = jnp.zeros((E * capacity,), jnp.float32).at[pair_slot].set(route_gates.reshape(-1))
    group_rows = group_width * capacity

    def expert_step(accumulated, group_index):
        mixture_sum, input_sum = accumulated
        offset = group_index * group_rows
        row_ids = lax.dynamic_slice_in_dim(token_of, offset, group_rows)
        occupied = lax.dynamic_slice_in_dim(filled, offset, group_rows) > 0
        slot_weight = lax.dynamic_slice_in_dim(slot_gate, offset, group_rows)
        first_expert = group_index * group_width
        gate_block = lax.dynamic_slice_in_dim(gate_full, first_expert, group_width, 0)
        up_block = lax.dynamic_slice_in_dim(up_full, first_expert, group_width, 0)
        down_block = lax.dynamic_slice_in_dim(down_full, first_expert, group_width, 0)
        inputs = jnp.where(
            occupied[:, None], normed_all[row_ids], jnp.zeros((), jnp.bfloat16)
        ).reshape(group_width, capacity, MODEL_WIDTH)
        upstream = upstream_all[row_ids].astype(jnp.float32)
        gate_value = jnp.einsum(
            "ecd,edf->ecf", inputs, gate_block, preferred_element_type=jnp.float32
        )
        up_value = jnp.einsum("ecd,edf->ecf", inputs, up_block, preferred_element_type=jnp.float32)
        sigmoid_gate = jax.nn.sigmoid(gate_value)
        silu_gate = gate_value * sigmoid_gate
        activation = (silu_gate * up_value).astype(jnp.bfloat16)
        partial_out = jnp.einsum(
            "ecf,efd->ecd", activation, down_block, preferred_element_type=jnp.float32
        ).reshape(group_rows, MODEL_WIDTH)
        mixture_sum = mixture_sum.at[row_ids].add(partial_out * slot_weight[:, None])
        slot_grad = jnp.sum(partial_out * upstream, axis=-1)
        grad_expert = (
            (upstream * slot_weight[:, None])
            .astype(jnp.bfloat16)
            .reshape(group_width, capacity, MODEL_WIDTH)
        )
        grad_act = jnp.einsum(
            "ecd,efd->ecf", grad_expert, down_block, preferred_element_type=jnp.float32
        )
        slope = sigmoid_gate * (1.0 + gate_value * (1.0 - sigmoid_gate))
        grad_gate = (grad_act * up_value * slope).astype(jnp.bfloat16)
        grad_up = (grad_act * silu_gate).astype(jnp.bfloat16)
        grad_inputs = jnp.einsum(
            "ecf,edf->ecd", grad_gate, gate_block, preferred_element_type=jnp.float32
        )
        grad_inputs = grad_inputs + jnp.einsum(
            "ecf,edf->ecd", grad_up, up_block, preferred_element_type=jnp.float32
        )
        input_sum = input_sum.at[row_ids].add(grad_inputs.reshape(group_rows, MODEL_WIDTH))
        gate_piece = jnp.einsum(
            "ecd,ecf->edf", inputs, grad_gate, preferred_element_type=jnp.float32
        )
        up_piece = jnp.einsum("ecd,ecf->edf", inputs, grad_up, preferred_element_type=jnp.float32)
        down_piece = jnp.einsum(
            "ecf,ecd->efd", activation, grad_expert, preferred_element_type=jnp.float32
        )
        return ((mixture_sum, input_sum), (slot_grad, gate_piece, up_piece, down_piece))

    initial = (
        jnp.zeros((sequence_span_length, MODEL_WIDTH), jnp.float32),
        jnp.zeros((sequence_span_length, MODEL_WIDTH), jnp.float32),
    )
    sums_out, pieces = lax.scan(expert_step, initial, jnp.arange(E // group_width, dtype=jnp.int32))
    mixture_part, input_part = sums_out
    slot_grads, gate_pieces, up_pieces, down_pieces = pieces
    hidden_cols = gate_full.shape[2]
    gate_grad = gate_pieces.reshape(E, MODEL_WIDTH, hidden_cols)
    up_grad = up_pieces.reshape(E, MODEL_WIDTH, hidden_cols)
    down_grad = down_pieces.reshape(E, hidden_cols, MODEL_WIDTH)
    pick_grads = slot_grads.reshape(-1)[pair_slot].reshape(sequence_span_length, TOPK)
    mixture_own, input_own, pick_own = (
        lax.psum_scatter(mixture_part, "col", scatter_dimension=0, tiled=True),
        lax.psum_scatter(input_part, "col", scatter_dimension=0, tiled=True),
        lax.psum_scatter(pick_grads, "col", scatter_dimension=0, tiled=True),
    )
    block_out = (hidden_mid + mixture_own).astype(jnp.bfloat16)
    own_gates = lax.dynamic_slice_in_dim(route_gates, first_row, local_row_block)
    own_mask = lax.dynamic_slice_in_dim(chosen_mask, first_row, local_row_block)
    centred = own_gates * (pick_own - jnp.sum(own_gates * pick_own, axis=-1, keepdims=True))
    grad_logits = jnp.sum(jnp.where(own_mask, centred[:, :, None], 0.0), axis=1).astype(
        jnp.bfloat16
    )
    grad_normed = input_own + jnp.dot(
        grad_logits, router_full.T, preferred_element_type=jnp.float32
    )
    router_grad = jnp.dot(normed_second.T, grad_logits, preferred_element_type=jnp.float32)
    tilted_second = grad_normed * gain_second.astype(jnp.float32)
    gain_second_grad = jnp.sum(grad_normed * unit_second, axis=0)
    grad_hidden = cotangent.astype(jnp.float32) + scale_second * (
        tilted_second - unit_second * jnp.mean(tilted_second * unit_second, axis=-1, keepdims=True)
    )
    grad_branch = grad_hidden.astype(jnp.bfloat16)
    output_grad = jnp.dot(attended_low.T, grad_branch, preferred_element_type=jnp.float32)
    attended_gradient = jnp.dot(
        grad_branch, output_full.T, preferred_element_type=jnp.float32
    ).astype(jnp.bfloat16)
    grouped_gradient = attended_gradient.reshape(
        local_row_block, KEY_VALUE_HEADS, heads_per_group, HEAD_SIZE
    ).transpose(1, 2, 0, 3)
    grad_query_groups, key_gradient_grouped, value_gradient_grouped = lax.map(
        lambda operands: attend_back(operands, allowed, scaling),
        (grouped_queries, grouped_keys, grouped_values, log_total, grouped_gradient),
    )
    grad_query_rot = grad_query_groups.transpose(2, 0, 1, 3).reshape(
        local_row_block, QUERY_HEADS, HEAD_SIZE
    )
    key_gradient_total = key_gradient_grouped.transpose(1, 0, 2).reshape(
        sequence_span_length, KEY_VALUE_HEADS * HEAD_SIZE
    )
    value_gradient_total = value_gradient_grouped.transpose(1, 0, 2).reshape(
        sequence_span_length, KEY_VALUE_HEADS * HEAD_SIZE
    )
    local_keys, value_own = (
        lax.psum_scatter(
            key_gradient_total.astype(jnp.bfloat16), "col", scatter_dimension=0, tiled=True
        ).astype(jnp.float32),
        lax.psum_scatter(
            value_gradient_total.astype(jnp.bfloat16), "col", scatter_dimension=0, tiled=True
        ).astype(jnp.float32),
    )
    grad_query_low = (
        apply_rotary(grad_query_rot, local_positions, -1.0)
        .reshape(local_row_block, QUERY_HEADS * HEAD_SIZE)
        .astype(jnp.bfloat16)
    )
    grad_key_low = (
        apply_rotary(
            local_keys.reshape(local_row_block, KEY_VALUE_HEADS, HEAD_SIZE), local_positions, -1.0
        )
        .reshape(local_row_block, KEY_VALUE_HEADS * HEAD_SIZE)
        .astype(jnp.bfloat16)
    )
    grad_value_low = value_own.astype(jnp.bfloat16)
    grad_normed_first = jnp.dot(grad_query_low, query_full.T, preferred_element_type=jnp.float32)
    grad_normed_first = grad_normed_first + jnp.dot(
        grad_key_low, gathered_keys.T, preferred_element_type=jnp.float32
    )
    grad_normed_first = grad_normed_first + jnp.dot(
        grad_value_low, gathered_values.T, preferred_element_type=jnp.float32
    )
    query_grad = jnp.dot(normed_first.T, grad_query_low, preferred_element_type=jnp.float32)
    key_grad = jnp.dot(normed_first.T, grad_key_low, preferred_element_type=jnp.float32)
    value_grad = jnp.dot(normed_first.T, grad_value_low, preferred_element_type=jnp.float32)
    tilted_first = grad_normed_first * gain_first.astype(jnp.float32)
    gain_first_grad = jnp.sum(grad_normed_first * unit_first, axis=0)
    input_grad = grad_hidden + scale_first * (
        tilted_first - unit_first * jnp.mean(tilted_first * unit_first, axis=-1, keepdims=True)
    )
    query_part, key_part, value_part, output_part = (
        lax.psum_scatter(
            query_grad.astype(jnp.bfloat16), "col", scatter_dimension=1, tiled=True
        ).astype(jnp.float32),
        lax.psum_scatter(
            key_grad.astype(jnp.bfloat16), "col", scatter_dimension=1, tiled=True
        ).astype(jnp.float32),
        lax.psum_scatter(
            value_grad.astype(jnp.bfloat16), "col", scatter_dimension=1, tiled=True
        ).astype(jnp.float32),
        lax.psum_scatter(
            output_grad.astype(jnp.bfloat16), "col", scatter_dimension=0, tiled=True
        ).astype(jnp.float32),
    )
    small_total = lax.psum((gain_first_grad, gain_second_grad, router_grad), ("row", "col"))
    query_out, key_out, value_out, output_out, gate_out, up_out, down_out = (
        lax.psum_scatter(
            query_part.astype(jnp.bfloat16), "row", scatter_dimension=0, tiled=True
        ).astype(jnp.float32),
        lax.psum_scatter(
            key_part.astype(jnp.bfloat16), "row", scatter_dimension=0, tiled=True
        ).astype(jnp.float32),
        lax.psum_scatter(
            value_part.astype(jnp.bfloat16), "row", scatter_dimension=0, tiled=True
        ).astype(jnp.float32),
        lax.psum_scatter(
            output_part.astype(jnp.bfloat16), "row", scatter_dimension=1, tiled=True
        ).astype(jnp.float32),
        lax.psum_scatter(
            gate_grad.astype(jnp.bfloat16), "row", scatter_dimension=1, tiled=True
        ).astype(jnp.float32),
        lax.psum_scatter(
            up_grad.astype(jnp.bfloat16), "row", scatter_dimension=1, tiled=True
        ).astype(jnp.float32),
        lax.psum_scatter(
            down_grad.astype(jnp.bfloat16), "row", scatter_dimension=2, tiled=True
        ).astype(jnp.float32),
    )
    row_block = attention_gain.shape[0]
    row_start = lax.axis_index("row") * row_block
    gain_first_out = lax.dynamic_slice_in_dim(small_total[0], row_start, row_block)
    gain_second_out = lax.dynamic_slice_in_dim(small_total[1], row_start, row_block)
    router_out = lax.dynamic_slice_in_dim(small_total[2], row_start, row_block, 0)
    return (
        block_out,
        input_grad,
        gain_first_out,
        query_out,
        key_out,
        value_out,
        output_out,
        gain_second_out,
        router_out,
        gate_out,
        up_out,
        down_out,
    )


GRID = ("row", "col")
PLANE = 4
LINE = 4


def nothing(*refs):
    pass


def after(block, *others):
    anywhere = pl.BlockSpec(memory_space=pl.ANY)
    return pl.pallas_call(
        nothing,
        out_shape=jax.ShapeDtypeStruct(block.shape, block.dtype),
        in_specs=[anywhere] * (1 + len(others)),
        out_specs=anywhere,
        input_output_aliases={0: 0},
        name="after",
    )(block, *others)


def swap_cores(block):
    return lax.ppermute(block, "col", [(0, 1), (1, 0)])


def both_cores(own):
    return jnp.concatenate([own, swap_cores(own)], axis=0)


def sum_cores(partial, kind):
    half = partial.shape[0] // 2
    away = partial[half:].astype(kind)
    return partial[:half] + swap_cores(away).astype(partial.dtype)


def own_first(table, core, axis):
    half = table.shape[axis] // 2
    mine = lax.dynamic_slice_in_dim(table, core * half, half, axis)
    theirs = lax.dynamic_slice_in_dim(table, (1 - core) * half, half, axis)
    return jnp.concatenate([mine, theirs], axis=axis)


def exchange(block):
    return lax.all_to_all(block, GRID, split_axis=0, concat_axis=0, tiled=True)


LINES = [[z * PLANE + p for z in range(LINE)] for p in range(PLANE)]


def line_shift(block, step):
    pairs = [
        (s * PLANE + p, (s + step) % LINE * PLANE + p) for s in range(LINE) for p in range(PLANE)
    ]
    return lax.ppermute(block, "row", pairs)


def plane_pairs(flip):
    return [(r, r ^ flip) for r in range(PLANE * LINE)]


def reorder(block, order, axis):
    picked = [lax.dynamic_index_in_dim(block, i, axis, True) for i in order]
    return jnp.concatenate(picked, axis=axis)


def row_gather(line, level, place):
    moved = [lax.ppermute(line, "row", plane_pairs(flip)) for flip in range(1, PLANE)]
    whole = jnp.concatenate([line, *moved], axis=0)
    order = [(place ^ p) * LINE + (level - z) % LINE for z in range(LINE) for p in range(PLANE)]
    return reorder(whole, order, 0).reshape(LINE * PLANE * line.shape[1], line.shape[2])


def row_reduce(halves, level, place):
    block = halves[0].shape[0] // (LINE * PLANE)
    halves = [h.reshape(LINE, 2, 2, block, h.shape[1]) for h in halves]
    marks = []
    for flips in ((1, 2), (2, 1)):
        for i, flip in enumerate(flips):
            axis = min(3 - flip, halves[i].ndim - 3)
            bit = (place // flip) % 2
            kept = lax.dynamic_index_in_dim(halves[i], bit, axis, False)
            away = lax.dynamic_index_in_dim(halves[i], 1 - bit, axis, False)
            away = lax.ppermute(away.astype(jnp.bfloat16), "row", plane_pairs(flip))
            halves[i] = kept + away.astype(jnp.float32)
            marks.append(halves[i])
    order = [(level + step) % LINE for step in range(LINE)]
    parts = [
        jnp.concatenate([lax.dynamic_index_in_dim(h, i, 0, False) for h in halves], axis=1)
        for i in order
    ]
    moved = [line_shift(parts[step].astype(jnp.bfloat16), step) for step in range(1, LINE)]
    total = parts[0]
    for part in moved:
        total = total + part.astype(jnp.float32)
    return total, marks[2:]


def line_gather(block):
    whole = lax.all_gather(block, "row", axis=0, tiled=False, axis_index_groups=LINES)
    return whole


def line_reduce(parts):
    return lax.psum_scatter(
        parts, "row", scatter_dimension=0, tiled=False, axis_index_groups=LINES
    )


def plane_move(block, move):
    return lax.ppermute(block, "row", plane_pairs(move))


def plane_exchange(block):
    far = swap_cores(block[1])
    pairs = [jnp.stack([block[0, m], far[m]]) for m in range(PLANE)]
    moved = {m: plane_move(pairs[m], m) for m in (1, 2, 3)}
    return [pairs[0], moved[1], moved[2], moved[3]]


def plane_all(block):
    groups = [[z * 2 * PLANE + d for d in range(2 * PLANE)] for z in range(LINE)]
    return lax.all_to_all(
        block, GRID, split_axis=0, concat_axis=0, tiled=True, axis_index_groups=groups
    )


def expert_body(
    where_ref,
    x_ref,
    cot_ref,
    weights_ref,
    router_ref,
    _,
    grad_in_ref,
    mix_ref,
    grad_expert_ref,
    act_ref,
    grad_gate_ref,
    grad_up_ref,
    grad_logits_ref,
):
    bf16, f32 = jnp.bfloat16, jnp.float32
    core, expert = where_ref[1], where_ref[2]
    nt = (((1,), (1,)), ((), ()))
    width = x_ref.shape[1]
    x = x_ref[...]
    half = x.shape[0] // 2
    there = jnp.concatenate([cot_ref[0, core], cot_ref[0, 1 - core]], axis=0)
    mask = there[:, width:].astype(f32) > 0
    upstream = there[:, :width].astype(f32)
    router = router_ref[...]
    logits = jnp.dot(x, router, preferred_element_type=f32)
    top = jnp.max(jnp.where(mask, logits, MASKED), axis=-1, keepdims=True)
    exponent = jnp.where(mask, jnp.exp(logits - top), 0.0)
    gates = exponent / jnp.maximum(jnp.sum(exponent, axis=-1, keepdims=True), 1e-30)
    mine = lax.broadcasted_iota(jnp.int32, gates.shape, 1) == expert
    slot_gate = jnp.sum(jnp.where(mine, gates, 0.0), axis=-1, keepdims=True)
    grad_expert = (upstream * slot_gate).astype(bf16)
    grad_expert_ref[...] = grad_expert
    cols = weights_ref.shape[3] // 3
    parts, out = [], None
    for side in range(2):
        gate_w = weights_ref[:, side, :, :cols].reshape(width, cols)
        up_w = weights_ref[:, side, :, cols : 2 * cols].reshape(width, cols)
        down_t = weights_ref[:, side, :, 2 * cols :].reshape(width, cols)
        gate_value = jnp.dot(x, gate_w, preferred_element_type=f32)
        up_value = jnp.dot(x, up_w, preferred_element_type=f32)
        sigmoid = 1.0 / (1.0 + jnp.exp(-gate_value))
        silu = gate_value * sigmoid
        act = (silu * up_value).astype(bf16)
        part = lax.dot_general(act, down_t, nt, preferred_element_type=f32)
        out = part if out is None else out + part
        grad_act = jnp.dot(grad_expert, down_t, preferred_element_type=f32)
        slope = sigmoid * (1.0 + gate_value * (1.0 - sigmoid))
        grad_gate = (grad_act * up_value * slope).astype(bf16)
        grad_up = (grad_act * silu).astype(bf16)
        act_ref[:, side * cols : (side + 1) * cols] = act
        grad_gate_ref[:, side * cols : (side + 1) * cols] = grad_gate
        grad_up_ref[:, side * cols : (side + 1) * cols] = grad_up
        parts.append((grad_gate, grad_up, gate_w, up_w))
    scaled = (out * slot_gate).astype(bf16)
    mix_ref[0, core] = scaled[:half]
    mix_ref[0, 1 - core] = scaled[half:]
    pick_grad = slot_gate * jnp.sum(out * upstream, axis=-1, keepdims=True)
    grad_logits = (pick_grad * (jnp.where(mine, 1.0, 0.0) - gates)).astype(bf16)
    grad_logits_ref[...] = grad_logits
    grad_in = lax.dot_general(grad_logits, router, nt, preferred_element_type=f32)
    for grad_gate, grad_up, gate_w, up_w in parts:
        grad_in += lax.dot_general(grad_gate, gate_w, nt, preferred_element_type=f32)
        grad_in += lax.dot_general(grad_up, up_w, nt, preferred_element_type=f32)
    grad_in_ref[...] = grad_in.astype(bf16)


def expert_rows(move, place, core, expert, x, cot, weights, router, mixture):
    slots, width = x.shape
    cols = weights.shape[3] // 3
    where = jnp.stack([place, core, expert]).astype(jnp.int32)

    def whole(shape):
        return pl.BlockSpec(shape, lambda i, w: (0,) * len(shape))

    outs = [width, width, width, 2 * cols, 2 * cols, 2 * cols, router.shape[1]]
    out_specs = [whole((slots, n)) for n in outs]
    out_shape = [jax.ShapeDtypeStruct((slots, n), jnp.bfloat16) for n in outs]
    mix_block = (1, 2, slots // 2, width)
    out_specs[1] = pl.BlockSpec(mix_block, lambda i, w: (w[0] ^ move, 0, 0, 0))
    out_shape[1] = jax.ShapeDtypeStruct((PLANE, *mix_block[1:]), jnp.bfloat16)
    resident = pl.BlockSpec(memory_space=pltpu.VMEM)
    first = mixture is None
    cot_spec = pl.BlockSpec((1, *cot.shape[1:]), lambda i, w: (w[0] ^ move, 0, 0, 0))
    anywhere = pl.BlockSpec(memory_space=pl.ANY)
    return pl.pallas_call(
        expert_body,
        grid_spec=pltpu.PrefetchScalarGridSpec(
            num_scalar_prefetch=1,
            grid=(1,),
            in_specs=[whole(x.shape), cot_spec, resident, resident, anywhere],
            out_specs=out_specs,
        ),
        out_shape=out_shape,
        input_output_aliases={} if first else {5: 1},
        compiler_params=pltpu.CompilerParams(vmem_limit_bytes=40 << 20),
        cost_estimate=pl.CostEstimate(
            flops=24 * slots * width * cols,
            bytes_accessed=2 * (5 * slots * width + 6 * slots * cols),
            transcendentals=slots * 2 * cols,
        ),
        name="expert_rows",
    )(where, x, cot, weights, router, x if first else mixture)


def picked(slots, share):
    ids = lax.broadcasted_iota(jnp.int32, (share, slots.shape[1]), 0)
    rows = [(slots[e : e + 1] == ids).astype(jnp.bfloat16) for e in range(slots.shape[0])]
    return jnp.concatenate(rows, axis=0)


def select_body(slots_ref, own_ref, other_ref, *rest):
    out_ref = rest[-1]
    share = out_ref.shape[3]
    pick = picked(slots_ref[0], share)
    half, width = own_ref.shape[1], own_ref.shape[2]
    rows = jnp.dot(pick[:, :half], own_ref[0], preferred_element_type=jnp.float32)
    rows += jnp.dot(pick[:, half:], other_ref[0], preferred_element_type=jnp.float32)
    out_ref[:, :, 0, :, :width] = rows.astype(jnp.bfloat16).reshape(2, PLANE, share, width)
    if len(rest) == 2:
        extra = jnp.dot(pick, rest[0][0], preferred_element_type=jnp.float32)
        extra = extra.astype(jnp.bfloat16)
        out_ref[:, :, 0, :, width:] = extra.reshape(2, PLANE, share, extra.shape[1])


def select_rows(slots, own, other, share, extra=None):
    lines, mates, span = slots.shape
    half, width = own.shape[1:]
    wide = width + (0 if extra is None else extra.shape[2])
    parts = [slots, own, other] + ([] if extra is None else [extra])

    def block(shape):
        return pl.BlockSpec((1, *shape), lambda i: (i, 0, 0))

    specs = [block((mates, span)), block((half, width)), block((half, width))]
    if extra is not None:
        specs.append(block((span, extra.shape[2])))
    return pl.pallas_call(
        select_body,
        grid=(lines,),
        in_specs=specs,
        out_specs=pl.BlockSpec((2, PLANE, 1, share, wide), lambda i: (0, 0, i, 0, 0)),
        out_shape=jax.ShapeDtypeStruct((2, PLANE, lines, share, wide), jnp.bfloat16),
        compiler_params=pltpu.CompilerParams(vmem_limit_bytes=40 << 20),
        cost_estimate=pl.CostEstimate(
            flops=2 * lines * mates * share * span * wide,
            bytes_accessed=2 * lines * (span + mates * share) * wide,
            transcendentals=0,
        ),
        name="select_rows",
    )(*parts)


def combine_body(slots_ref, near_ref, far_ref, kept_ref, away_ref):
    chips, _, share, width = near_ref.shape
    half = kept_ref.shape[1]
    pick = picked(slots_ref[0], share).T
    near = near_ref[:, 0].reshape(chips * share, width)
    far = far_ref[:, 0].reshape(chips * share, width)
    total = jnp.dot(pick, jnp.concatenate([near, far]), preferred_element_type=jnp.float32)
    kept_ref[0] = total[:half].astype(kept_ref.dtype)
    away_ref[0] = total[half:].astype(away_ref.dtype)


def combine_rows(slots, near, far, far_block=0):
    lines, mates, span = slots.shape
    chips = mates // 2
    share, width = near.shape[2:]
    part = pl.BlockSpec((1, span // 2, width), lambda i: (i, 0, 0))
    shape = (lines, span // 2, width)
    return pl.pallas_call(
        combine_body,
        grid=(lines,),
        in_specs=[
            pl.BlockSpec((1, mates, span), lambda i: (i, 0, 0)),
            pl.BlockSpec((chips, 1, share, width), lambda i: (0, i, 0, 0)),
            pl.BlockSpec((chips, 1, share, width), lambda i: (far_block, i, 0, 0)),
        ],
        out_specs=[part, part],
        out_shape=[
            jax.ShapeDtypeStruct(shape, jnp.bfloat16),
            jax.ShapeDtypeStruct(shape, jnp.bfloat16),
        ],
        compiler_params=pltpu.CompilerParams(vmem_limit_bytes=40 << 20),
        cost_estimate=pl.CostEstimate(
            flops=2 * lines * mates * share * span * width,
            bytes_accessed=2 * lines * (2 * span + mates * share) * width,
            transcendentals=0,
        ),
        name="combine_rows",
    )(slots, near, far)


def shard_body(pieces, left_refs, right_refs, out_ref):
    count, _, block, _ = out_ref.shape
    lefts = [ref[...].T for ref in left_refs]
    for i in range(len(right_refs) // pieces):
        rights = right_refs[i * pieces : (i + 1) * pieces]
        full = None
        for left, right in zip(lefts, rights):
            part = jnp.dot(left, right[...], preferred_element_type=jnp.float32)
            full = part if full is None else full + part
        full = full.astype(jnp.bfloat16)
        cols = full.shape[1] // 2
        for core in range(2):
            part = full[:, core * cols : (core + 1) * cols]
            out_ref[:, core, :, i * cols : (i + 1) * cols] = part.reshape(count, block, cols)


def shard_grad(lefts, rights, rows, count=4):
    pieces = len(lefts)
    slots, width = lefts[0].shape
    cols = rights[0].shape[1] // 2
    block = width // rows
    wide = cols * (len(rights) // pieces)

    def body(*refs):
        shard_body(pieces, refs[:pieces], refs[pieces:-1], refs[-1])

    out = pl.pallas_call(
        body,
        grid=(rows // count,),
        in_specs=[pl.BlockSpec((slots, count * block), lambda i: (0, i)) for _ in lefts]
        + [pl.BlockSpec((slots, 2 * cols), lambda i: (0, 0)) for _ in rights],
        out_specs=pl.BlockSpec((count, 2, block, wide), lambda i: (i, 0, 0, 0)),
        out_shape=jax.ShapeDtypeStruct((rows, 2, block, wide), jnp.bfloat16),
        compiler_params=pltpu.CompilerParams(vmem_limit_bytes=48 << 20),
        cost_estimate=pl.CostEstimate(
            flops=4 * pieces * slots * width * wide,
            bytes_accessed=2 * (pieces * slots * (width + 2 * wide) + 2 * width * wide),
            transcendentals=0,
        ),
        name="shard_grad",
    )(*lefts, *rights)
    return out.reshape(2 * rows, block, wide)


def tokens_move(
    hidden_in,
    segments,
    routes,
    attention_gain,
    query_weight,
    key_matrix,
    value_matrix,
    output_weight,
    expert_gain,
    router_weight,
    gate_weight,
    up_weight,
    down_weight,
    cotangent,
):
    bf16, f32 = jnp.bfloat16, jnp.float32
    core, row = lax.axis_index("col"), lax.axis_index("row")
    level, place = row // PLANE, row % PLANE
    local = hidden_in.shape[0]
    span = segments.shape[1]
    row_block = query_weight.shape[0]
    rows = MODEL_WIDTH // row_block
    hidden_block = gate_weight.shape[2]
    ffe = 2 * hidden_block
    capacity = max(2, 3 * span * TOPK // (2 * E))
    share = capacity // 2
    head_cols = query_weight.shape[1]
    kv_cols = key_matrix.shape[1]
    heads = head_cols // HEAD_SIZE
    mates = 2 * PLANE
    my_expert = row * 2 + core
    relative = [(place * 2 + core) ^ (2 * m + k) for k in range(2) for m in range(PLANE)]
    nt = (((1,), (1,)), ((), ()))
    tn = (((0,), (0,)), ((), ()))

    routes_rows = span * TOPK // 64
    routes_own = routes.T.astype(bf16).reshape(routes_rows, 64)
    routes_own = jnp.pad(routes_own, ((0, row_block - routes_rows), (0, 0)))
    packed = jnp.concatenate(
        [
            query_weight,
            key_matrix,
            value_matrix,
            output_weight.T,
            router_weight,
            attention_gain[:, None],
            expert_gain[:, None],
            routes_own,
            jnp.zeros((row_block, 126 - E - routes_own.shape[1]), bf16),
        ],
        axis=1,
    )
    packed_line = jnp.stack([packed] + [line_shift(packed, step) for step in range(1, LINE)])
    o0 = head_cols + 2 * kv_cols
    first = o0 + head_cols + E + 2
    routes_line = packed_line[:, :routes_rows, first : first + 64].reshape(LINE, TOPK, span)
    routes_line = reorder(routes_line, [(level - z) % LINE for z in range(LINE)], 0)
    routes_line = routes_line.astype(jnp.int32)
    packed_full = row_gather(packed_line, level, place)
    qkv_cols, out_full = packed_full[:, :o0], packed_full[:, o0:]
    output_t = out_full[:, :head_cols]
    router_full = out_full[:, head_cols : head_cols + E]
    gain_first = out_full[:, head_cols + E].astype(f32)
    gain_second = out_full[:, head_cols + E + 1].astype(f32)

    expert_ids = jnp.arange(E, dtype=jnp.int32)
    slot_near, slot_there, masks = [], [], []
    for i in range(LINE):
        named, counts = slot_ranks(routes_line[i].T)
        slot_of = jnp.where(named, counts - core * share, -1).T
        slot_of = lax.dynamic_slice_in_dim(own_first(slot_of, core, 1), level * mates, mates)
        slot_there.append(slot_of)
        slot_near.append(reorder(slot_of, relative, 0))
        masks.append(own_first(jnp.pad(named.astype(bf16), ((0, 0), (0, 128 - E))), core, 0))
    slot_near, slot_there, mask_line = [jnp.stack(t) for t in (slot_near, slot_there, masks)]

    slots = LINE * share * mates

    nil = packed_line[1, 0, 0] * 0
    weights = jnp.concatenate(
        [gate_weight, up_weight, down_weight.transpose(0, 2, 1) + nil], axis=2
    )
    weights = exchange(after(weights, packed_line))
    cot_line = line_gather(after(cotangent, packed_line))

    hidden_all = both_cores(hidden_in)
    tokens_all = hidden_all.astype(f32)
    scale_all = lax.rsqrt(jnp.mean(tokens_all * tokens_all, axis=-1, keepdims=True) + EPSILON)
    normed_all = (tokens_all * scale_all * gain_first).astype(bf16)
    places = own_first(positions(segments[0]), core, 0)
    segment_ids = own_first(segments[0], core, 0)
    token_index = own_first(jnp.arange(span, dtype=jnp.int32), core, 0)
    allowed = (segment_ids[:, None] == segment_ids[None, :]) & (
        token_index[None, :] <= token_index[:, None]
    )
    raw = jnp.dot(normed_all, qkv_cols, preferred_element_type=f32)
    queries = apply_rotary(raw[:, :head_cols].reshape(span, heads, HEAD_SIZE), places, 1.0)
    queries = queries.astype(bf16).transpose(1, 0, 2)
    keys = apply_rotary(
        raw[:, head_cols : head_cols + kv_cols].reshape(span, 1, HEAD_SIZE), places, 1.0
    ).astype(bf16)[:, 0]
    values = raw[:, head_cols + kv_cols :].astype(bf16)
    scaling = HEAD_SIZE ** (-0.5)
    attended, log_total = attend_group((queries, keys, values), allowed, scaling)
    attended_low = attended.transpose(1, 0, 2).reshape(span, head_cols).astype(bf16)
    branch_part = lax.dot_general(attended_low, output_t, nt, preferred_element_type=f32)
    tokens_in = hidden_in.astype(f32)
    hidden_mid = tokens_in + sum_cores(branch_part, f32)
    scale_second = lax.rsqrt(jnp.mean(hidden_mid * hidden_mid, axis=-1, keepdims=True) + EPSILON)
    unit_second = hidden_mid * scale_second
    normed_second = (unit_second * gain_second).astype(bf16)

    cot_line = after(cot_line, normed_second)
    cot_swap = swap_cores(cot_line)
    cot_rows = select_rows(slot_there, cot_line, cot_swap, share, mask_line)
    normed_line = line_gather(after(normed_second, weights, cot_rows))
    cot_rows = plane_all(cot_rows.reshape(mates, LINE, share, MODEL_WIDTH + 128))
    normed_swap = swap_cores(normed_line)
    normed_rows = select_rows(slot_near, after(normed_line, cot_rows), normed_swap, share)
    pieces = plane_exchange(normed_rows)

    pieces = [p.reshape(2 * LINE * share, MODEL_WIDTH) for p in pieces]
    cot_rows = cot_rows.reshape(PLANE, 2, LINE * share, MODEL_WIDTH + 128)
    weights = weights.reshape(rows, 2, row_block, 3 * hidden_block)
    done, mixture, back = [], None, []
    for move in range(PLANE):
        if move == 3:
            pieces[3] = after(pieces[3], back[1])
        found = expert_rows(
            move, place, core, my_expert, pieces[move], cot_rows, weights, out_full[:, head_cols:], mixture
        )
        mixture = found[1]
        done.append(found)
        back.append(plane_move(found[0], move) if move else found[0])
    _, _, grad_expert, activation, grad_gate, grad_up, grad_logits = [
        list(a) for a in zip(*done)
    ]

    def combine(table, near, far, far_block=0):
        kept, away = combine_rows(table, near, far, far_block)
        return (kept.astype(f32) + swap_cores(away).astype(f32)).astype(bf16)

    shape = (2, LINE, share, MODEL_WIDTH)
    back = [b.reshape(shape) for b in back]
    grad_expert[3] = after(grad_expert[3], back[2])
    down_home = exchange(after(shard_grad(grad_expert, activation, rows), back[3]))
    router_grad = sum(
        lax.dot_general(g, p, tn, preferred_element_type=f32) for g, p in zip(grad_logits, pieces)
    )
    router_grad = router_grad[:E].T
    far = swap_cores(after(jnp.stack([b[1] for b in back]), down_home, router_grad))
    grad_parts = combine(slot_near, jnp.stack([b[0] for b in back]), far)
    grad_normed = line_reduce(grad_parts).astype(f32)
    mixture = mixture.reshape(mates, LINE, share, MODEL_WIDTH)
    mixture = plane_all(after(mixture, down_home))
    mixture_there = after(mixture, grad_parts)
    mixture_parts = combine(slot_there, mixture_there, mixture_there, 1)
    mixture_own = line_reduce(mixture_parts).astype(f32)
    gate_up_home = shard_grad(pieces, grad_gate + grad_up, rows)
    gate_up_home = exchange(after(gate_up_home, mixture))

    grad_normed = after(grad_normed, mixture_parts)
    tilted = grad_normed * gain_second
    gain_second_grad = jnp.sum(grad_normed * unit_second, axis=0)
    grad_hidden = cotangent.astype(f32) + scale_second * (
        tilted - unit_second * jnp.mean(tilted * unit_second, axis=-1, keepdims=True)
    )
    branch_all = both_cores(grad_hidden.astype(bf16))

    output_t_grad = lax.dot_general(branch_all, attended_low, tn, preferred_element_type=f32)
    grad_attended = jnp.dot(branch_all, output_t, preferred_element_type=f32).astype(bf16)
    grad_attended = grad_attended.reshape(span, heads, HEAD_SIZE).transpose(1, 0, 2)
    grad_queries, grad_keys, grad_values = attend_back(
        (queries, keys, values, log_total, grad_attended), allowed, scaling
    )
    grad_query_low = (
        apply_rotary(grad_queries.transpose(1, 0, 2), places, -1.0)
        .reshape(span, head_cols)
        .astype(bf16)
    )
    grad_key_low = apply_rotary(grad_keys[:, None], places, -1.0)[:, 0].astype(bf16)
    grad_qkv = jnp.concatenate([grad_query_low, grad_key_low, grad_values.astype(bf16)], axis=1)
    qkv_grad = lax.dot_general(normed_all, grad_qkv, tn, preferred_element_type=f32)
    first_part = lax.dot_general(grad_qkv, qkv_cols, nt, preferred_element_type=f32)
    unit_all = tokens_all * scale_all
    gain_first_grad = jnp.sum(first_part * unit_all, axis=0)
    grad_first = sum_cores(first_part, f32)
    unit_first = tokens_in * scale_all[:local]
    tilted_first = grad_first * gain_first
    input_grad = grad_hidden + scale_all[:local] * (
        tilted_first - unit_first * jnp.mean(tilted_first * unit_first, axis=-1, keepdims=True)
    )
    block_out = (hidden_mid + mixture_own).astype(bf16)

    extra = jnp.concatenate(
        [
            router_grad,
            gain_second_grad[:, None],
            gain_first_grad[:, None],
            jnp.zeros((MODEL_WIDTH, 128 - E - 2), f32),
        ],
        axis=1,
    )
    owned, marks = row_reduce(
        [jnp.concatenate([output_t_grad, extra], axis=1), qkv_grad], level, place
    )
    output_own, qkv_own = owned[:, :head_cols], owned[:, head_cols + 128 :]
    small_own = owned[:, head_cols : head_cols + 128]
    small_own = small_own + swap_cores(small_own)
    gate_up_home = after(gate_up_home, *marks, block_out, input_grad)
    return (
        block_out,
        input_grad,
        small_own[:, E + 1],
        qkv_own[:, :head_cols],
        qkv_own[:, head_cols : head_cols + kv_cols],
        qkv_own[:, head_cols + kv_cols :],
        output_own[:, :head_cols].T,
        small_own[:, E],
        small_own[:, :E],
        gate_up_home[:, :, :hidden_block].astype(f32),
        gate_up_home[:, :, hidden_block:].astype(f32),
        down_home.astype(f32).transpose(0, 2, 1),
    )


def solution(mesh):
    in_specs = (
        P(("row", "col"), None),
        P("row", None),
        P("row", None),
        P("row"),
        P("row", "col"),
        P("row", "col"),
        P("row", "col"),
        P("col", "row"),
        P("row"),
        P("row", None),
        P(None, "row", "col"),
        P(None, "row", "col"),
        P(None, "col", "row"),
        P(("row", "col"), None),
    )
    out_specs = (
        P(("row", "col"), None),
        P(("row", "col"), None),
        P("row"),
        P("row", "col"),
        P("row", "col"),
        P("row", "col"),
        P("col", "row"),
        P("row"),
        P("row", None),
        P(None, "row", "col"),
        P(None, "row", "col"),
        P(None, "col", "row"),
    )
    rows, cols = mesh.shape["row"], mesh.shape["col"]
    one_each = rows == 4 * PLANE and cols == KEY_VALUE_HEADS and rows * cols == E
    return jax.shard_map(
        tokens_move if one_each else weights_move, mesh=mesh,
        in_specs=in_specs,
        out_specs=out_specs,
        check_vma=False,
    )
```

```python
import jax
import jax.numpy as jnp
from jax import lax
from jax.experimental import pallas as pl
from jax.experimental.pallas import tpu as pltpu
from jax.sharding import PartitionSpec as P

MODEL_WIDTH = 1536
QUERY_HEADS = 12
KEY_VALUE_HEADS = 2
HEAD_SIZE = 128
E = 32
TOPK = 4


EPSILON = 1e-06
ROPE_BASE = 1000000.0
MASKED = -1e30


def positions(segment_ids):
    total_length = segment_ids.shape[0]
    token_index = jnp.arange(total_length, dtype=jnp.int32)
    earlier = (segment_ids[:, None] == segment_ids[None, :]) & (
        token_index[None, :] < token_index[:, None]
    )
    return jnp.sum(earlier.astype(jnp.int32), axis=1)


def apply_rotary(values, places, direction):
    half_size = values.shape[-1] // 2
    frequency = ROPE_BASE ** (-2.0 * jnp.arange(half_size, dtype=jnp.float32) / values.shape[-1])
    angles = places.astype(jnp.float32)[:, None] * frequency[None, :]
    cosine_part = jnp.cos(angles)[:, None, :]
    sine_part = direction * jnp.sin(angles)[:, None, :]
    first_half = values[..., :half_size]
    second_half = values[..., half_size:]
    return jnp.concatenate(
        [
            first_half * cosine_part - second_half * sine_part,
            second_half * cosine_part + first_half * sine_part,
        ],
        axis=-1,
    )


def slot_ranks(route_ids):
    total_length = route_ids.shape[0]
    token_index = jnp.arange(total_length, dtype=jnp.int32)
    expert_ids = jnp.arange(E, dtype=jnp.int32)
    named = jnp.any(route_ids[:, :, None] == expert_ids[None, None, :], axis=1)
    before = (token_index[None, :] < token_index[:, None]).astype(jnp.bfloat16)
    counts = jnp.dot(before, named.astype(jnp.bfloat16), preferred_element_type=jnp.float32)
    return (named, counts.astype(jnp.int32))


def slot_tables(route_ids, experts, capacity):
    flat_ids = route_ids.reshape(-1)
    named, counts = slot_ranks(route_ids)
    rank_ids = jnp.sum(
        jnp.where(
            route_ids[:, :, None] == jnp.arange(experts, dtype=jnp.int32)[None, None, :],
            counts[:, None, :],
            0,
        ),
        axis=-1,
    ).reshape(-1)
    pair_slot = flat_ids * capacity + rank_ids
    owners = jnp.arange(flat_ids.shape[0], dtype=jnp.int32) // route_ids.shape[1]
    token_of = jnp.zeros((experts * capacity,), jnp.int32).at[pair_slot].set(owners)
    filled = jnp.zeros((experts * capacity,), jnp.int32).at[pair_slot].set(1)
    return (pair_slot, token_of, filled)


def masked_scores(queries, key_row_block, allowed, scaling):
    scores = (
        jnp.einsum("gqd,kd->gqk", queries, key_row_block, preferred_element_type=jnp.float32)
        * scaling
    )
    return jnp.where(allowed[None], scores, MASKED)


def attend_group(operands, allowed, scaling):
    queries, key_row_block, value_row_block = operands
    scores = masked_scores(queries, key_row_block, allowed, scaling)
    highest = jnp.max(scores, axis=-1, keepdims=True)
    exponent = jnp.exp(scores - highest)
    summed = jnp.sum(exponent, axis=-1, keepdims=True)
    weights_low = (exponent / summed).astype(jnp.bfloat16)
    result = jnp.einsum(
        "gqk,kd->gqd", weights_low, value_row_block, preferred_element_type=jnp.float32
    )
    return (result, highest + jnp.log(summed))


def attend_back(operands, allowed, scaling):
    queries, key_row_block, value_row_block, log_total, grad_result = operands
    scores = masked_scores(queries, key_row_block, allowed, scaling)
    weights_full = jnp.where(allowed[None], jnp.exp(scores - log_total), 0.0)
    weights_low = weights_full.astype(jnp.bfloat16)
    grad_values = jnp.einsum(
        "gqk,gqd->kd", weights_low, grad_result, preferred_element_type=jnp.float32
    )
    grad_weights = jnp.einsum(
        "gqd,kd->gqk", grad_result, value_row_block, preferred_element_type=jnp.float32
    )
    centre = jnp.sum(weights_full * grad_weights, axis=-1, keepdims=True)
    grad_scores = (weights_full * (grad_weights - centre)).astype(jnp.bfloat16)
    grad_queries = (
        jnp.einsum("gqk,kd->gqd", grad_scores, key_row_block, preferred_element_type=jnp.float32)
        * scaling
    )
    grad_keys = (
        jnp.einsum("gqk,gqd->kd", grad_scores, queries, preferred_element_type=jnp.float32)
        * scaling
    )
    return (grad_queries, grad_keys, grad_values)


def weights_move(
    hidden_in,
    segments,
    routes,
    attention_gain,
    query_weight,
    key_matrix,
    value_matrix,
    output_weight,
    expert_gain,
    router_weight,
    gate_weight,
    up_weight,
    down_weight,
    cotangent,
):
    gain_first, query_cols, key_cols, value_cols, output_rows = (
        lax.all_gather(attention_gain, "row", axis=0, tiled=True),
        lax.all_gather(query_weight, "row", axis=0, tiled=True),
        lax.all_gather(key_matrix, "row", axis=0, tiled=True),
        lax.all_gather(value_matrix, "row", axis=0, tiled=True),
        lax.all_gather(output_weight, "row", axis=1, tiled=True),
    )
    query_full, gathered_keys, gathered_values, output_full = (
        lax.all_gather(query_cols, "col", axis=1, tiled=True),
        lax.all_gather(key_cols, "col", axis=1, tiled=True),
        lax.all_gather(value_cols, "col", axis=1, tiled=True),
        lax.all_gather(output_rows, "col", axis=0, tiled=True),
    )
    gain_second, router_full, gate_full, up_full, down_full = (
        lax.all_gather(expert_gain, "row", axis=0, tiled=True),
        lax.all_gather(router_weight, "row", axis=0, tiled=True),
        lax.all_gather(gate_weight, "row", axis=1, tiled=True),
        lax.all_gather(up_weight, "row", axis=1, tiled=True),
        lax.all_gather(down_weight, "row", axis=2, tiled=True),
    )
    local_row_block = hidden_in.shape[0]
    sequence_span_length = segments.shape[1]
    first_row = lax.axis_index("col") * local_row_block
    segment_ids = segments[0]
    places_all = positions(segment_ids)
    local_positions = lax.dynamic_slice_in_dim(places_all, first_row, local_row_block)
    own_segments = lax.dynamic_slice_in_dim(segment_ids, first_row, local_row_block)
    query_index = first_row + jnp.arange(local_row_block, dtype=jnp.int32)
    key_index = jnp.arange(sequence_span_length, dtype=jnp.int32)
    allowed = (own_segments[:, None] == segment_ids[None, :]) & (
        key_index[None, :] <= query_index[:, None]
    )
    tokens_in = hidden_in.astype(jnp.float32)
    scale_first = lax.rsqrt(jnp.mean(tokens_in * tokens_in, axis=-1, keepdims=True) + EPSILON)
    unit_first = tokens_in * scale_first
    normed_first = (unit_first * gain_first.astype(jnp.float32)).astype(jnp.bfloat16)
    query_raw = jnp.dot(normed_first, query_full, preferred_element_type=jnp.float32).reshape(
        local_row_block, QUERY_HEADS, HEAD_SIZE
    )
    unrotated_keys = jnp.dot(
        normed_first, gathered_keys, preferred_element_type=jnp.float32
    ).reshape(local_row_block, KEY_VALUE_HEADS, HEAD_SIZE)
    values_reduced = jnp.dot(
        normed_first, gathered_values, preferred_element_type=jnp.float32
    ).astype(jnp.bfloat16)
    rotated_queries = apply_rotary(query_raw, local_positions, 1.0).astype(jnp.bfloat16)
    rotated_keys = (
        apply_rotary(unrotated_keys, local_positions, 1.0)
        .astype(jnp.bfloat16)
        .reshape(local_row_block, KEY_VALUE_HEADS * HEAD_SIZE)
    )
    key_row_block, value_row_block = (
        lax.all_gather(rotated_keys, "col", axis=0, tiled=True),
        lax.all_gather(values_reduced, "col", axis=0, tiled=True),
    )
    heads_per_group = QUERY_HEADS // KEY_VALUE_HEADS
    scaling = HEAD_SIZE ** (-0.5)
    grouped_queries = rotated_queries.reshape(
        local_row_block, KEY_VALUE_HEADS, heads_per_group, HEAD_SIZE
    ).transpose(1, 2, 0, 3)
    grouped_keys = key_row_block.reshape(
        sequence_span_length, KEY_VALUE_HEADS, HEAD_SIZE
    ).transpose(1, 0, 2)
    grouped_values = value_row_block.reshape(
        sequence_span_length, KEY_VALUE_HEADS, HEAD_SIZE
    ).transpose(1, 0, 2)
    attended, log_total = lax.map(
        lambda operands: attend_group(operands, allowed, scaling),
        (grouped_queries, grouped_keys, grouped_values),
    )
    attended_low = (
        attended.transpose(2, 0, 1, 3)
        .reshape(local_row_block, QUERY_HEADS * HEAD_SIZE)
        .astype(jnp.bfloat16)
    )
    branch = jnp.dot(attended_low, output_full, preferred_element_type=jnp.float32)
    hidden_mid = tokens_in + branch
    scale_second = lax.rsqrt(jnp.mean(hidden_mid * hidden_mid, axis=-1, keepdims=True) + EPSILON)
    unit_second = hidden_mid * scale_second
    normed_second = (unit_second * gain_second.astype(jnp.float32)).astype(jnp.bfloat16)
    normed_all, upstream_all = (
        lax.all_gather(normed_second, "col", axis=0, tiled=True),
        lax.all_gather(cotangent, "col", axis=0, tiled=True),
    )
    logits = jnp.dot(normed_all, router_full, preferred_element_type=jnp.float32)
    expert_ids = jnp.arange(E, dtype=jnp.int32)
    chosen_mask = routes[:, :, None] == expert_ids[None, None, :]
    chosen = jnp.sum(jnp.where(chosen_mask, logits[:, None, :], 0.0), axis=-1)
    exponent = jnp.exp(chosen - jnp.max(chosen, axis=-1, keepdims=True))
    route_gates = exponent / jnp.sum(exponent, axis=-1, keepdims=True)
    group_width = 4
    capacity = max(2, 3 * sequence_span_length * TOPK // (2 * E))
    pair_slot, token_of, filled = slot_tables(routes, E, capacity)
    slot_gate = jnp.zeros((E * capacity,), jnp.float32).at[pair_slot].set(route_gates.reshape(-1))
    group_rows = group_width * capacity

    def expert_step(accumulated, group_index):
        mixture_sum, input_sum = accumulated
        offset = group_index * group_rows
        row_ids = lax.dynamic_slice_in_dim(token_of, offset, group_rows)
        occupied = lax.dynamic_slice_in_dim(filled, offset, group_rows) > 0
        slot_weight = lax.dynamic_slice_in_dim(slot_gate, offset, group_rows)
        first_expert = group_index * group_width
        gate_block = lax.dynamic_slice_in_dim(gate_full, first_expert, group_width, 0)
        up_block = lax.dynamic_slice_in_dim(up_full, first_expert, group_width, 0)
        down_block = lax.dynamic_slice_in_dim(down_full, first_expert, group_width, 0)
        inputs = jnp.where(
            occupied[:, None], normed_all[row_ids], jnp.zeros((), jnp.bfloat16)
        ).reshape(group_width, capacity, MODEL_WIDTH)
        upstream = upstream_all[row_ids].astype(jnp.float32)
        gate_value = jnp.einsum(
            "ecd,edf->ecf", inputs, gate_block, preferred_element_type=jnp.float32
        )
        up_value = jnp.einsum("ecd,edf->ecf", inputs, up_block, preferred_element_type=jnp.float32)
        sigmoid_gate = jax.nn.sigmoid(gate_value)
        silu_gate = gate_value * sigmoid_gate
        activation = (silu_gate * up_value).astype(jnp.bfloat16)
        partial_out = jnp.einsum(
            "ecf,efd->ecd", activation, down_block, preferred_element_type=jnp.float32
        ).reshape(group_rows, MODEL_WIDTH)
        mixture_sum = mixture_sum.at[row_ids].add(partial_out * slot_weight[:, None])
        slot_grad = jnp.sum(partial_out * upstream, axis=-1)
        grad_expert = (
            (upstream * slot_weight[:, None])
            .astype(jnp.bfloat16)
            .reshape(group_width, capacity, MODEL_WIDTH)
        )
        grad_act = jnp.einsum(
            "ecd,efd->ecf", grad_expert, down_block, preferred_element_type=jnp.float32
        )
        slope = sigmoid_gate * (1.0 + gate_value * (1.0 - sigmoid_gate))
        grad_gate = (grad_act * up_value * slope).astype(jnp.bfloat16)
        grad_up = (grad_act * silu_gate).astype(jnp.bfloat16)
        grad_inputs = jnp.einsum(
            "ecf,edf->ecd", grad_gate, gate_block, preferred_element_type=jnp.float32
        )
        grad_inputs = grad_inputs + jnp.einsum(
            "ecf,edf->ecd", grad_up, up_block, preferred_element_type=jnp.float32
        )
        input_sum = input_sum.at[row_ids].add(grad_inputs.reshape(group_rows, MODEL_WIDTH))
        gate_piece = jnp.einsum(
            "ecd,ecf->edf", inputs, grad_gate, preferred_element_type=jnp.float32
        )
        up_piece = jnp.einsum("ecd,ecf->edf", inputs, grad_up, preferred_element_type=jnp.float32)
        down_piece = jnp.einsum(
            "ecf,ecd->efd", activation, grad_expert, preferred_element_type=jnp.float32
        )
        return ((mixture_sum, input_sum), (slot_grad, gate_piece, up_piece, down_piece))

    initial = (
        jnp.zeros((sequence_span_length, MODEL_WIDTH), jnp.float32),
        jnp.zeros((sequence_span_length, MODEL_WIDTH), jnp.float32),
    )
    sums_out, pieces = lax.scan(expert_step, initial, jnp.arange(E // group_width, dtype=jnp.int32))
    mixture_part, input_part = sums_out
    slot_grads, gate_pieces, up_pieces, down_pieces = pieces
    hidden_cols = gate_full.shape[2]
    gate_grad = gate_pieces.reshape(E, MODEL_WIDTH, hidden_cols)
    up_grad = up_pieces.reshape(E, MODEL_WIDTH, hidden_cols)
    down_grad = down_pieces.reshape(E, hidden_cols, MODEL_WIDTH)
    pick_grads = slot_grads.reshape(-1)[pair_slot].reshape(sequence_span_length, TOPK)
    mixture_own, input_own, pick_own = (
        lax.psum_scatter(mixture_part, "col", scatter_dimension=0, tiled=True),
        lax.psum_scatter(input_part, "col", scatter_dimension=0, tiled=True),
        lax.psum_scatter(pick_grads, "col", scatter_dimension=0, tiled=True),
    )
    block_out = (hidden_mid + mixture_own).astype(jnp.bfloat16)
    own_gates = lax.dynamic_slice_in_dim(route_gates, first_row, local_row_block)
    own_mask = lax.dynamic_slice_in_dim(chosen_mask, first_row, local_row_block)
    centred = own_gates * (pick_own - jnp.sum(own_gates * pick_own, axis=-1, keepdims=True))
    grad_logits = jnp.sum(jnp.where(own_mask, centred[:, :, None], 0.0), axis=1).astype(
        jnp.bfloat16
    )
    grad_normed = input_own + jnp.dot(
        grad_logits, router_full.T, preferred_element_type=jnp.float32
    )
    router_grad = jnp.dot(normed_second.T, grad_logits, preferred_element_type=jnp.float32)
    tilted_second = grad_normed * gain_second.astype(jnp.float32)
    gain_second_grad = jnp.sum(grad_normed * unit_second, axis=0)
    grad_hidden = cotangent.astype(jnp.float32) + scale_second * (
        tilted_second - unit_second * jnp.mean(tilted_second * unit_second, axis=-1, keepdims=True)
    )
    grad_branch = grad_hidden.astype(jnp.bfloat16)
    output_grad = jnp.dot(attended_low.T, grad_branch, preferred_element_type=jnp.float32)
    attended_gradient = jnp.dot(
        grad_branch, output_full.T, preferred_element_type=jnp.float32
    ).astype(jnp.bfloat16)
    grouped_gradient = attended_gradient.reshape(
        local_row_block, KEY_VALUE_HEADS, heads_per_group, HEAD_SIZE
    ).transpose(1, 2, 0, 3)
    grad_query_groups, key_gradient_grouped, value_gradient_grouped = lax.map(
        lambda operands: attend_back(operands, allowed, scaling),
        (grouped_queries, grouped_keys, grouped_values, log_total, grouped_gradient),
    )
    grad_query_rot = grad_query_groups.transpose(2, 0, 1, 3).reshape(
        local_row_block, QUERY_HEADS, HEAD_SIZE
    )
    key_gradient_total = key_gradient_grouped.transpose(1, 0, 2).reshape(
        sequence_span_length, KEY_VALUE_HEADS * HEAD_SIZE
    )
    value_gradient_total = value_gradient_grouped.transpose(1, 0, 2).reshape(
        sequence_span_length, KEY_VALUE_HEADS * HEAD_SIZE
    )
    local_keys, value_own = (
        lax.psum_scatter(
            key_gradient_total.astype(jnp.bfloat16), "col", scatter_dimension=0, tiled=True
        ).astype(jnp.float32),
        lax.psum_scatter(
            value_gradient_total.astype(jnp.bfloat16), "col", scatter_dimension=0, tiled=True
        ).astype(jnp.float32),
    )
    grad_query_low = (
        apply_rotary(grad_query_rot, local_positions, -1.0)
        .reshape(local_row_block, QUERY_HEADS * HEAD_SIZE)
        .astype(jnp.bfloat16)
    )
    grad_key_low = (
        apply_rotary(
            local_keys.reshape(local_row_block, KEY_VALUE_HEADS, HEAD_SIZE), local_positions, -1.0
        )
        .reshape(local_row_block, KEY_VALUE_HEADS * HEAD_SIZE)
        .astype(jnp.bfloat16)
    )
    grad_value_low = value_own.astype(jnp.bfloat16)
    grad_normed_first = jnp.dot(grad_query_low, query_full.T, preferred_element_type=jnp.float32)
    grad_normed_first = grad_normed_first + jnp.dot(
        grad_key_low, gathered_keys.T, preferred_element_type=jnp.float32
    )
    grad_normed_first = grad_normed_first + jnp.dot(
        grad_value_low, gathered_values.T, preferred_element_type=jnp.float32
    )
    query_grad = jnp.dot(normed_first.T, grad_query_low, preferred_element_type=jnp.float32)
    key_grad = jnp.dot(normed_first.T, grad_key_low, preferred_element_type=jnp.float32)
    value_grad = jnp.dot(normed_first.T, grad_value_low, preferred_element_type=jnp.float32)
    tilted_first = grad_normed_first * gain_first.astype(jnp.float32)
    gain_first_grad = jnp.sum(grad_normed_first * unit_first, axis=0)
    input_grad = grad_hidden + scale_first * (
        tilted_first - unit_first * jnp.mean(tilted_first * unit_first, axis=-1, keepdims=True)
    )
    query_part, key_part, value_part, output_part = (
        lax.psum_scatter(
            query_grad.astype(jnp.bfloat16), "col", scatter_dimension=1, tiled=True
        ).astype(jnp.float32),
        lax.psum_scatter(
            key_grad.astype(jnp.bfloat16), "col", scatter_dimension=1, tiled=True
        ).astype(jnp.float32),
        lax.psum_scatter(
            value_grad.astype(jnp.bfloat16), "col", scatter_dimension=1, tiled=True
        ).astype(jnp.float32),
        lax.psum_scatter(
            output_grad.astype(jnp.bfloat16), "col", scatter_dimension=0, tiled=True
        ).astype(jnp.float32),
    )
    small_total = lax.psum((gain_first_grad, gain_second_grad, router_grad), ("row", "col"))
    query_out, key_out, value_out, output_out, gate_out, up_out, down_out = (
        lax.psum_scatter(
            query_part.astype(jnp.bfloat16), "row", scatter_dimension=0, tiled=True
        ).astype(jnp.float32),
        lax.psum_scatter(
            key_part.astype(jnp.bfloat16), "row", scatter_dimension=0, tiled=True
        ).astype(jnp.float32),
        lax.psum_scatter(
            value_part.astype(jnp.bfloat16), "row", scatter_dimension=0, tiled=True
        ).astype(jnp.float32),
        lax.psum_scatter(
            output_part.astype(jnp.bfloat16), "row", scatter_dimension=1, tiled=True
        ).astype(jnp.float32),
        lax.psum_scatter(
            gate_grad.astype(jnp.bfloat16), "row", scatter_dimension=1, tiled=True
        ).astype(jnp.float32),
        lax.psum_scatter(
            up_grad.astype(jnp.bfloat16), "row", scatter_dimension=1, tiled=True
        ).astype(jnp.float32),
        lax.psum_scatter(
            down_grad.astype(jnp.bfloat16), "row", scatter_dimension=2, tiled=True
        ).astype(jnp.float32),
    )
    row_block = attention_gain.shape[0]
    row_start = lax.axis_index("row") * row_block
    gain_first_out = lax.dynamic_slice_in_dim(small_total[0], row_start, row_block)
    gain_second_out = lax.dynamic_slice_in_dim(small_total[1], row_start, row_block)
    router_out = lax.dynamic_slice_in_dim(small_total[2], row_start, row_block, 0)
    return (
        block_out,
        input_grad,
        gain_first_out,
        query_out,
        key_out,
        value_out,
        output_out,
        gain_second_out,
        router_out,
        gate_out,
        up_out,
        down_out,
    )


GRID = ("row", "col")
PLANE = 4
LINE = 4


def nothing(*refs):
    pass


def after(block, *others):
    anywhere = pl.BlockSpec(memory_space=pl.ANY)
    return pl.pallas_call(
        nothing,
        out_shape=jax.ShapeDtypeStruct(block.shape, block.dtype),
        in_specs=[anywhere] * (1 + len(others)),
        out_specs=anywhere,
        input_output_aliases={0: 0},
        name="after",
    )(block, *others)


def swap_cores(block):
    return lax.ppermute(block, "col", [(0, 1), (1, 0)])


def both_cores(own):
    return jnp.concatenate([own, swap_cores(own)], axis=0)


def sum_cores(partial, kind):
    half = partial.shape[0] // 2
    away = partial[half:].astype(kind)
    return partial[:half] + swap_cores(away).astype(partial.dtype)


def own_first(table, core, axis):
    half = table.shape[axis] // 2
    mine = lax.dynamic_slice_in_dim(table, core * half, half, axis)
    theirs = lax.dynamic_slice_in_dim(table, (1 - core) * half, half, axis)
    return jnp.concatenate([mine, theirs], axis=axis)


def exchange(block):
    return lax.all_to_all(block, GRID, split_axis=0, concat_axis=0, tiled=True)


LINES = [[z * PLANE + p for z in range(LINE)] for p in range(PLANE)]


def line_shift(block, step):
    pairs = [
        (s * PLANE + p, (s + step) % LINE * PLANE + p) for s in range(LINE) for p in range(PLANE)
    ]
    return lax.ppermute(block, "row", pairs)


def plane_pairs(flip):
    return [(r, r ^ flip) for r in range(PLANE * LINE)]


def reorder(block, order, axis):
    picked = [lax.dynamic_index_in_dim(block, i, axis, True) for i in order]
    return jnp.concatenate(picked, axis=axis)


def row_gather(line, level, place):
    moved = [lax.ppermute(line, "row", plane_pairs(flip)) for flip in range(1, PLANE)]
    whole = jnp.concatenate([line, *moved], axis=0)
    order = [(place ^ p) * LINE + (level - z) % LINE for z in range(LINE) for p in range(PLANE)]
    return reorder(whole, order, 0).reshape(LINE * PLANE * line.shape[1], line.shape[2])


def row_reduce(halves, level, place):
    block = halves[0].shape[0] // (LINE * PLANE)
    halves = [h.reshape(LINE, 2, 2, block, h.shape[1]) for h in halves]
    marks = []
    for flips in ((1, 2), (2, 1)):
        for i, flip in enumerate(flips):
            axis = min(3 - flip, halves[i].ndim - 3)
            bit = (place // flip) % 2
            kept = lax.dynamic_index_in_dim(halves[i], bit, axis, False)
            away = lax.dynamic_index_in_dim(halves[i], 1 - bit, axis, False)
            away = lax.ppermute(away.astype(jnp.bfloat16), "row", plane_pairs(flip))
            halves[i] = kept + away.astype(jnp.float32)
            marks.append(halves[i])
    order = [(level + step) % LINE for step in range(LINE)]
    parts = [
        jnp.concatenate([lax.dynamic_index_in_dim(h, i, 0, False) for h in halves], axis=1)
        for i in order
    ]
    moved = [line_shift(parts[step].astype(jnp.bfloat16), step) for step in range(1, LINE)]
    total = parts[0]
    for part in moved:
        total = total + part.astype(jnp.float32)
    return total, marks[2:]


def line_gather(block):
    whole = lax.all_gather(block, "row", axis=0, tiled=False, axis_index_groups=LINES)
    return whole


def line_reduce(parts):
    return lax.psum_scatter(
        parts, "row", scatter_dimension=0, tiled=False, axis_index_groups=LINES
    )


def plane_move(block, move):
    return lax.ppermute(block, "row", plane_pairs(move))


def plane_exchange(block):
    far = swap_cores(block[1])
    pairs = [jnp.stack([block[0, m], far[m]]) for m in range(PLANE)]
    moved = {m: plane_move(pairs[m], m) for m in (1, 2, 3)}
    return [pairs[0], moved[1], moved[2], moved[3]]


def plane_all(block):
    groups = [[z * 2 * PLANE + d for d in range(2 * PLANE)] for z in range(LINE)]
    return lax.all_to_all(
        block, GRID, split_axis=0, concat_axis=0, tiled=True, axis_index_groups=groups
    )


def expert_body(
    where_ref,
    x_ref,
    cot_ref,
    weights_ref,
    router_ref,
    _,
    grad_in_ref,
    mix_ref,
    grad_expert_ref,
    act_ref,
    grad_gate_ref,
    grad_up_ref,
    grad_logits_ref,
):
    bf16, f32 = jnp.bfloat16, jnp.float32
    core, expert = where_ref[1], where_ref[2]
    nt = (((1,), (1,)), ((), ()))
    width = x_ref.shape[1]
    x = x_ref[...]
    half = x.shape[0] // 2
    there = jnp.concatenate([cot_ref[0, core], cot_ref[0, 1 - core]], axis=0)
    mask = there[:, width:].astype(f32) > 0
    upstream = there[:, :width].astype(f32)
    router = router_ref[...]
    logits = jnp.dot(x, router, preferred_element_type=f32)
    top = jnp.max(jnp.where(mask, logits, MASKED), axis=-1, keepdims=True)
    exponent = jnp.where(mask, jnp.exp(logits - top), 0.0)
    gates = exponent / jnp.maximum(jnp.sum(exponent, axis=-1, keepdims=True), 1e-30)
    mine = lax.broadcasted_iota(jnp.int32, gates.shape, 1) == expert
    slot_gate = jnp.sum(jnp.where(mine, gates, 0.0), axis=-1, keepdims=True)
    grad_expert = (upstream * slot_gate).astype(bf16)
    grad_expert_ref[...] = grad_expert
    cols = weights_ref.shape[3] // 3
    parts, out = [], None
    for side in range(2):
        gate_w = weights_ref[:, side, :, :cols].reshape(width, cols)
        up_w = weights_ref[:, side, :, cols : 2 * cols].reshape(width, cols)
        down_t = weights_ref[:, side, :, 2 * cols :].reshape(width, cols)
        gate_value = jnp.dot(x, gate_w, preferred_element_type=f32)
        up_value = jnp.dot(x, up_w, preferred_element_type=f32)
        sigmoid = 1.0 / (1.0 + jnp.exp(-gate_value))
        silu = gate_value * sigmoid
        act = (silu * up_value).astype(bf16)
        part = lax.dot_general(act, down_t, nt, preferred_element_type=f32)
        out = part if out is None else out + part
        grad_act = jnp.dot(grad_expert, down_t, preferred_element_type=f32)
        slope = sigmoid * (1.0 + gate_value * (1.0 - sigmoid))
        grad_gate = (grad_act * up_value * slope).astype(bf16)
        grad_up = (grad_act * silu).astype(bf16)
        act_ref[:, side * cols : (side + 1) * cols] = act
        grad_gate_ref[:, side * cols : (side + 1) * cols] = grad_gate
        grad_up_ref[:, side * cols : (side + 1) * cols] = grad_up
        parts.append((grad_gate, grad_up, gate_w, up_w))
    scaled = (out * slot_gate).astype(bf16)
    mix_ref[0, core] = scaled[:half]
    mix_ref[0, 1 - core] = scaled[half:]
    pick_grad = slot_gate * jnp.sum(out * upstream, axis=-1, keepdims=True)
    grad_logits = (pick_grad * (jnp.where(mine, 1.0, 0.0) - gates)).astype(bf16)
    grad_logits_ref[...] = grad_logits
    grad_in = lax.dot_general(grad_logits, router, nt, preferred_element_type=f32)
    for grad_gate, grad_up, gate_w, up_w in parts:
        grad_in += lax.dot_general(grad_gate, gate_w, nt, preferred_element_type=f32)
        grad_in += lax.dot_general(grad_up, up_w, nt, preferred_element_type=f32)
    grad_in_ref[...] = grad_in.astype(bf16)


def expert_rows(move, place, core, expert, x, cot, weights, router, mixture):
    slots, width = x.shape
    cols = weights.shape[3] // 3
    where = jnp.stack([place, core, expert]).astype(jnp.int32)

    def whole(shape):
        return pl.BlockSpec(shape, lambda i, w: (0,) * len(shape))

    outs = [width, width, width, 2 * cols, 2 * cols, 2 * cols, router.shape[1]]
    out_specs = [whole((slots, n)) for n in outs]
    out_shape = [jax.ShapeDtypeStruct((slots, n), jnp.bfloat16) for n in outs]
    mix_block = (1, 2, slots // 2, width)
    out_specs[1] = pl.BlockSpec(mix_block, lambda i, w: (w[0] ^ move, 0, 0, 0))
    out_shape[1] = jax.ShapeDtypeStruct((PLANE, *mix_block[1:]), jnp.bfloat16)
    resident = pl.BlockSpec(memory_space=pltpu.VMEM)
    first = mixture is None
    cot_spec = pl.BlockSpec((1, *cot.shape[1:]), lambda i, w: (w[0] ^ move, 0, 0, 0))
    anywhere = pl.BlockSpec(memory_space=pl.ANY)
    return pl.pallas_call(
        expert_body,
        grid_spec=pltpu.PrefetchScalarGridSpec(
            num_scalar_prefetch=1,
            grid=(1,),
            in_specs=[whole(x.shape), cot_spec, resident, resident, anywhere],
            out_specs=out_specs,
        ),
        out_shape=out_shape,
        input_output_aliases={} if first else {5: 1},
        compiler_params=pltpu.CompilerParams(vmem_limit_bytes=40 << 20),
        cost_estimate=pl.CostEstimate(
            flops=24 * slots * width * cols,
            bytes_accessed=2 * (5 * slots * width + 6 * slots * cols),
            transcendentals=slots * 2 * cols,
        ),
        name="expert_rows",
    )(where, x, cot, weights, router, x if first else mixture)


def picked(slots, share):
    ids = lax.broadcasted_iota(jnp.int32, (share, slots.shape[1]), 0)
    rows = [(slots[e : e + 1] == ids).astype(jnp.bfloat16) for e in range(slots.shape[0])]
    return jnp.concatenate(rows, axis=0)


def select_body(slots_ref, own_ref, other_ref, *rest):
    out_ref = rest[-1]
    share = out_ref.shape[3]
    pick = picked(slots_ref[0], share)
    half, width = own_ref.shape[1], own_ref.shape[2]
    rows = jnp.dot(pick[:, :half], own_ref[0], preferred_element_type=jnp.float32)
    rows += jnp.dot(pick[:, half:], other_ref[0], preferred_element_type=jnp.float32)
    out_ref[:, :, 0, :, :width] = rows.astype(jnp.bfloat16).reshape(2, PLANE, share, width)
    if len(rest) == 2:
        extra = jnp.dot(pick, rest[0][0], preferred_element_type=jnp.float32)
        extra = extra.astype(jnp.bfloat16)
        out_ref[:, :, 0, :, width:] = extra.reshape(2, PLANE, share, extra.shape[1])


def select_rows(slots, own, other, share, extra=None):
    lines, mates, span = slots.shape
    half, width = own.shape[1:]
    wide = width + (0 if extra is None else extra.shape[2])
    parts = [slots, own, other] + ([] if extra is None else [extra])

    def block(shape):
        return pl.BlockSpec((1, *shape), lambda i: (i, 0, 0))

    specs = [block((mates, span)), block((half, width)), block((half, width))]
    if extra is not None:
        specs.append(block((span, extra.shape[2])))
    return pl.pallas_call(
        select_body,
        grid=(lines,),
        in_specs=specs,
        out_specs=pl.BlockSpec((2, PLANE, 1, share, wide), lambda i: (0, 0, i, 0, 0)),
        out_shape=jax.ShapeDtypeStruct((2, PLANE, lines, share, wide), jnp.bfloat16),
        compiler_params=pltpu.CompilerParams(vmem_limit_bytes=40 << 20),
        cost_estimate=pl.CostEstimate(
            flops=2 * lines * mates * share * span * wide,
            bytes_accessed=2 * lines * (span + mates * share) * wide,
            transcendentals=0,
        ),
        name="select_rows",
    )(*parts)


def combine_body(slots_ref, near_ref, far_ref, kept_ref, away_ref):
    chips, _, share, width = near_ref.shape
    half = kept_ref.shape[1]
    pick = picked(slots_ref[0], share).T
    near = near_ref[:, 0].reshape(chips * share, width)
    far = far_ref[:, 0].reshape(chips * share, width)
    total = jnp.dot(pick, jnp.concatenate([near, far]), preferred_element_type=jnp.float32)
    kept_ref[0] = total[:half].astype(kept_ref.dtype)
    away_ref[0] = total[half:].astype(away_ref.dtype)


def combine_rows(slots, near, far, far_block=0):
    lines, mates, span = slots.shape
    chips = mates // 2
    share, width = near.shape[2:]
    part = pl.BlockSpec((1, span // 2, width), lambda i: (i, 0, 0))
    shape = (lines, span // 2, width)
    return pl.pallas_call(
        combine_body,
        grid=(lines,),
        in_specs=[
            pl.BlockSpec((1, mates, span), lambda i: (i, 0, 0)),
            pl.BlockSpec((chips, 1, share, width), lambda i: (0, i, 0, 0)),
            pl.BlockSpec((chips, 1, share, width), lambda i: (far_block, i, 0, 0)),
        ],
        out_specs=[part, part],
        out_shape=[
            jax.ShapeDtypeStruct(shape, jnp.bfloat16),
            jax.ShapeDtypeStruct(shape, jnp.bfloat16),
        ],
        compiler_params=pltpu.CompilerParams(vmem_limit_bytes=40 << 20),
        cost_estimate=pl.CostEstimate(
            flops=2 * lines * mates * share * span * width,
            bytes_accessed=2 * lines * (2 * span + mates * share) * width,
            transcendentals=0,
        ),
        name="combine_rows",
    )(slots, near, far)


def shard_body(pieces, left_refs, right_refs, out_ref):
    count, _, block, _ = out_ref.shape
    lefts = [ref[...].T for ref in left_refs]
    for i in range(len(right_refs) // pieces):
        rights = right_refs[i * pieces : (i + 1) * pieces]
        full = None
        for left, right in zip(lefts, rights):
            part = jnp.dot(left, right[...], preferred_element_type=jnp.float32)
            full = part if full is None else full + part
        full = full.astype(jnp.bfloat16)
        cols = full.shape[1] // 2
        for core in range(2):
            part = full[:, core * cols : (core + 1) * cols]
            out_ref[:, core, :, i * cols : (i + 1) * cols] = part.reshape(count, block, cols)


def shard_grad(lefts, rights, rows, count=4):
    pieces = len(lefts)
    slots, width = lefts[0].shape
    cols = rights[0].shape[1] // 2
    block = width // rows
    wide = cols * (len(rights) // pieces)

    def body(*refs):
        shard_body(pieces, refs[:pieces], refs[pieces:-1], refs[-1])

    out = pl.pallas_call(
        body,
        grid=(rows // count,),
        in_specs=[pl.BlockSpec((slots, count * block), lambda i: (0, i)) for _ in lefts]
        + [pl.BlockSpec((slots, 2 * cols), lambda i: (0, 0)) for _ in rights],
        out_specs=pl.BlockSpec((count, 2, block, wide), lambda i: (i, 0, 0, 0)),
        out_shape=jax.ShapeDtypeStruct((rows, 2, block, wide), jnp.bfloat16),
        compiler_params=pltpu.CompilerParams(vmem_limit_bytes=48 << 20),
        cost_estimate=pl.CostEstimate(
            flops=4 * pieces * slots * width * wide,
            bytes_accessed=2 * (pieces * slots * (width + 2 * wide) + 2 * width * wide),
            transcendentals=0,
        ),
        name="shard_grad",
    )(*lefts, *rights)
    return out.reshape(2 * rows, block, wide)


def tokens_move(
    hidden_in,
    segments,
    routes,
    attention_gain,
    query_weight,
    key_matrix,
    value_matrix,
    output_weight,
    expert_gain,
    router_weight,
    gate_weight,
    up_weight,
    down_weight,
    cotangent,
):
    bf16, f32 = jnp.bfloat16, jnp.float32
    core, row = lax.axis_index("col"), lax.axis_index("row")
    level, place = row // PLANE, row % PLANE
    local = hidden_in.shape[0]
    span = segments.shape[1]
    row_block = query_weight.shape[0]
    rows = MODEL_WIDTH // row_block
    hidden_block = gate_weight.shape[2]
    ffe = 2 * hidden_block
    capacity = max(2, 3 * span * TOPK // (2 * E))
    share = capacity // 2
    head_cols = query_weight.shape[1]
    kv_cols = key_matrix.shape[1]
    heads = head_cols // HEAD_SIZE
    mates = 2 * PLANE
    my_expert = row * 2 + core
    relative = [(place * 2 + core) ^ (2 * m + k) for k in range(2) for m in range(PLANE)]
    nt = (((1,), (1,)), ((), ()))
    tn = (((0,), (0,)), ((), ()))

    routes_rows = span * TOPK // 64
    routes_own = routes.T.astype(bf16).reshape(routes_rows, 64)
    routes_own = jnp.pad(routes_own, ((0, row_block - routes_rows), (0, 0)))
    packed = jnp.concatenate(
        [
            query_weight,
            key_matrix,
            value_matrix,
            output_weight.T,
            router_weight,
            attention_gain[:, None],
            expert_gain[:, None],
            routes_own,
            jnp.zeros((row_block, 126 - E - routes_own.shape[1]), bf16),
        ],
        axis=1,
    )
    packed_line = jnp.stack([packed] + [line_shift(packed, step) for step in range(1, LINE)])
    o0 = head_cols + 2 * kv_cols
    first = o0 + head_cols + E + 2
    routes_line = packed_line[:, :routes_rows, first : first + 64].reshape(LINE, TOPK, span)
    routes_line = reorder(routes_line, [(level - z) % LINE for z in range(LINE)], 0)
    routes_line = routes_line.astype(jnp.int32)
    packed_full = row_gather(packed_line, level, place)
    qkv_cols, out_full = packed_full[:, :o0], packed_full[:, o0:]
    output_t = out_full[:, :head_cols]
    router_full = out_full[:, head_cols : head_cols + E]
    gain_first = out_full[:, head_cols + E].astype(f32)
    gain_second = out_full[:, head_cols + E + 1].astype(f32)

    expert_ids = jnp.arange(E, dtype=jnp.int32)
    slot_near, slot_there, masks = [], [], []
    for i in range(LINE):
        named, counts = slot_ranks(routes_line[i].T)
        slot_of = jnp.where(named, counts - core * share, -1).T
        slot_of = lax.dynamic_slice_in_dim(own_first(slot_of, core, 1), level * mates, mates)
        slot_there.append(slot_of)
        slot_near.append(reorder(slot_of, relative, 0))
        masks.append(own_first(jnp.pad(named.astype(bf16), ((0, 0), (0, 128 - E))), core, 0))
    slot_near, slot_there, mask_line = [jnp.stack(t) for t in (slot_near, slot_there, masks)]

    slots = LINE * share * mates

    nil = packed_line[1, 0, 0] * 0
    weights = jnp.concatenate(
        [gate_weight, up_weight, down_weight.transpose(0, 2, 1) + nil], axis=2
    )
    weights = exchange(after(weights, packed_line))
    cot_line = line_gather(after(cotangent, packed_line))

    hidden_all = both_cores(hidden_in)
    tokens_all = hidden_all.astype(f32)
    scale_all = lax.rsqrt(jnp.mean(tokens_all * tokens_all, axis=-1, keepdims=True) + EPSILON)
    normed_all = (tokens_all * scale_all * gain_first).astype(bf16)
    places = own_first(positions(segments[0]), core, 0)
    segment_ids = own_first(segments[0], core, 0)
    token_index = own_first(jnp.arange(span, dtype=jnp.int32), core, 0)
    allowed = (segment_ids[:, None] == segment_ids[None, :]) & (
        token_index[None, :] <= token_index[:, None]
    )
    raw = jnp.dot(normed_all, qkv_cols, preferred_element_type=f32)
    queries = apply_rotary(raw[:, :head_cols].reshape(span, heads, HEAD_SIZE), places, 1.0)
    queries = queries.astype(bf16).transpose(1, 0, 2)
    keys = apply_rotary(
        raw[:, head_cols : head_cols + kv_cols].reshape(span, 1, HEAD_SIZE), places, 1.0
    ).astype(bf16)[:, 0]
    values = raw[:, head_cols + kv_cols :].astype(bf16)
    scaling = HEAD_SIZE ** (-0.5)
    attended, log_total = attend_group((queries, keys, values), allowed, scaling)
    attended_low = attended.transpose(1, 0, 2).reshape(span, head_cols).astype(bf16)
    branch_part = lax.dot_general(attended_low, output_t, nt, preferred_element_type=f32)
    tokens_in = hidden_in.astype(f32)
    hidden_mid = tokens_in + sum_cores(branch_part, f32)
    scale_second = lax.rsqrt(jnp.mean(hidden_mid * hidden_mid, axis=-1, keepdims=True) + EPSILON)
    unit_second = hidden_mid * scale_second
    normed_second = (unit_second * gain_second).astype(bf16)

    cot_line = after(cot_line, normed_second)
    cot_swap = swap_cores(cot_line)
    cot_rows = select_rows(slot_there, cot_line, cot_swap, share, mask_line)
    normed_line = line_gather(after(normed_second, weights, cot_rows))
    cot_rows = plane_all(cot_rows.reshape(mates, LINE, share, MODEL_WIDTH + 128))
    normed_swap = swap_cores(normed_line)
    normed_rows = select_rows(slot_near, after(normed_line, cot_rows), normed_swap, share)
    pieces = plane_exchange(normed_rows)

    pieces = [p.reshape(2 * LINE * share, MODEL_WIDTH) for p in pieces]
    cot_rows = cot_rows.reshape(PLANE, 2, LINE * share, MODEL_WIDTH + 128)
    weights = weights.reshape(rows, 2, row_block, 3 * hidden_block)
    done, mixture, back = [], None, []
    for move in range(PLANE):
        if move == 3:
            pieces[3] = after(pieces[3], back[1])
        found = expert_rows(
            move, place, core, my_expert, pieces[move], cot_rows, weights, out_full[:, head_cols:], mixture
        )
        mixture = found[1]
        done.append(found)
        back.append(plane_move(found[0], move) if move else found[0])
    _, _, grad_expert, activation, grad_gate, grad_up, grad_logits = [
        list(a) for a in zip(*done)
    ]

    def combine(table, near, far, far_block=0):
        kept, away = combine_rows(table, near, far, far_block)
        return (kept.astype(f32) + swap_cores(away).astype(f32)).astype(bf16)

    shape = (2, LINE, share, MODEL_WIDTH)
    back = [b.reshape(shape) for b in back]
    grad_expert[3] = after(grad_expert[3], back[2])
    down_home = exchange(shard_grad(grad_expert, activation, rows))
    router_grad = sum(
        lax.dot_general(g, p, tn, preferred_element_type=f32) for g, p in zip(grad_logits, pieces)
    )
    router_grad = router_grad[:E].T
    far = swap_cores(after(jnp.stack([b[1] for b in back]), down_home, router_grad))
    grad_parts = combine(slot_near, jnp.stack([b[0] for b in back]), far)
    grad_normed = line_reduce(grad_parts).astype(f32)
    mixture = mixture.reshape(mates, LINE, share, MODEL_WIDTH)
    mixture = plane_all(after(mixture, down_home))
    mixture_there = after(mixture, grad_parts)
    mixture_parts = combine(slot_there, mixture_there, mixture_there, 1)
    mixture_own = line_reduce(mixture_parts).astype(f32)
    gate_up_home = shard_grad(pieces, grad_gate + grad_up, rows)
    gate_up_home = exchange(after(gate_up_home, mixture))

    grad_normed = after(grad_normed, mixture_parts)
    tilted = grad_normed * gain_second
    gain_second_grad = jnp.sum(grad_normed * unit_second, axis=0)
    grad_hidden = cotangent.astype(f32) + scale_second * (
        tilted - unit_second * jnp.mean(tilted * unit_second, axis=-1, keepdims=True)
    )
    branch_all = both_cores(grad_hidden.astype(bf16))

    output_t_grad = lax.dot_general(branch_all, attended_low, tn, preferred_element_type=f32)
    grad_attended = jnp.dot(branch_all, output_t, preferred_element_type=f32).astype(bf16)
    grad_attended = grad_attended.reshape(span, heads, HEAD_SIZE).transpose(1, 0, 2)
    grad_queries, grad_keys, grad_values = attend_back(
        (queries, keys, values, log_total, grad_attended), allowed, scaling
    )
    grad_query_low = (
        apply_rotary(grad_queries.transpose(1, 0, 2), places, -1.0)
        .reshape(span, head_cols)
        .astype(bf16)
    )
    grad_key_low = apply_rotary(grad_keys[:, None], places, -1.0)[:, 0].astype(bf16)
    grad_qkv = jnp.concatenate([grad_query_low, grad_key_low, grad_values.astype(bf16)], axis=1)
    qkv_grad = lax.dot_general(normed_all, grad_qkv, tn, preferred_element_type=f32)
    first_part = lax.dot_general(grad_qkv, qkv_cols, nt, preferred_element_type=f32)
    unit_all = tokens_all * scale_all
    gain_first_grad = jnp.sum(first_part * unit_all, axis=0)
    grad_first = sum_cores(first_part, f32)
    unit_first = tokens_in * scale_all[:local]
    tilted_first = grad_first * gain_first
    input_grad = grad_hidden + scale_all[:local] * (
        tilted_first - unit_first * jnp.mean(tilted_first * unit_first, axis=-1, keepdims=True)
    )
    block_out = (hidden_mid + mixture_own).astype(bf16)

    extra = jnp.concatenate(
        [
            router_grad,
            gain_second_grad[:, None],
            gain_first_grad[:, None],
            jnp.zeros((MODEL_WIDTH, 128 - E - 2), f32),
        ],
        axis=1,
    )
    owned, marks = row_reduce(
        [jnp.concatenate([output_t_grad, extra], axis=1), qkv_grad], level, place
    )
    output_own, qkv_own = owned[:, :head_cols], owned[:, head_cols + 128 :]
    small_own = owned[:, head_cols : head_cols + 128]
    small_own = small_own + swap_cores(small_own)
    gate_up_home = after(gate_up_home, *marks, block_out, input_grad)
    return (
        block_out,
        input_grad,
        small_own[:, E + 1],
        qkv_own[:, :head_cols],
        qkv_own[:, head_cols : head_cols + kv_cols],
        qkv_own[:, head_cols + kv_cols :],
        output_own[:, :head_cols].T,
        small_own[:, E],
        small_own[:, :E],
        gate_up_home[:, :, :hidden_block].astype(f32),
        gate_up_home[:, :, hidden_block:].astype(f32),
        down_home.astype(f32).transpose(0, 2, 1),
    )


def solution(mesh):
    in_specs = (
        P(("row", "col"), None),
        P("row", None),
        P("row", None),
        P("row"),
        P("row", "col"),
        P("row", "col"),
        P("row", "col"),
        P("col", "row"),
        P("row"),
        P("row", None),
        P(None, "row", "col"),
        P(None, "row", "col"),
        P(None, "col", "row"),
        P(("row", "col"), None),
    )
    out_specs = (
        P(("row", "col"), None),
        P(("row", "col"), None),
        P("row"),
        P("row", "col"),
        P("row", "col"),
        P("row", "col"),
        P("col", "row"),
        P("row"),
        P("row", None),
        P(None, "row", "col"),
        P(None, "row", "col"),
        P(None, "col", "row"),
    )
    rows, cols = mesh.shape["row"], mesh.shape["col"]
    one_each = rows == 4 * PLANE and cols == KEY_VALUE_HEADS and rows * cols == E
    return jax.shard_map(
        tokens_move if one_each else weights_move, mesh=mesh,
        in_specs=in_specs,
        out_specs=out_specs,
        check_vma=False,
    )
```
